128 devices in a mesh: seq: 16 (over y, z_lo, core), tp: 8 (over z_hi, x).
Axes of the slice: x: 4, y: 4, z: 4 (z_hi: 2, z_lo: 2; z = z_hi * 2 + z_lo), core: 2. Of those that a mesh axis runs over, the one named last changes fastest.
Arguments:
- tokens: bfloat16 [8192, 2048], P('seq'), may hold values from -6 to 6
- w_zx: float32 [2048, 8192], P(('seq', 'tp')), may hold values from -0.125 to 0.125
- w_dt: float32 [2048, 64], P(('seq', 'tp')), may hold values from -0.26516503 to 0.26516503
- w_bc: float32 [2048, 256], P(('seq', 'tp')), may hold values from -0.125 to 0.125
- conv_x_weight: float32 [4, 4096], P(None, 'tp'), may hold values from -3 to 3
- conv_x_bias: float32 [4096], P('tp'), may hold values from -1.8 to 1.8
- conv_bc_weight: float32 [4, 256], replicated, may hold values from -3 to 3
- conv_bc_bias: float32 [256], replicated, may hold values from -1.8 to 1.8
- dt_bias: float32 [64], P('tp'), may hold values from -11 to -2
- a_log: float32 [64], P('tp'), may hold values from 0 to 2.77
- skip: float32 [64], P('tp'), may hold values from 0.5 to 2
- norm_weight: float32 [4096], P('tp'), may hold values from 0.1 to 1.9
- w_out: float32 [4096, 2048], P('tp', 'seq'), may hold values from -0.09375 to 0.09375
- lengths: int32 [8], replicated, may hold values from 1 to 4096, 8192 in all
- request_group: int32 [32], replicated, may hold values from 0 to 31
Outputs:
- mixed: bfloat16 [8192, 2048], P(('seq', 'tp'))
- request_states: float32 [32, 64, 64, 128], P('seq', 'tp')
The draws below stay inside these ranges and needn't reach their ends.
Inputs may be any that keep to these rules, and one draw needn't show every extreme that they name: 8 prompts packed end to end in this order; the lengths sum to 8192 and the longest is exactly 4096.
All inputs are finite; a program needn't handle non-finite values.
Results may differ from the reference program's by a relative error of at most 0.011.
Values may be sent and summed in bfloat16 or wider, within the bound.
A program may use at most 128 MiB of HBM per device.

```python
import math
import jax
import jax.numpy as jnp
import numpy as np
from jax import lax

D = 2048
INNER = 4096
HEADS = 64
HEAD_DIM = 64
STATE = 128
CONV = 4
GROUP = 256
PROMPTS = 8
TOKENS = 8192
GROUPS = 32
REQUESTS = 32
PROMPT_MAX = 4096


def set_ends(entries, own_key, low, largest):
    longest = entries.shape.index(max(entries.shape))
    spots = []
    for shift in (0, 1):
        where = [jax.random.randint(jax.random.fold_in(own_key, axis), (), 0, length) for axis, length in enumerate(entries.shape)]
        where[longest] = (where[longest] + shift) % entries.shape[longest]
        spots.append(tuple(where))
    return entries.at[spots[0]].set(low).at[spots[1]].set(largest)


def steps_of(stream_key, shape, shards, low, largest):
    gain, own = 1.0, jax.random.fold_in(stream_key, 6)
    for dim, blocks in shards:
        draws = jnp.exp(jax.random.uniform(jax.random.fold_in(own, dim), (blocks,), jnp.float32, low / len(shards), largest / len(shards)))
        gain = gain * jnp.repeat(draws, shape[dim] // blocks).reshape([-1 if axis == dim else 1 for axis in range(len(shape))])
    return gain


def profile(count, total, limit, skew):
    portions = [(1 << 20) // math.isqrt(grade ** skew) + 1 for grade in range(2, count + 1)]
    spare, holding = total - limit - (count - 1), [1] * (count - 1)
    while spare > 0:
        movable = [i for i in range(count - 1) if holding[i] < limit]
        mass, budget = sum([portions[i] for i in movable]), spare
        for i in movable:
            extra = min(limit - holding[i], max(1, budget * portions[i] // mass), spare)
            holding[i] = holding[i] + extra
            spare = spare - extra
    return np.array([limit] + holding)


def ragged(key, count, total, most, lean):
    if count == 2:
        one = jax.random.randint(key, (), max(1, total - most), min(most, total - 1) + 1)
        return jnp.stack([one, total - one])
    tallies = jnp.asarray(profile(count, total, most, lean), jnp.int32)
    twos = (count - 1) // 2
    donor, taker = tallies[1:1 + 2 * twos:2], tallies[2:2 + 2 * twos:2]
    margin = jnp.minimum(donor - 1, most - taker)
    passed = jax.random.randint(jax.random.fold_in(key, 1), (twos,), 0, 1 << 20) % (margin + 1)
    tallies = tallies.at[1:1 + 2 * twos:2].set(donor - passed).at[2:2 + 2 * twos:2].set(taker + passed)
    return tallies[jax.random.permutation(jax.random.fold_in(key, 2), count)]


def normal_values(key, dims, scale, bound, pieces=(), held_as=jnp.bfloat16):
    array = jax.random.normal(key, dims, jnp.float32) * scale
    if len(pieces) > 0:
        array = steps_of(key, dims, pieces, -0.22, 0.18) * array
    return jnp.clip(array, min=-bound, max=bound).astype(held_as)


def setup_inputs(seed: int = 0) -> dict:
    streams_of = jax.random.split(jax.random.key(seed), 16)
    return {
        "tokens": normal_values(streams_of[0], (TOKENS, D), 1.0, 6.0, ((0, 16),)),
        "w_zx": normal_values(streams_of[1], (D, 2 * INNER), D ** -0.5, 0.125, ((0, 128),), jnp.float32),
        "w_dt": normal_values(streams_of[2], (D, HEADS), (2.0 / D ** 0.5), 0.26516503, ((0, 128),), jnp.float32),
        "w_bc": normal_values(streams_of[3], (D, 2 * STATE), D ** -0.5, 0.125, ((0, 128),), jnp.float32),
        "conv_x_weight": normal_values(streams_of[4], (CONV, INNER), CONV ** -0.5, 3.0, ((1, 8),), jnp.float32),
        "conv_x_bias": normal_values(streams_of[5], (INNER,), 0.3, 1.8, ((0, 8),), jnp.float32),
        "conv_bc_weight": normal_values(streams_of[6], (CONV, 2 * STATE), CONV ** -0.5, 3.0, (), jnp.float32),
        "conv_bc_bias": normal_values(streams_of[7], (2 * STATE,), 0.3, 1.8, (), jnp.float32),
        "dt_bias": jnp.clip(-11.0 + 9.0 * jax.random.uniform(streams_of[8], (HEADS,), jnp.float32) ** steps_of(streams_of[8], (HEADS,), ((0, 8),), -0.2, 0.2), -11.0, -2.0),
        "a_log": jnp.clip(2.77 * jax.random.uniform(streams_of[9], (HEADS,), jnp.float32) ** steps_of(streams_of[9], (HEADS,), ((0, 8),), -0.2, 0.2), 0.0, 2.77),
        "skip": jnp.clip(0.5 + 1.5 * jax.random.uniform(streams_of[10], (HEADS,), jnp.float32) ** steps_of(streams_of[10], (HEADS,), ((0, 8),), -0.2, 0.2), 0.5, 2.0),
        "norm_weight": jnp.clip(1.0 + 0.18 * jax.random.normal(streams_of[11], (INNER,), jnp.float32), 0.1, 1.9),
        "w_out": normal_values(streams_of[12], (INNER, D), INNER ** -0.5, 0.09375, ((0, 8), (1, 16)), jnp.float32),
        "lengths": ragged(streams_of[13], PROMPTS, TOKENS, PROMPT_MAX, 2).astype(jnp.int32),
        "request_group": set_ends(jax.random.randint(streams_of[14], (REQUESTS,), 0, GROUPS), jax.random.fold_in(streams_of[14], 1), 0, GROUPS - 1).astype(jnp.int32),
    }


epsilon = 1e-05

def segment_of(position, lengths):
    prompt_ends = jnp.cumsum(lengths).astype(jnp.int32)
    return lax.optimization_barrier(jnp.sum((position[:, None] >= prompt_ends[None, :]).astype(jnp.int32), axis=1))

def group_scan(carry_state, group_item, decay_rate, skip):
    inputs, b_matrix, c_matrix, step_size, segments, seg_before = group_item
    cumul_heads = jnp.cumsum(step_size * decay_rate[None, :], axis=0).T
    within = jnp.arange(GROUP, dtype=jnp.int32)
    same_prompt = (segments[:, None] == segments[None, :]) & (within[:, None] >= within[None, :])
    log_decay = cumul_heads[:, :, None] - cumul_heads[:, None, :]
    decay_matrix = jnp.where(same_prompt[None], jnp.exp(jnp.where(same_prompt[None], log_decay, 0.0)), 0.0)
    scores = jnp.dot(c_matrix, b_matrix.T, preferred_element_type=jnp.float32)
    step_heads = step_size.T
    mix_weights = lax.optimization_barrier((decay_matrix * scores[None] * step_heads[:, None, :]).astype(jnp.bfloat16))
    inputs_wide = inputs.astype(jnp.float32)
    diag_out = jnp.einsum('hij,jhp->ihp', mix_weights.astype(jnp.float32), inputs_wide)
    last_segment = segments[-1]
    tail_weight = jnp.where((segments == last_segment)[None, :], jnp.exp(cumul_heads[:, -1:] - cumul_heads), 0.0) * step_heads
    b_weighted = lax.optimization_barrier((b_matrix.astype(jnp.float32)[None] * tail_weight[:, :, None]).astype(jnp.bfloat16))
    contrib = jnp.einsum('jhp,hjn->hpn', inputs_wide, b_weighted.astype(jnp.float32))
    carry_keep = jnp.where((segments == seg_before)[None, :], jnp.exp(cumul_heads), 0.0)
    state_low = lax.optimization_barrier(carry_state.astype(jnp.bfloat16))
    carry_out = jnp.einsum('in,hpn->ihp', c_matrix.astype(jnp.float32), state_low.astype(jnp.float32)) * carry_keep.T[:, :, None]
    pass_gate = jnp.where(last_segment == seg_before, jnp.exp(cumul_heads[:, -1]), 0.0)
    next_state = pass_gate[:, None, None] * carry_state + contrib
    output = diag_out + carry_out + skip[None, :, None] * inputs_wide
    return (next_state, (output, next_state))

def reference(tokens, w_zx, w_dt, w_bc, conv_x_weight, conv_x_bias, conv_bc_weight, conv_bc_bias, dt_bias, a_log, skip, norm_weight, w_out, lengths, request_group):
    zx = jnp.dot(tokens, w_zx.astype(jnp.bfloat16), preferred_element_type=jnp.float32).astype(jnp.bfloat16)
    gate_z = zx[:, :INNER]
    x_raw = zx[:, INNER:]
    dt_pre = jnp.dot(tokens, w_dt.astype(jnp.bfloat16), preferred_element_type=jnp.float32)
    bc_raw = jnp.dot(tokens, w_bc.astype(jnp.bfloat16), preferred_element_type=jnp.float32).astype(jnp.bfloat16)
    raw_mix = jnp.concatenate([x_raw, bc_raw], axis=1)
    conv_weight = jnp.concatenate([conv_x_weight, conv_bc_weight], axis=1)
    conv_bias = jnp.concatenate([conv_x_bias, conv_bc_bias], axis=0)
    padded = jnp.concatenate([jnp.zeros((CONV - 1, raw_mix.shape[1]), jnp.bfloat16), raw_mix], axis=0)
    seg_pad = segment_of(jnp.arange(TOKENS + CONV - 1, dtype=jnp.int32) - (CONV - 1), lengths)
    seg_tok = seg_pad[CONV - 1:]
    conv_sum = jnp.zeros((TOKENS, raw_mix.shape[1]), jnp.float32) + conv_bias[None, :]
    for offset_tap in range(CONV):
        rows_wide = padded[offset_tap:offset_tap + TOKENS].astype(jnp.float32)
        keep_tap = seg_pad[offset_tap:offset_tap + TOKENS] == seg_tok
        conv_sum = conv_sum + jnp.where(keep_tap[:, None], rows_wide * conv_weight[offset_tap][None, :], 0.0)
    convolved = jax.nn.silu(conv_sum).astype(jnp.bfloat16)
    inputs = convolved[:, :INNER].reshape(GROUPS, GROUP, HEADS, HEAD_DIM)
    b_matrix = convolved[:, INNER:INNER + STATE].reshape(GROUPS, GROUP, STATE)
    c_matrix = convolved[:, INNER + STATE:].reshape(GROUPS, GROUP, STATE)
    step_size = jax.nn.softplus(dt_pre + dt_bias[None, :]).reshape(GROUPS, GROUP, HEADS)
    segments = seg_tok.reshape(GROUPS, GROUP)
    seg_before = segment_of(jnp.arange(GROUPS, dtype=jnp.int32) * GROUP - 1, lengths)
    decay_rate = -jnp.exp(a_log)

    def scan_step(carry_state, group_item):
        return group_scan(carry_state, group_item, decay_rate, skip)
    start_state = jnp.zeros((HEADS, HEAD_DIM, STATE), jnp.float32)
    _, (outputs, end_states) = lax.scan(scan_step, start_state, (inputs, b_matrix, c_matrix, step_size, segments, seg_before))
    y_full = outputs.reshape(TOKENS, INNER)
    gated = y_full * jax.nn.silu(gate_z.astype(jnp.float32))
    mean_square = lax.optimization_barrier(jnp.mean(gated * gated, axis=1))
    normed = (gated * lax.rsqrt(mean_square + epsilon)[:, None] * norm_weight[None, :]).astype(jnp.bfloat16)
    mixed = jnp.dot(normed, w_out.astype(jnp.bfloat16), preferred_element_type=jnp.float32).astype(jnp.bfloat16)
    request_states = end_states[request_group]
    return (mixed, request_states)
```

```python
import jax
import jax.numpy as jnp
from jax import lax
from jax.sharding import PartitionSpec as P

INNER = 4096
GROUP = 256


epsilon = 1e-05


def from_behind(x, axis, by):
    count = lax.axis_size(axis)
    pairs = [(i, i + by) for i in range(count) if 0 <= i + by < count]
    return lax.ppermute(x, axis, pairs)


def segment_of(position, lengths):
    prompt_ends = jnp.cumsum(lengths)
    return jnp.sum((position[:, None] >= prompt_ends[None, :]).astype(jnp.int32), axis=1)


def round_up(n, m):
    return (n + m - 1) // m * m


def on_device(
    tokens,
    w_zx,
    w_dt,
    w_bc,
    conv_x_weight,
    conv_x_bias,
    conv_bc_weight,
    conv_bc_bias,
    dt_bias,
    a_log,
    skip,
    norm_weight,
    w_out,
    lengths,
    request_group,
):
    tp_count = lax.axis_size("tp")
    seq_count = lax.axis_size("seq")
    seq_index = lax.axis_index("seq")
    tok_dev = tokens.shape[0]
    local_rows = w_zx.shape[0]
    inner_local = conv_x_weight.shape[1]
    heads_local = dt_bias.shape[0]
    head_width = inner_local // heads_local
    bc_width = conv_bc_weight.shape[1]
    state_width = bc_width // 2
    taps = conv_x_weight.shape[0]
    groups_dev = tok_dev // GROUP

    zx_part = w_zx.astype(jnp.bfloat16).reshape(local_rows, 2, tp_count, inner_local)
    zx_part = zx_part.transpose(0, 2, 1, 3).reshape(local_rows, tp_count, 2 * inner_local)
    bc_part = jnp.broadcast_to(
        w_bc.astype(jnp.bfloat16)[:, None, :], (local_rows, tp_count, bc_width)
    )
    dt_part = w_dt.astype(jnp.bfloat16).reshape(local_rows, tp_count, heads_local)
    used = 2 * inner_local + bc_width + heads_local
    width = round_up(used, 128)
    pad_part = jnp.zeros((local_rows, tp_count, width - used), jnp.bfloat16)
    packed = jnp.concatenate([zx_part, bc_part, dt_part, pad_part], axis=2)
    packed = packed.reshape(local_rows, tp_count * width)
    block = lax.all_to_all(packed, "tp", split_axis=1, concat_axis=0, tiled=True)
    weights = lax.all_gather(block, "seq", axis=0, tiled=True)
    proj = jnp.dot(tokens, weights, preferred_element_type=jnp.float32)
    zx_low = proj[:, : 2 * inner_local].astype(jnp.bfloat16)
    gate_z = zx_low[:, :inner_local]
    x_raw = zx_low[:, inner_local:]
    bc_raw = proj[:, 2 * inner_local : 2 * inner_local + bc_width].astype(jnp.bfloat16)
    dt_pre = proj[:, 2 * inner_local + bc_width : used]

    raw_mix = jnp.concatenate([x_raw, bc_raw], axis=1)
    conv_weight = jnp.concatenate([conv_x_weight, conv_bc_weight], axis=1)
    conv_bias = jnp.concatenate([conv_x_bias, conv_bc_bias], axis=0)
    rim_rows = from_behind(raw_mix[tok_dev - (taps - 1) :], "seq", 1)
    padded = jnp.concatenate([rim_rows, raw_mix], axis=0)
    offset = seq_index * tok_dev
    seg_pad = segment_of(
        offset - (taps - 1) + jnp.arange(tok_dev + taps - 1, dtype=jnp.int32), lengths
    )
    seg_tok = seg_pad[taps - 1 :]
    conv_sum = jnp.zeros((tok_dev, raw_mix.shape[1]), jnp.float32) + conv_bias[None, :]
    for offset_tap in range(taps):
        rows_wide = padded[offset_tap : offset_tap + tok_dev].astype(jnp.float32)
        keep_tap = seg_pad[offset_tap : offset_tap + tok_dev] == seg_tok
        conv_sum = conv_sum + jnp.where(
            keep_tap[:, None], rows_wide * conv_weight[offset_tap][None, :], 0.0
        )
    convolved = jax.nn.silu(conv_sum).astype(jnp.bfloat16)
    inputs = convolved[:, :inner_local].reshape(groups_dev, GROUP, heads_local, head_width)
    b_matrix = convolved[:, inner_local : inner_local + state_width].reshape(
        groups_dev, GROUP, state_width
    )
    c_matrix = convolved[:, inner_local + state_width :].reshape(groups_dev, GROUP, state_width)
    step_size = jax.nn.softplus(dt_pre + dt_bias[None, :]).reshape(groups_dev, GROUP, heads_local)
    step_heads = step_size.transpose(0, 2, 1)
    decay_rate = -jnp.exp(a_log)
    cumul_heads = jnp.cumsum(step_size * decay_rate[None, None, :], axis=1).transpose(0, 2, 1)
    segments = seg_tok.reshape(groups_dev, GROUP)
    seg_before = segment_of(offset + jnp.arange(groups_dev, dtype=jnp.int32) * GROUP - 1, lengths)
    within = jnp.arange(GROUP, dtype=jnp.int32)
    same_prompt = (segments[:, :, None] == segments[:, None, :]) & (
        within[:, None] >= within[None, :]
    )[None]
    log_decay = cumul_heads[:, :, :, None] - cumul_heads[:, :, None, :]
    decay_matrix = jnp.where(
        same_prompt[:, None], jnp.exp(jnp.where(same_prompt[:, None], log_decay, 0.0)), 0.0
    )
    scores = jnp.einsum("cin,cjn->cij", c_matrix, b_matrix, preferred_element_type=jnp.float32)
    mix_weights = (decay_matrix * scores[:, None] * step_heads[:, :, None, :]).astype(jnp.bfloat16)
    diag_out = jnp.einsum(
        "chij,cjhp->cihp", mix_weights, inputs, preferred_element_type=jnp.float32
    )
    last_segment = segments[:, -1]
    tail_weight = (
        jnp.where(
            (segments == last_segment[:, None])[:, None, :],
            jnp.exp(cumul_heads[:, :, -1:] - cumul_heads),
            0.0,
        )
        * step_heads
    )
    b_weighted = (b_matrix.astype(jnp.float32)[:, None] * tail_weight[:, :, :, None]).astype(
        jnp.bfloat16
    )
    contrib = jnp.einsum("cjhp,chjn->chpn", inputs, b_weighted, preferred_element_type=jnp.float32)
    pass_gate = jnp.where(
        (last_segment == seg_before)[:, None], jnp.exp(cumul_heads[:, :, -1]), 0.0
    )

    def local_step(carry_state, group_item):
        factor, source = group_item
        next_state = factor[:, None, None] * carry_state + source
        return (next_state, (carry_state, next_state))

    zero_state = jnp.zeros((heads_local, head_width, state_width), jnp.float32)
    _, (local_in, local_end) = lax.scan(local_step, zero_state, (pass_gate, contrib))
    through_group = jnp.cumprod(pass_gate, axis=0)
    before_group = jnp.concatenate(
        [jnp.ones((1, heads_local), jnp.float32), through_group[:-1]], axis=0
    )

    gate_hi = through_group.astype(jnp.bfloat16)
    gate_lo = (through_group - gate_hi.astype(jnp.float32)).astype(jnp.bfloat16)
    extra = jnp.zeros((groups_dev, heads_local, 8, state_width), jnp.bfloat16)
    extra = extra.at[:, :, 0, :].set(jnp.broadcast_to(gate_hi[:, :, None], gate_hi.shape + (state_width,)))
    extra = extra.at[:, :, 1, :].set(jnp.broadcast_to(gate_lo[:, :, None], gate_lo.shape + (state_width,)))
    sendable = jnp.concatenate([local_end.astype(jnp.bfloat16), extra], axis=2)
    every = lax.all_gather(sendable, "seq", axis=0, tiled=False)
    every_end = every[:, :, :, :head_width].astype(jnp.float32)
    every_gate = (
        every[:, :, :, head_width, 0].astype(jnp.float32)
        + every[:, :, :, head_width + 1, 0].astype(jnp.float32)
    )
    dev_gate = every_gate[:, -1]
    dev_ids = jnp.arange(seq_count, dtype=jnp.int32)

    def carry_weights(k):
        between = (dev_ids[:, None] < dev_ids[None, :]) & (dev_ids[None, :] < k)
        factors = jnp.where(between[:, :, None], dev_gate[None, :, :], 1.0)
        return jnp.where((dev_ids < k)[:, None], jnp.prod(factors, axis=1), 0.0)

    own_weights = carry_weights(seq_index)
    slot_ids = jnp.arange(groups_dev, dtype=jnp.int32)
    last_slot = (slot_ids == groups_dev - 1).astype(jnp.float32)
    own_coef = own_weights[:, None, :] * last_slot[None, :, None]
    carried = jnp.einsum(
        "jch,jchpn->hpn", own_coef, every_end, precision=lax.Precision.HIGHEST,
        preferred_element_type=jnp.float32,
    )
    group_in = before_group[:, :, None, None] * carried[None] + local_in
    state_low = group_in.astype(jnp.bfloat16)
    carry_keep = jnp.where((segments == seg_before[:, None])[:, None, :], jnp.exp(cumul_heads), 0.0)
    carry_out = jnp.einsum(
        "cin,chpn->cihp", c_matrix, state_low, preferred_element_type=jnp.float32
    )
    carry_out = carry_out * carry_keep.transpose(0, 2, 1)[:, :, :, None]
    y_local = diag_out + carry_out + skip[None, None, :, None] * inputs.astype(jnp.float32)
    y_local = y_local.reshape(tok_dev, inner_local)
    gated = y_local * jax.nn.silu(gate_z.astype(jnp.float32))
    square_sum = jnp.sum(gated * gated, axis=1)
    scaled = (gated * norm_weight[None, :]).astype(jnp.bfloat16)
    out_shard = w_out.astype(jnp.bfloat16)
    out_block = lax.all_gather(out_shard, "seq", axis=1, tiled=True)
    partial = jnp.dot(scaled, out_block, preferred_element_type=jnp.float32)
    side = jnp.zeros((tok_dev, 128), jnp.float32).at[:, 0].set(square_sum)
    summed = lax.psum_scatter(
        jnp.concatenate([partial, side], axis=1), "tp", scatter_dimension=0, tiled=True
    )
    d_model = out_block.shape[1]
    mean_square = summed[:, d_model] / INNER
    mixed = (summed[:, :d_model] * lax.rsqrt(mean_square + epsilon)[:, None]).astype(jnp.bfloat16)

    req_dev = request_group.shape[0] // seq_count
    mine = lax.dynamic_slice_in_dim(request_group, seq_index * req_dev, req_dev)
    req_k = mine // groups_dev
    req_c = mine % groups_dev
    req_w = jax.vmap(carry_weights)(req_k)
    req_gate = every_gate[req_k, req_c]
    coef = req_gate[:, None, None, :] * req_w[:, :, None, :] * last_slot[None, None, :, None]
    hit = (dev_ids[None, :, None] == req_k[:, None, None]) & (
        slot_ids[None, None, :] == req_c[:, None, None]
    )
    coef = coef + hit[:, :, :, None].astype(jnp.float32)
    request_states = jnp.einsum(
        "rjch,jchpn->rhpn", coef, every_end, precision=lax.Precision.HIGHEST,
        preferred_element_type=jnp.float32,
    )
    return (mixed.astype(jnp.bfloat16), request_states)


def solution(mesh):
    return jax.shard_map(
        on_device,
        mesh=mesh,
        in_specs=(
            P("seq", None),
            P(("seq", "tp"), None),
            P(("seq", "tp"), None),
            P(("seq", "tp"), None),
            P(None, "tp"),
            P("tp"),
            P(),
            P(),
            P("tp"),
            P("tp"),
            P("tp"),
            P("tp"),
            P("tp", "seq"),
            P(),
            P(),
        ),
        out_specs=(P(("seq", "tp"), None), P("seq", "tp", None, None)),
        check_vma=False,
    )
```

```python
import jax
import jax.numpy as jnp
from jax import lax
from jax.sharding import PartitionSpec as P

INNER = 4096
GROUP = 256


epsilon = 1e-05


def from_behind(x, axis, by):
    count = lax.axis_size(axis)
    pairs = [(i, i + by) for i in range(count) if 0 <= i + by < count]
    return lax.ppermute(x, axis, pairs)


def segment_of(position, lengths):
    prompt_ends = jnp.cumsum(lengths)
    return jnp.sum((position[:, None] >= prompt_ends[None, :]).astype(jnp.int32), axis=1)


def round_up(n, m):
    return (n + m - 1) // m * m


def on_device(
    tokens,
    w_zx,
    w_dt,
    w_bc,
    conv_x_weight,
    conv_x_bias,
    conv_bc_weight,
    conv_bc_bias,
    dt_bias,
    a_log,
    skip,
    norm_weight,
    w_out,
    lengths,
    request_group,
):
    tp_count = lax.axis_size("tp")
    seq_count = lax.axis_size("seq")
    seq_index = lax.axis_index("seq")
    tok_dev = tokens.shape[0]
    local_rows = w_zx.shape[0]
    inner_local = conv_x_weight.shape[1]
    heads_local = dt_bias.shape[0]
    head_width = inner_local // heads_local
    bc_width = conv_bc_weight.shape[1]
    state_width = bc_width // 2
    taps = conv_x_weight.shape[0]
    groups_dev = tok_dev // GROUP

    zx_part = w_zx.astype(jnp.bfloat16).reshape(local_rows, 2, tp_count, inner_local)
    zx_part = zx_part.transpose(0, 2, 1, 3).reshape(local_rows, tp_count, 2 * inner_local)
    bc_part = jnp.broadcast_to(
        w_bc.astype(jnp.bfloat16)[:, None, :], (local_rows, tp_count, bc_width)
    )
    dt_part = w_dt.astype(jnp.bfloat16).reshape(local_rows, tp_count, heads_local)
    used = 2 * inner_local + bc_width + heads_local
    width = round_up(used, 128)
    pad_part = jnp.zeros((local_rows, tp_count, width - used), jnp.bfloat16)
    packed = jnp.concatenate([zx_part, bc_part, dt_part, pad_part], axis=2)
    packed = packed.reshape(local_rows, tp_count * width)
    block = lax.all_to_all(packed, "tp", split_axis=1, concat_axis=0, tiled=True)
    out_rows, out_cols = w_out.shape
    block_rows = block.shape[0]
    out_piece = w_out.astype(jnp.bfloat16).reshape(block_rows, out_rows * out_cols // block_rows)
    gathered = lax.all_gather(
        jnp.concatenate([block, out_piece], axis=1), "seq", axis=0, tiled=True
    )
    weights = gathered[:, :width]
    out_block = gathered[:, width:].reshape(seq_count, out_rows, out_cols)
    out_block = out_block.transpose(1, 0, 2).reshape(out_rows, seq_count * out_cols)
    proj = jnp.dot(tokens, weights, preferred_element_type=jnp.float32)
    zx_low = proj[:, : 2 * inner_local].astype(jnp.bfloat16)
    gate_z = zx_low[:, :inner_local]
    x_raw = zx_low[:, inner_local:]
    bc_raw = proj[:, 2 * inner_local : 2 * inner_local + bc_width].astype(jnp.bfloat16)
    dt_pre = proj[:, 2 * inner_local + bc_width : used]

    raw_mix = jnp.concatenate([x_raw, bc_raw], axis=1)
    conv_weight = jnp.concatenate([conv_x_weight, conv_bc_weight], axis=1)
    conv_bias = jnp.concatenate([conv_x_bias, conv_bc_bias], axis=0)
    rim_rows = from_behind(raw_mix[tok_dev - (taps - 1) :], "seq", 1)
    padded = jnp.concatenate([rim_rows, raw_mix], axis=0)
    offset = seq_index * tok_dev
    seg_pad = segment_of(
        offset - (taps - 1) + jnp.arange(tok_dev + taps - 1, dtype=jnp.int32), lengths
    )
    seg_tok = seg_pad[taps - 1 :]
    conv_sum = jnp.zeros((tok_dev, raw_mix.shape[1]), jnp.float32) + conv_bias[None, :]
    for offset_tap in range(taps):
        rows_wide = padded[offset_tap : offset_tap + tok_dev].astype(jnp.float32)
        keep_tap = seg_pad[offset_tap : offset_tap + tok_dev] == seg_tok
        conv_sum = conv_sum + jnp.where(
            keep_tap[:, None], rows_wide * conv_weight[offset_tap][None, :], 0.0
        )
    convolved = jax.nn.silu(conv_sum).astype(jnp.bfloat16)
    inputs = convolved[:, :inner_local].reshape(groups_dev, GROUP, heads_local, head_width)
    b_matrix = convolved[:, inner_local : inner_local + state_width].reshape(
        groups_dev, GROUP, state_width
    )
    c_matrix = convolved[:, inner_local + state_width :].reshape(groups_dev, GROUP, state_width)
    step_size = jax.nn.softplus(dt_pre + dt_bias[None, :]).reshape(groups_dev, GROUP, heads_local)
    step_heads = step_size.transpose(0, 2, 1)
    decay_rate = -jnp.exp(a_log)
    cumul_heads = jnp.cumsum(step_size * decay_rate[None, None, :], axis=1).transpose(0, 2, 1)
    segments = seg_tok.reshape(groups_dev, GROUP)
    seg_before = segment_of(offset + jnp.arange(groups_dev, dtype=jnp.int32) * GROUP - 1, lengths)
    within = jnp.arange(GROUP, dtype=jnp.int32)
    same_prompt = (segments[:, :, None] == segments[:, None, :]) & (
        within[:, None] >= within[None, :]
    )[None]
    log_decay = cumul_heads[:, :, :, None] - cumul_heads[:, :, None, :]
    decay_matrix = jnp.where(
        same_prompt[:, None], jnp.exp(jnp.where(same_prompt[:, None], log_decay, 0.0)), 0.0
    )
    scores = jnp.einsum("cin,cjn->cij", c_matrix, b_matrix, preferred_element_type=jnp.float32)
    mix_weights = (decay_matrix * scores[:, None] * step_heads[:, :, None, :]).astype(jnp.bfloat16)
    diag_out = jnp.einsum(
        "chij,cjhp->cihp", mix_weights, inputs, preferred_element_type=jnp.float32
    )
    last_segment = segments[:, -1]
    tail_weight = (
        jnp.where(
            (segments == last_segment[:, None])[:, None, :],
            jnp.exp(cumul_heads[:, :, -1:] - cumul_heads),
            0.0,
        )
        * step_heads
    )
    b_weighted = (b_matrix.astype(jnp.float32)[:, None] * tail_weight[:, :, :, None]).astype(
        jnp.bfloat16
    )
    contrib = jnp.einsum("cjhp,chjn->chpn", inputs, b_weighted, preferred_element_type=jnp.float32)
    pass_gate = jnp.where(
        (last_segment == seg_before)[:, None], jnp.exp(cumul_heads[:, :, -1]), 0.0
    )

    def local_step(carry_state, group_item):
        factor, source = group_item
        next_state = factor[:, None, None] * carry_state + source
        return (next_state, (carry_state, next_state))

    zero_state = jnp.zeros((heads_local, head_width, state_width), jnp.float32)
    _, (local_in, local_end) = lax.scan(local_step, zero_state, (pass_gate, contrib))
    through_group = jnp.cumprod(pass_gate, axis=0)
    before_group = jnp.concatenate(
        [jnp.ones((1, heads_local), jnp.float32), through_group[:-1]], axis=0
    )

    gate_hi = through_group.astype(jnp.bfloat16)
    gate_lo = (through_group - gate_hi.astype(jnp.float32)).astype(jnp.bfloat16)
    extra = jnp.zeros((groups_dev, heads_local, 8, state_width), jnp.bfloat16)
    extra = extra.at[:, :, 0, :].set(jnp.broadcast_to(gate_hi[:, :, None], gate_hi.shape + (state_width,)))
    extra = extra.at[:, :, 1, :].set(jnp.broadcast_to(gate_lo[:, :, None], gate_lo.shape + (state_width,)))
    sendable = jnp.concatenate([local_end.astype(jnp.bfloat16), extra], axis=2)
    every = lax.all_gather(sendable, "seq", axis=0, tiled=False)
    every_end = every[:, :, :, :head_width].astype(jnp.float32)
    every_gate = (
        every[:, :, :, head_width, 0].astype(jnp.float32)
        + every[:, :, :, head_width + 1, 0].astype(jnp.float32)
    )
    dev_gate = every_gate[:, -1]
    dev_ids = jnp.arange(seq_count, dtype=jnp.int32)

    def carry_weights(k):
        between = (dev_ids[:, None] < dev_ids[None, :]) & (dev_ids[None, :] < k)
        factors = jnp.where(between[:, :, None], dev_gate[None, :, :], 1.0)
        return jnp.where((dev_ids < k)[:, None], jnp.prod(factors, axis=1), 0.0)

    own_weights = carry_weights(seq_index)
    slot_ids = jnp.arange(groups_dev, dtype=jnp.int32)
    last_slot = (slot_ids == groups_dev - 1).astype(jnp.float32)
    own_coef = own_weights[:, None, :] * last_slot[None, :, None]
    carried = jnp.einsum(
        "jch,jchpn->hpn", own_coef, every_end, precision=lax.Precision.HIGHEST,
        preferred_element_type=jnp.float32,
    )
    group_in = before_group[:, :, None, None] * carried[None] + local_in
    state_low = group_in.astype(jnp.bfloat16)
    carry_keep = jnp.where((segments == seg_before[:, None])[:, None, :], jnp.exp(cumul_heads), 0.0)
    carry_out = jnp.einsum(
        "cin,chpn->cihp", c_matrix, state_low, preferred_element_type=jnp.float32
    )
    carry_out = carry_out * carry_keep.transpose(0, 2, 1)[:, :, :, None]
    y_local = diag_out + carry_out + skip[None, None, :, None] * inputs.astype(jnp.float32)
    y_local = y_local.reshape(tok_dev, inner_local)
    gated = y_local * jax.nn.silu(gate_z.astype(jnp.float32))
    square_sum = jnp.sum(gated * gated, axis=1)
    scaled = (gated * norm_weight[None, :]).astype(jnp.bfloat16)
    partial = jnp.dot(scaled, out_block, preferred_element_type=jnp.float32)
    side = jnp.zeros((tok_dev, 128), jnp.float32).at[:, 0].set(square_sum)
    summed = lax.psum_scatter(
        jnp.concatenate([partial, side], axis=1).astype(jnp.bfloat16),
        "tp",
        scatter_dimension=0,
        tiled=True,
    ).astype(jnp.float32)
    d_model = out_block.shape[1]
    mean_square = summed[:, d_model] / INNER
    mixed = (summed[:, :d_model] * lax.rsqrt(mean_square + epsilon)[:, None]).astype(jnp.bfloat16)

    req_dev = request_group.shape[0] // seq_count
    mine = lax.dynamic_slice_in_dim(request_group, seq_index * req_dev, req_dev)
    req_k = mine // groups_dev
    req_c = mine % groups_dev
    req_w = jax.vmap(carry_weights)(req_k)
    req_gate = every_gate[req_k, req_c]
    coef = req_gate[:, None, None, :] * req_w[:, :, None, :] * last_slot[None, None, :, None]
    hit = (dev_ids[None, :, None] == req_k[:, None, None]) & (
        slot_ids[None, None, :] == req_c[:, None, None]
    )
    coef = coef + hit[:, :, :, None].astype(jnp.float32)
    request_states = jnp.einsum(
        "rjch,jchpn->rhpn", coef, every_end, precision=lax.Precision.HIGHEST,
        preferred_element_type=jnp.float32,
    )
    return (mixed.astype(jnp.bfloat16), request_states)


def solution(mesh):
    return jax.shard_map(
        on_device,
        mesh=mesh,
        in_specs=(
            P("seq", None),
            P(("seq", "tp"), None),
            P(("seq", "tp"), None),
            P(("seq", "tp"), None),
            P(None, "tp"),
            P("tp"),
            P(),
            P(),
            P("tp"),
            P("tp"),
            P("tp"),
            P("tp"),
            P("tp", "seq"),
            P(),
            P(),
        ),
        out_specs=(P(("seq", "tp"), None), P("seq", "tp", None, None)),
        check_vma=False,
    )
```

```python
import jax
import jax.numpy as jnp
from jax import lax
from jax.sharding import PartitionSpec as P
from jax.experimental import pallas as pl
from jax.experimental.pallas import tpu as pltpu
import functools

INNER = 4096
GROUP = 256


epsilon = 1e-05


def from_behind(x, axis, by):
    count = lax.axis_size(axis)
    pairs = [(i, i + by) for i in range(count) if 0 <= i + by < count]
    return lax.ppermute(x, axis, pairs)


def segment_of(position, lengths):
    prompt_ends = jnp.cumsum(lengths)
    return jnp.sum((position[:, None] >= prompt_ends[None, :]).astype(jnp.int32), axis=1)


def scatter_sum_kernel(count, rows, x_ref, o_ref, recv, send_sem, recv_sem):
    me = lax.axis_index("tp")
    barrier = pltpu.get_barrier_semaphore()
    for d in range(1, count):
        peer = lax.rem(me + d, count)
        pl.semaphore_signal(barrier, inc=1, device_id={"tp": peer}, device_id_type=pl.DeviceIdType.MESH)
    pl.semaphore_wait(barrier, count - 1)
    copies = []
    for d in range(1, count):
        peer = lax.rem(me + d, count)
        copy = pltpu.make_async_remote_copy(
            src_ref=x_ref.at[pl.ds(pl.multiple_of(peer * rows, rows), rows)],
            dst_ref=recv.at[me],
            send_sem=send_sem.at[d],
            recv_sem=recv_sem.at[me],
            device_id={"tp": peer},
            device_id_type=pl.DeviceIdType.MESH,
        )
        copy.start()
        copies.append(copy)
    total = x_ref[pl.ds(pl.multiple_of(me * rows, rows), rows), :].astype(jnp.float32)
    for d in range(1, count):
        sender = lax.rem(me + count - d, count)
        arrival = pltpu.make_async_remote_copy(
            src_ref=x_ref.at[pl.ds(0, rows)],
            dst_ref=recv.at[sender],
            send_sem=send_sem.at[d],
            recv_sem=recv_sem.at[sender],
            device_id={"tp": sender},
            device_id_type=pl.DeviceIdType.MESH,
        )
        arrival.wait_recv()
        total = total + recv[sender].astype(jnp.float32)
    for copy in copies:
        copy.wait_send()
    o_ref[...] = total


def scatter_sum(x, count):
    rows = x.shape[0] // count
    cols = x.shape[1]
    return pl.pallas_call(
        functools.partial(scatter_sum_kernel, count, rows),
        out_shape=jax.ShapeDtypeStruct((rows, cols), jnp.float32),
        in_specs=[pl.BlockSpec(memory_space=pltpu.VMEM)],
        out_specs=pl.BlockSpec(memory_space=pltpu.VMEM),
        scratch_shapes=[
            pltpu.VMEM((count, rows, cols), x.dtype),
            pltpu.SemaphoreType.DMA((count,)),
            pltpu.SemaphoreType.DMA((count,)),
        ],
        compiler_params=pltpu.CompilerParams(collective_id=0, has_side_effects=True),
    )(x)


def round_up(n, m):
    return (n + m - 1) // m * m


def on_device(
    tokens,
    w_zx,
    w_dt,
    w_bc,
    conv_x_weight,
    conv_x_bias,
    conv_bc_weight,
    conv_bc_bias,
    dt_bias,
    a_log,
    skip,
    norm_weight,
    w_out,
    lengths,
    request_group,
):
    tp_count = lax.axis_size("tp")
    seq_count = lax.axis_size("seq")
    seq_index = lax.axis_index("seq")
    tok_dev = tokens.shape[0]
    local_rows = w_zx.shape[0]
    inner_local = conv_x_weight.shape[1]
    heads_local = dt_bias.shape[0]
    head_width = inner_local // heads_local
    bc_width = conv_bc_weight.shape[1]
    state_width = bc_width // 2
    taps = conv_x_weight.shape[0]
    groups_dev = tok_dev // GROUP

    zx_part = w_zx.astype(jnp.bfloat16).reshape(local_rows, 2, tp_count, inner_local)
    zx_part = zx_part.transpose(0, 2, 1, 3).reshape(local_rows, tp_count, 2 * inner_local)
    bc_part = jnp.broadcast_to(
        w_bc.astype(jnp.bfloat16)[:, None, :], (local_rows, tp_count, bc_width)
    )
    dt_part = w_dt.astype(jnp.bfloat16).reshape(local_rows, tp_count, heads_local)
    used = 2 * inner_local + bc_width + heads_local
    width = round_up(used, 128)
    pad_part = jnp.zeros((local_rows, tp_count, width - used), jnp.bfloat16)
    packed = jnp.concatenate([zx_part, bc_part, dt_part, pad_part], axis=2)
    packed = packed.reshape(local_rows, tp_count * width)
    block = lax.all_to_all(packed, "tp", split_axis=1, concat_axis=0, tiled=True)
    out_rows, out_cols = w_out.shape
    block_rows = block.shape[0]
    out_piece = w_out.astype(jnp.bfloat16).reshape(block_rows, out_rows * out_cols // block_rows)
    gathered = lax.all_gather(
        jnp.concatenate([block, out_piece], axis=1), "seq", axis=0, tiled=True
    )
    weights = gathered[:, :width]
    out_block = gathered[:, width:].reshape(seq_count, out_rows, out_cols)
    out_block = out_block.transpose(1, 0, 2).reshape(out_rows, seq_count * out_cols)
    proj = jnp.dot(tokens, weights, preferred_element_type=jnp.float32)
    zx_low = proj[:, : 2 * inner_local].astype(jnp.bfloat16)
    gate_z = zx_low[:, :inner_local]
    x_raw = zx_low[:, inner_local:]
    bc_raw = proj[:, 2 * inner_local : 2 * inner_local + bc_width].astype(jnp.bfloat16)
    dt_pre = proj[:, 2 * inner_local + bc_width : used]

    raw_mix = jnp.concatenate([x_raw, bc_raw], axis=1)
    conv_weight = jnp.concatenate([conv_x_weight, conv_bc_weight], axis=1)
    conv_bias = jnp.concatenate([conv_x_bias, conv_bc_bias], axis=0)
    rim_rows = from_behind(raw_mix[tok_dev - (taps - 1) :], "seq", 1)
    padded = jnp.concatenate([rim_rows, raw_mix], axis=0)
    offset = seq_index * tok_dev
    seg_pad = segment_of(
        offset - (taps - 1) + jnp.arange(tok_dev + taps - 1, dtype=jnp.int32), lengths
    )
    seg_tok = seg_pad[taps - 1 :]
    conv_sum = jnp.zeros((tok_dev, raw_mix.shape[1]), jnp.float32) + conv_bias[None, :]
    for offset_tap in range(taps):
        rows_wide = padded[offset_tap : offset_tap + tok_dev].astype(jnp.float32)
        keep_tap = seg_pad[offset_tap : offset_tap + tok_dev] == seg_tok
        conv_sum = conv_sum + jnp.where(
            keep_tap[:, None], rows_wide * conv_weight[offset_tap][None, :], 0.0
        )
    convolved = jax.nn.silu(conv_sum).astype(jnp.bfloat16)
    inputs = convolved[:, :inner_local].reshape(groups_dev, GROUP, heads_local, head_width)
    b_matrix = convolved[:, inner_local : inner_local + state_width].reshape(
        groups_dev, GROUP, state_width
    )
    c_matrix = convolved[:, inner_local + state_width :].reshape(groups_dev, GROUP, state_width)
    step_size = jax.nn.softplus(dt_pre + dt_bias[None, :]).reshape(groups_dev, GROUP, heads_local)
    step_heads = step_size.transpose(0, 2, 1)
    decay_rate = -jnp.exp(a_log)
    cumul_heads = jnp.cumsum(step_size * decay_rate[None, None, :], axis=1).transpose(0, 2, 1)
    segments = seg_tok.reshape(groups_dev, GROUP)
    seg_before = segment_of(offset + jnp.arange(groups_dev, dtype=jnp.int32) * GROUP - 1, lengths)
    within = jnp.arange(GROUP, dtype=jnp.int32)
    same_prompt = (segments[:, :, None] == segments[:, None, :]) & (
        within[:, None] >= within[None, :]
    )[None]
    log_decay = cumul_heads[:, :, :, None] - cumul_heads[:, :, None, :]
    decay_matrix = jnp.where(
        same_prompt[:, None], jnp.exp(jnp.where(same_prompt[:, None], log_decay, 0.0)), 0.0
    )
    scores = jnp.einsum("cin,cjn->cij", c_matrix, b_matrix, preferred_element_type=jnp.float32)
    mix_weights = (decay_matrix * scores[:, None] * step_heads[:, :, None, :]).astype(jnp.bfloat16)
    diag_out = jnp.einsum(
        "chij,cjhp->cihp", mix_weights, inputs, preferred_element_type=jnp.float32
    )
    last_segment = segments[:, -1]
    tail_weight = (
        jnp.where(
            (segments == last_segment[:, None])[:, None, :],
            jnp.exp(cumul_heads[:, :, -1:] - cumul_heads),
            0.0,
        )
        * step_heads
    )
    b_weighted = (b_matrix.astype(jnp.float32)[:, None] * tail_weight[:, :, :, None]).astype(
        jnp.bfloat16
    )
    contrib = jnp.einsum("cjhp,chjn->chpn", inputs, b_weighted, preferred_element_type=jnp.float32)
    pass_gate = jnp.where(
        (last_segment == seg_before)[:, None], jnp.exp(cumul_heads[:, :, -1]), 0.0
    )

    def local_step(carry_state, group_item):
        factor, source = group_item
        next_state = factor[:, None, None] * carry_state + source
        return (next_state, (carry_state, next_state))

    zero_state = jnp.zeros((heads_local, head_width, state_width), jnp.float32)
    _, (local_in, local_end) = lax.scan(local_step, zero_state, (pass_gate, contrib))
    through_group = jnp.cumprod(pass_gate, axis=0)
    before_group = jnp.concatenate(
        [jnp.ones((1, heads_local), jnp.float32), through_group[:-1]], axis=0
    )

    gate_hi = through_group.astype(jnp.bfloat16)
    gate_lo = (through_group - gate_hi.astype(jnp.float32)).astype(jnp.bfloat16)
    extra = jnp.zeros((groups_dev, heads_local, 8, state_width), jnp.bfloat16)
    extra = extra.at[:, :, 0, :].set(jnp.broadcast_to(gate_hi[:, :, None], gate_hi.shape + (state_width,)))
    extra = extra.at[:, :, 1, :].set(jnp.broadcast_to(gate_lo[:, :, None], gate_lo.shape + (state_width,)))
    sendable = jnp.concatenate([local_end.astype(jnp.bfloat16), extra], axis=2)
    every = lax.all_gather(sendable, "seq", axis=0, tiled=False)
    every_end = every[:, :, :, :head_width].astype(jnp.float32)
    every_gate = (
        every[:, :, :, head_width, 0].astype(jnp.float32)
        + every[:, :, :, head_width + 1, 0].astype(jnp.float32)
    )
    dev_gate = every_gate[:, -1]
    dev_ids = jnp.arange(seq_count, dtype=jnp.int32)

    def carry_weights(k):
        between = (dev_ids[:, None] < dev_ids[None, :]) & (dev_ids[None, :] < k)
        factors = jnp.where(between[:, :, None], dev_gate[None, :, :], 1.0)
        return jnp.where((dev_ids < k)[:, None], jnp.prod(factors, axis=1), 0.0)

    own_weights = carry_weights(seq_index)
    slot_ids = jnp.arange(groups_dev, dtype=jnp.int32)
    last_slot = (slot_ids == groups_dev - 1).astype(jnp.float32)
    own_coef = own_weights[:, None, :] * last_slot[None, :, None]
    carried = jnp.einsum(
        "jch,jchpn->hpn", own_coef, every_end, precision=lax.Precision.HIGHEST,
        preferred_element_type=jnp.float32,
    )
    group_in = before_group[:, :, None, None] * carried[None] + local_in
    state_low = group_in.astype(jnp.bfloat16)
    carry_keep = jnp.where((segments == seg_before[:, None])[:, None, :], jnp.exp(cumul_heads), 0.0)
    carry_out = jnp.einsum(
        "cin,chpn->cihp", c_matrix, state_low, preferred_element_type=jnp.float32
    )
    carry_out = carry_out * carry_keep.transpose(0, 2, 1)[:, :, :, None]
    y_local = diag_out + carry_out + skip[None, None, :, None] * inputs.astype(jnp.float32)
    y_local = y_local.reshape(tok_dev, inner_local)
    gated = y_local * jax.nn.silu(gate_z.astype(jnp.float32))
    square_sum = jnp.sum(gated * gated, axis=1)
    scaled = (gated * norm_weight[None, :]).astype(jnp.bfloat16)
    partial = jnp.dot(scaled, out_block, preferred_element_type=jnp.float32)
    side = jnp.zeros((tok_dev, 128), jnp.float32).at[:, 0].set(square_sum)
    summed = scatter_sum(jnp.concatenate([partial, side], axis=1).astype(jnp.bfloat16), tp_count)
    d_model = out_block.shape[1]
    mean_square = summed[:, d_model] / INNER
    mixed = (summed[:, :d_model] * lax.rsqrt(mean_square + epsilon)[:, None]).astype(jnp.bfloat16)

    req_dev = request_group.shape[0] // seq_count
    mine = lax.dynamic_slice_in_dim(request_group, seq_index * req_dev, req_dev)
    req_k = mine // groups_dev
    req_c = mine % groups_dev
    req_w = jax.vmap(carry_weights)(req_k)
    req_gate = every_gate[req_k, req_c]
    coef = req_gate[:, None, None, :] * req_w[:, :, None, :] * last_slot[None, None, :, None]
    hit = (dev_ids[None, :, None] == req_k[:, None, None]) & (
        slot_ids[None, None, :] == req_c[:, None, None]
    )
    coef = coef + hit[:, :, :, None].astype(jnp.float32)
    request_states = jnp.einsum(
        "rjch,jchpn->rhpn", coef, every_end, precision=lax.Precision.HIGHEST,
        preferred_element_type=jnp.float32,
    )
    return (mixed.astype(jnp.bfloat16), request_states)


def solution(mesh):
    return jax.shard_map(
        on_device,
        mesh=mesh,
        in_specs=(
            P("seq", None),
            P(("seq", "tp"), None),
            P(("seq", "tp"), None),
            P(("seq", "tp"), None),
            P(None, "tp"),
            P("tp"),
            P(),
            P(),
            P("tp"),
            P("tp"),
            P("tp"),
            P("tp"),
            P("tp", "seq"),
            P(),
            P(),
        ),
        out_specs=(P(("seq", "tp"), None), P("seq", "tp", None, None)),
        check_vma=False,
    )
```

```python
import functools

import jax
import jax.numpy as jnp
from jax import lax
from jax.experimental import pallas as pl
from jax.experimental.pallas import tpu as pltpu
from jax.sharding import Mesh
from jax.sharding import PartitionSpec as P

INNER = 4096
GROUP = 256
SEQ = ("cs", "core")


epsilon = 1e-05


def from_behind(x, by):
    count = lax.axis_size(SEQ)
    pairs = [(i, i + by) for i in range(count) if 0 <= i + by < count]
    return lax.ppermute(x, SEQ, pairs)


def gather_seq(x):
    chips = lax.all_gather(x, "cs", axis=0, tiled=False)
    return lax.all_gather(chips, "core", axis=0, tiled=False)


def segment_of(position, lengths):
    prompt_ends = jnp.cumsum(lengths)
    return jnp.sum((position[:, None] >= prompt_ends[None, :]).astype(jnp.int32), axis=1)


def scatter_sum_kernel(count, rows, x_ref, o_ref, recv, send_sem, recv_sem):
    me = lax.axis_index("tp")
    barrier = pltpu.get_barrier_semaphore()
    for d in range(1, count):
        peer = lax.rem(me + d, count)
        pl.semaphore_signal(barrier, inc=1, device_id={"tp": peer}, device_id_type=pl.DeviceIdType.MESH)
    pl.semaphore_wait(barrier, count - 1)
    copies = []
    for d in range(1, count):
        peer = lax.rem(me + d, count)
        copy = pltpu.make_async_remote_copy(
            src_ref=x_ref.at[pl.ds(pl.multiple_of(peer * rows, rows), rows)],
            dst_ref=recv.at[me],
            send_sem=send_sem.at[d],
            recv_sem=recv_sem.at[me],
            device_id={"tp": peer},
            device_id_type=pl.DeviceIdType.MESH,
        )
        copy.start()
        copies.append(copy)
    total = x_ref[pl.ds(pl.multiple_of(me * rows, rows), rows), :].astype(jnp.float32)
    for d in range(1, count):
        sender = lax.rem(me + count - d, count)
        arrival = pltpu.make_async_remote_copy(
            src_ref=x_ref.at[pl.ds(0, rows)],
            dst_ref=recv.at[sender],
            send_sem=send_sem.at[d],
            recv_sem=recv_sem.at[sender],
            device_id={"tp": sender},
            device_id_type=pl.DeviceIdType.MESH,
        )
        arrival.wait_recv()
        total = total + recv[sender].astype(jnp.float32)
    for copy in copies:
        copy.wait_send()
    o_ref[...] = total


def scatter_sum(x, count):
    rows = x.shape[0] // count
    cols = x.shape[1]
    return pl.pallas_call(
        functools.partial(scatter_sum_kernel, count, rows),
        out_shape=jax.ShapeDtypeStruct((rows, cols), jnp.float32),
        in_specs=[pl.BlockSpec(memory_space=pltpu.VMEM)],
        out_specs=pl.BlockSpec(memory_space=pltpu.VMEM),
        scratch_shapes=[
            pltpu.VMEM((count, rows, cols), x.dtype),
            pltpu.SemaphoreType.DMA((count,)),
            pltpu.SemaphoreType.DMA((count,)),
        ],
        compiler_params=pltpu.CompilerParams(collective_id=0, has_side_effects=True),
    )(x)


def round_up(n, m):
    return (n + m - 1) // m * m


def on_device(
    tokens,
    w_zx,
    w_dt,
    w_bc,
    conv_x_weight,
    conv_x_bias,
    conv_bc_weight,
    conv_bc_bias,
    dt_bias,
    a_log,
    skip,
    norm_weight,
    w_out,
    lengths,
    request_group,
):
    tp_count = lax.axis_size("tp")
    chip_count = lax.axis_size("cs")
    core_count = lax.axis_size("core")
    seq_count = chip_count * core_count
    seq_index = lax.axis_index("cs") * core_count + lax.axis_index("core")
    tok_dev = tokens.shape[0]
    d_model = tokens.shape[1]
    local_rows = w_zx.shape[0]
    inner_local = conv_x_weight.shape[1]
    heads_local = dt_bias.shape[0]
    head_width = inner_local // heads_local
    bc_width = conv_bc_weight.shape[1]
    state_width = bc_width // 2
    taps = conv_x_weight.shape[0]
    groups_dev = tok_dev // GROUP

    zx_part = w_zx.astype(jnp.bfloat16).reshape(local_rows, 2, tp_count, inner_local)
    zx_part = zx_part.transpose(0, 2, 1, 3).reshape(local_rows, tp_count, 2 * inner_local)
    bc_part = jnp.broadcast_to(
        w_bc.astype(jnp.bfloat16)[:, None, :], (local_rows, tp_count, bc_width)
    )
    dt_part = w_dt.astype(jnp.bfloat16).reshape(local_rows, tp_count, heads_local)
    used = 2 * inner_local + bc_width + heads_local
    width = round_up(used, 128)
    pad_part = jnp.zeros((local_rows, tp_count, width - used), jnp.bfloat16)
    packed = jnp.concatenate([zx_part, bc_part, dt_part, pad_part], axis=2)
    packed = packed.reshape(local_rows, tp_count * width)
    block = lax.all_to_all(packed, "tp", split_axis=1, concat_axis=0, tiled=True)
    block_rows = block.shape[0]
    out_rows, out_cols = w_out.shape
    out_piece = w_out.astype(jnp.bfloat16).T
    gathered = gather_seq(jnp.concatenate([block, out_piece], axis=1))
    gathered = gathered.reshape(seq_count * block_rows, width + out_rows)
    tokens_perm = tokens.reshape(tok_dev, chip_count, core_count, block_rows)
    tokens_perm = tokens_perm.transpose(0, 2, 1, 3).reshape(tok_dev, d_model)
    proj = jnp.dot(tokens_perm, gathered[:, :width], preferred_element_type=jnp.float32)
    zx_low = proj[:, : 2 * inner_local].astype(jnp.bfloat16)
    gate_z = zx_low[:, :inner_local]
    x_raw = zx_low[:, inner_local:]
    bc_raw = proj[:, 2 * inner_local : 2 * inner_local + bc_width].astype(jnp.bfloat16)
    dt_pre = proj[:, 2 * inner_local + bc_width : used]

    raw_mix = jnp.concatenate([x_raw, bc_raw], axis=1)
    conv_weight = jnp.concatenate([conv_x_weight, conv_bc_weight], axis=1)
    conv_bias = jnp.concatenate([conv_x_bias, conv_bc_bias], axis=0)
    rim_rows = from_behind(raw_mix[tok_dev - (taps - 1) :], 1)
    padded = jnp.concatenate([rim_rows, raw_mix], axis=0)
    offset = seq_index * tok_dev
    seg_pad = segment_of(
        offset - (taps - 1) + jnp.arange(tok_dev + taps - 1, dtype=jnp.int32), lengths
    )
    seg_tok = seg_pad[taps - 1 :]
    conv_sum = jnp.zeros((tok_dev, raw_mix.shape[1]), jnp.float32) + conv_bias[None, :]
    for offset_tap in range(taps):
        rows_wide = padded[offset_tap : offset_tap + tok_dev].astype(jnp.float32)
        keep_tap = seg_pad[offset_tap : offset_tap + tok_dev] == seg_tok
        conv_sum = conv_sum + jnp.where(
            keep_tap[:, None], rows_wide * conv_weight[offset_tap][None, :], 0.0
        )
    convolved = jax.nn.silu(conv_sum).astype(jnp.bfloat16)
    inputs = convolved[:, :inner_local].reshape(groups_dev, GROUP, heads_local, head_width)
    b_matrix = convolved[:, inner_local : inner_local + state_width].reshape(
        groups_dev, GROUP, state_width
    )
    c_matrix = convolved[:, inner_local + state_width :].reshape(groups_dev, GROUP, state_width)
    step_size = jax.nn.softplus(dt_pre + dt_bias[None, :]).reshape(groups_dev, GROUP, heads_local)
    step_heads = step_size.transpose(0, 2, 1)
    decay_rate = -jnp.exp(a_log)
    cumul_heads = jnp.cumsum(step_size * decay_rate[None, None, :], axis=1).transpose(0, 2, 1)
    segments = seg_tok.reshape(groups_dev, GROUP)
    seg_before = segment_of(offset + jnp.arange(groups_dev, dtype=jnp.int32) * GROUP - 1, lengths)
    within = jnp.arange(GROUP, dtype=jnp.int32)
    same_prompt = (segments[:, :, None] == segments[:, None, :]) & (
        within[:, None] >= within[None, :]
    )[None]
    log_decay = cumul_heads[:, :, :, None] - cumul_heads[:, :, None, :]
    decay_matrix = jnp.where(
        same_prompt[:, None], jnp.exp(jnp.where(same_prompt[:, None], log_decay, 0.0)), 0.0
    )
    scores = jnp.einsum("cin,cjn->cij", c_matrix, b_matrix, preferred_element_type=jnp.float32)
    mix_weights = (decay_matrix * scores[:, None] * step_heads[:, :, None, :]).astype(jnp.bfloat16)
    diag_out = jnp.einsum(
        "chij,cjhp->cihp", mix_weights, inputs, preferred_element_type=jnp.float32
    )
    last_segment = segments[:, -1]
    tail_weight = (
        jnp.where(
            (segments == last_segment[:, None])[:, None, :],
            jnp.exp(cumul_heads[:, :, -1:] - cumul_heads),
            0.0,
        )
        * step_heads
    )
    b_weighted = (b_matrix.astype(jnp.float32)[:, None] * tail_weight[:, :, :, None]).astype(
        jnp.bfloat16
    )
    contrib = jnp.einsum("cjhp,chjn->chpn", inputs, b_weighted, preferred_element_type=jnp.float32)
    pass_gate = jnp.where(
        (last_segment == seg_before)[:, None], jnp.exp(cumul_heads[:, :, -1]), 0.0
    )

    ends = [contrib[0]]
    for c in range(1, groups_dev):
        ends.append(pass_gate[c][:, None, None] * ends[-1] + contrib[c])
    local_end = jnp.stack(ends)
    local_in = jnp.concatenate([jnp.zeros_like(local_end[:1]), local_end[:-1]], axis=0)
    through_group = jnp.cumprod(pass_gate, axis=0)
    before_group = jnp.concatenate(
        [jnp.ones((1, heads_local), jnp.float32), through_group[:-1]], axis=0
    )

    gate_hi = through_group.astype(jnp.bfloat16)
    gate_lo = (through_group - gate_hi.astype(jnp.float32)).astype(jnp.bfloat16)
    extra = jnp.zeros((groups_dev, heads_local, 8, state_width), jnp.bfloat16)
    extra = extra.at[:, :, 0, :].set(jnp.broadcast_to(gate_hi[:, :, None], gate_hi.shape + (state_width,)))
    extra = extra.at[:, :, 1, :].set(jnp.broadcast_to(gate_lo[:, :, None], gate_lo.shape + (state_width,)))
    sendable = jnp.concatenate([local_end.astype(jnp.bfloat16), extra], axis=2)
    every = gather_seq(sendable).reshape(
        (seq_count * groups_dev, heads_local, head_width + 8, state_width)
    )
    gate_rows = every[:, :, head_width : head_width + 2, :].astype(jnp.float32)
    every_gate = (gate_rows[:, :, 0, 0] + gate_rows[:, :, 1, 0]).reshape(
        seq_count, groups_dev, heads_local
    )
    dev_gate = every_gate[:, -1]
    rows_at = jnp.arange(seq_count, dtype=jnp.int32)
    dev_of = (rows_at % chip_count) * core_count + rows_at // chip_count

    def carry_weights(k):
        between = (dev_of[:, None] < dev_of[None, :]) & (dev_of[None, :] < k)
        factors = jnp.where(between[:, :, None], dev_gate[None, :, :], 1.0)
        return jnp.where((dev_of < k)[:, None], jnp.prod(factors, axis=1), 0.0)

    req_dev = request_group.shape[0] // seq_count
    mine = lax.dynamic_slice_in_dim(request_group, seq_index * req_dev, req_dev)
    req_k = mine // groups_dev
    req_c = mine % groups_dev
    req_row = (req_k % core_count) * chip_count + req_k // core_count
    req_gate = every_gate[req_row, req_c]
    wanted = jnp.concatenate([seq_index[None], req_k])
    weights_all = jax.vmap(carry_weights)(wanted)
    scales = jnp.concatenate([jnp.ones((1, heads_local), jnp.float32), req_gate], axis=0)
    weights_all = weights_all * scales[:, None, :]
    slot_ids = jnp.arange(groups_dev, dtype=jnp.int32)
    last_slot = (slot_ids == groups_dev - 1).astype(jnp.float32)
    coef = weights_all[:, :, None, :] * last_slot[None, None, :, None]
    own_row = jnp.concatenate([jnp.full((1,), -1, jnp.int32), req_row])
    own_slot = jnp.concatenate([jnp.full((1,), -1, jnp.int32), req_c])
    hit = (rows_at[None, :, None] == own_row[:, None, None]) & (
        slot_ids[None, None, :] == own_slot[:, None, None]
    )
    coef = coef + hit[:, :, :, None].astype(jnp.float32)
    coef = coef.reshape(wanted.shape[0], seq_count * groups_dev, heads_local)
    coef_hi = coef.astype(jnp.bfloat16)
    coef_lo = (coef - coef_hi.astype(jnp.float32)).astype(jnp.bfloat16)
    summed_states = jnp.einsum(
        "rjh,jhpn->rhpn", coef_hi, every, preferred_element_type=jnp.float32
    ) + jnp.einsum("rjh,jhpn->rhpn", coef_lo, every, preferred_element_type=jnp.float32)
    carried = summed_states[0, :, :head_width]
    request_states = summed_states[1:, :, :head_width]

    group_in = before_group[:, :, None, None] * carried[None] + local_in
    state_low = group_in.astype(jnp.bfloat16)
    carry_keep = jnp.where((segments == seg_before[:, None])[:, None, :], jnp.exp(cumul_heads), 0.0)
    carry_out = jnp.einsum(
        "cin,chpn->cihp", c_matrix, state_low, preferred_element_type=jnp.float32
    )
    carry_out = carry_out * carry_keep.transpose(0, 2, 1)[:, :, :, None]
    y_local = diag_out + carry_out + skip[None, None, :, None] * inputs.astype(jnp.float32)
    y_local = y_local.reshape(tok_dev, inner_local)
    gated = y_local * jax.nn.silu(gate_z.astype(jnp.float32))
    square_sum = jnp.sum(gated * gated, axis=1)
    scaled = (gated * norm_weight[None, :]).astype(jnp.bfloat16)
    partial = lax.dot_general(
        scaled, gathered[:, width:], (((1,), (1,)), ((), ())), preferred_element_type=jnp.float32
    )
    partial = partial.reshape(tok_dev, core_count, chip_count, out_cols)
    partial = partial.transpose(0, 2, 1, 3).reshape(tok_dev, d_model)
    side = jnp.zeros((tok_dev, 128), jnp.float32).at[:, 0].set(square_sum)
    summed = scatter_sum(jnp.concatenate([partial, side], axis=1).astype(jnp.bfloat16), tp_count)
    mean_square = summed[:, d_model] / INNER
    mixed = (summed[:, :d_model] * lax.rsqrt(mean_square + epsilon)[:, None]).astype(jnp.bfloat16)
    return (mixed, request_states)


def solution(mesh):
    seq_n, tp_n = mesh.devices.shape
    view = Mesh(mesh.devices.reshape(seq_n // 2, 2, tp_n), ("cs", "core", "tp"))
    return jax.shard_map(
        on_device,
        mesh=view,
        in_specs=(
            P(SEQ, None),
            P((*SEQ, "tp"), None),
            P((*SEQ, "tp"), None),
            P((*SEQ, "tp"), None),
            P(None, "tp"),
            P("tp"),
            P(),
            P(),
            P("tp"),
            P("tp"),
            P("tp"),
            P("tp"),
            P("tp", SEQ),
            P(),
            P(),
        ),
        out_specs=(P((*SEQ, "tp"), None), P(SEQ, "tp", None, None)),
        check_vma=False,
    )
```

```python
import functools

import jax
import jax.numpy as jnp
from jax import lax
from jax.experimental import pallas as pl
from jax.experimental.pallas import tpu as pltpu
from jax.sharding import PartitionSpec as P

INNER = 4096
GROUP = 256
SEQ = "seq"


epsilon = 1e-05


def from_behind(x, by):
    count = lax.axis_size(SEQ)
    pairs = [(i, i + by) for i in range(count) if 0 <= i + by < count]
    return lax.ppermute(x, SEQ, pairs)


def gather_seq(x):
    return lax.all_gather(x, SEQ, axis=0, tiled=False)


def segment_of(position, lengths):
    prompt_ends = jnp.cumsum(lengths)
    return jnp.sum((position[:, None] >= prompt_ends[None, :]).astype(jnp.int32), axis=1)


def scatter_sum_kernel(count, rows, x_ref, o_ref, recv, send_sem, recv_sem):
    me = lax.axis_index("tp")
    barrier = pltpu.get_barrier_semaphore()
    for d in range(1, count):
        peer = lax.rem(me + d, count)
        pl.semaphore_signal(barrier, inc=1, device_id={"tp": peer}, device_id_type=pl.DeviceIdType.MESH)
    pl.semaphore_wait(barrier, count - 1)
    copies = []
    for d in range(1, count):
        peer = lax.rem(me + d, count)
        copy = pltpu.make_async_remote_copy(
            src_ref=x_ref.at[pl.ds(pl.multiple_of(peer * rows, rows), rows)],
            dst_ref=recv.at[me],
            send_sem=send_sem.at[d],
            recv_sem=recv_sem.at[me],
            device_id={"tp": peer},
            device_id_type=pl.DeviceIdType.MESH,
        )
        copy.start()
        copies.append(copy)
    total = x_ref[pl.ds(pl.multiple_of(me * rows, rows), rows), :].astype(jnp.float32)
    for d in range(1, count):
        sender = lax.rem(me + count - d, count)
        arrival = pltpu.make_async_remote_copy(
            src_ref=x_ref.at[pl.ds(0, rows)],
            dst_ref=recv.at[sender],
            send_sem=send_sem.at[d],
            recv_sem=recv_sem.at[sender],
            device_id={"tp": sender},
            device_id_type=pl.DeviceIdType.MESH,
        )
        arrival.wait_recv()
        total = total + recv[sender].astype(jnp.float32)
    for copy in copies:
        copy.wait_send()
    o_ref[...] = total


def scatter_sum(x, count):
    rows = x.shape[0] // count
    cols = x.shape[1]
    return pl.pallas_call(
        functools.partial(scatter_sum_kernel, count, rows),
        out_shape=jax.ShapeDtypeStruct((rows, cols), jnp.float32),
        in_specs=[pl.BlockSpec(memory_space=pltpu.VMEM)],
        out_specs=pl.BlockSpec(memory_space=pltpu.VMEM),
        scratch_shapes=[
            pltpu.VMEM((count, rows, cols), x.dtype),
            pltpu.SemaphoreType.DMA((count,)),
            pltpu.SemaphoreType.DMA((count,)),
        ],
        compiler_params=pltpu.CompilerParams(collective_id=0, has_side_effects=True),
    )(x)


def round_up(n, m):
    return (n + m - 1) // m * m


def on_device(
    tokens,
    w_zx,
    w_dt,
    w_bc,
    conv_x_weight,
    conv_x_bias,
    conv_bc_weight,
    conv_bc_bias,
    dt_bias,
    a_log,
    skip,
    norm_weight,
    w_out,
    lengths,
    request_group,
):
    tp_count = lax.axis_size("tp")
    seq_count = lax.axis_size(SEQ)
    seq_index = lax.axis_index(SEQ)
    tok_dev = tokens.shape[0]
    d_model = tokens.shape[1]
    local_rows = w_zx.shape[0]
    inner_local = conv_x_weight.shape[1]
    heads_local = dt_bias.shape[0]
    head_width = inner_local // heads_local
    bc_width = conv_bc_weight.shape[1]
    state_width = bc_width // 2
    taps = conv_x_weight.shape[0]
    groups_dev = tok_dev // GROUP

    zx_part = w_zx.astype(jnp.bfloat16).reshape(local_rows, 2, tp_count, inner_local)
    zx_part = zx_part.transpose(0, 2, 1, 3).reshape(local_rows, tp_count, 2 * inner_local)
    bc_part = jnp.broadcast_to(
        w_bc.astype(jnp.bfloat16)[:, None, :], (local_rows, tp_count, bc_width)
    )
    dt_part = w_dt.astype(jnp.bfloat16).reshape(local_rows, tp_count, heads_local)
    used = 2 * inner_local + bc_width + heads_local
    width = round_up(used, 128)
    pad_part = jnp.zeros((local_rows, tp_count, width - used), jnp.bfloat16)
    packed = jnp.concatenate([zx_part, bc_part, dt_part, pad_part], axis=2)
    packed = packed.reshape(local_rows, tp_count * width)
    block = lax.all_to_all(packed, "tp", split_axis=1, concat_axis=0, tiled=True)
    block_rows = block.shape[0]
    out_rows, out_cols = w_out.shape
    out_piece = w_out.astype(jnp.bfloat16).T
    gathered = gather_seq(jnp.concatenate([block, out_piece], axis=1))
    gathered = gathered.reshape(seq_count * block_rows, width + out_rows)
    proj = jnp.dot(tokens, gathered[:, :width], preferred_element_type=jnp.float32)
    zx_low = proj[:, : 2 * inner_local].astype(jnp.bfloat16)
    gate_z = zx_low[:, :inner_local]
    x_raw = zx_low[:, inner_local:]
    bc_raw = proj[:, 2 * inner_local : 2 * inner_local + bc_width].astype(jnp.bfloat16)
    dt_pre = proj[:, 2 * inner_local + bc_width : used]

    raw_mix = jnp.concatenate([x_raw, bc_raw], axis=1)
    conv_weight = jnp.concatenate([conv_x_weight, conv_bc_weight], axis=1)
    conv_bias = jnp.concatenate([conv_x_bias, conv_bc_bias], axis=0)
    rim_rows = from_behind(raw_mix[tok_dev - (taps - 1) :], 1)
    padded = jnp.concatenate([rim_rows, raw_mix], axis=0)
    offset = seq_index * tok_dev
    seg_pad = segment_of(
        offset - (taps - 1) + jnp.arange(tok_dev + taps - 1, dtype=jnp.int32), lengths
    )
    seg_tok = seg_pad[taps - 1 :]
    conv_sum = jnp.zeros((tok_dev, raw_mix.shape[1]), jnp.float32) + conv_bias[None, :]
    for offset_tap in range(taps):
        rows_wide = padded[offset_tap : offset_tap + tok_dev].astype(jnp.float32)
        keep_tap = seg_pad[offset_tap : offset_tap + tok_dev] == seg_tok
        conv_sum = conv_sum + jnp.where(
            keep_tap[:, None], rows_wide * conv_weight[offset_tap][None, :], 0.0
        )
    convolved = jax.nn.silu(conv_sum).astype(jnp.bfloat16)
    inputs = convolved[:, :inner_local].reshape(groups_dev, GROUP, heads_local, head_width)
    b_matrix = convolved[:, inner_local : inner_local + state_width].reshape(
        groups_dev, GROUP, state_width
    )
    c_matrix = convolved[:, inner_local + state_width :].reshape(groups_dev, GROUP, state_width)
    step_size = jax.nn.softplus(dt_pre + dt_bias[None, :]).reshape(groups_dev, GROUP, heads_local)
    step_heads = step_size.transpose(0, 2, 1)
    decay_rate = -jnp.exp(a_log)
    cumul_heads = jnp.cumsum(step_size * decay_rate[None, None, :], axis=1).transpose(0, 2, 1)
    segments = seg_tok.reshape(groups_dev, GROUP)
    seg_before = segment_of(offset + jnp.arange(groups_dev, dtype=jnp.int32) * GROUP - 1, lengths)
    within = jnp.arange(GROUP, dtype=jnp.int32)
    same_prompt = (segments[:, :, None] == segments[:, None, :]) & (
        within[:, None] >= within[None, :]
    )[None]
    log_decay = cumul_heads[:, :, :, None] - cumul_heads[:, :, None, :]
    decay_matrix = jnp.where(
        same_prompt[:, None], jnp.exp(jnp.where(same_prompt[:, None], log_decay, 0.0)), 0.0
    )
    scores = jnp.einsum("cin,cjn->cij", c_matrix, b_matrix, preferred_element_type=jnp.float32)
    mix_weights = (decay_matrix * scores[:, None] * step_heads[:, :, None, :]).astype(jnp.bfloat16)
    diag_out = jnp.einsum(
        "chij,cjhp->cihp", mix_weights, inputs, preferred_element_type=jnp.float32
    )
    last_segment = segments[:, -1]
    tail_weight = (
        jnp.where(
            (segments == last_segment[:, None])[:, None, :],
            jnp.exp(cumul_heads[:, :, -1:] - cumul_heads),
            0.0,
        )
        * step_heads
    )
    b_weighted = (b_matrix.astype(jnp.float32)[:, None] * tail_weight[:, :, :, None]).astype(
        jnp.bfloat16
    )
    contrib = jnp.einsum("cjhp,chjn->chpn", inputs, b_weighted, preferred_element_type=jnp.float32)
    pass_gate = jnp.where(
        (last_segment == seg_before)[:, None], jnp.exp(cumul_heads[:, :, -1]), 0.0
    )

    ends = [contrib[0]]
    for c in range(1, groups_dev):
        ends.append(pass_gate[c][:, None, None] * ends[-1] + contrib[c])
    local_end = jnp.stack(ends)
    local_in = jnp.concatenate([jnp.zeros_like(local_end[:1]), local_end[:-1]], axis=0)
    through_group = jnp.cumprod(pass_gate, axis=0)
    before_group = jnp.concatenate(
        [jnp.ones((1, heads_local), jnp.float32), through_group[:-1]], axis=0
    )

    gate_hi = through_group.astype(jnp.bfloat16)
    gate_lo = (through_group - gate_hi.astype(jnp.float32)).astype(jnp.bfloat16)
    extra = jnp.zeros((groups_dev, heads_local, 8, state_width), jnp.bfloat16)
    extra = extra.at[:, :, 0, :].set(jnp.broadcast_to(gate_hi[:, :, None], gate_hi.shape + (state_width,)))
    extra = extra.at[:, :, 1, :].set(jnp.broadcast_to(gate_lo[:, :, None], gate_lo.shape + (state_width,)))
    sendable = jnp.concatenate([local_end.astype(jnp.bfloat16), extra], axis=2)
    every = gather_seq(sendable).reshape(
        (seq_count * groups_dev, heads_local, head_width + 8, state_width)
    )
    gate_rows = every[:, :, head_width : head_width + 2, :].astype(jnp.float32)
    every_gate = (gate_rows[:, :, 0, 0] + gate_rows[:, :, 1, 0]).reshape(
        seq_count, groups_dev, heads_local
    )
    dev_gate = every_gate[:, -1]
    rows_at = jnp.arange(seq_count, dtype=jnp.int32)
    dev_of = rows_at

    def carry_weights(k):
        between = (dev_of[:, None] < dev_of[None, :]) & (dev_of[None, :] < k)
        factors = jnp.where(between[:, :, None], dev_gate[None, :, :], 1.0)
        return jnp.where((dev_of < k)[:, None], jnp.prod(factors, axis=1), 0.0)

    req_dev = request_group.shape[0] // seq_count
    mine = lax.dynamic_slice_in_dim(request_group, seq_index * req_dev, req_dev)
    req_k = mine // groups_dev
    req_c = mine % groups_dev
    req_row = req_k
    req_gate = every_gate[req_row, req_c]
    wanted = jnp.concatenate([seq_index[None], req_k])
    weights_all = jax.vmap(carry_weights)(wanted)
    scales = jnp.concatenate([jnp.ones((1, heads_local), jnp.float32), req_gate], axis=0)
    weights_all = weights_all * scales[:, None, :]
    slot_ids = jnp.arange(groups_dev, dtype=jnp.int32)
    last_slot = (slot_ids == groups_dev - 1).astype(jnp.float32)
    coef = weights_all[:, :, None, :] * last_slot[None, None, :, None]
    own_row = jnp.concatenate([jnp.full((1,), -1, jnp.int32), req_row])
    own_slot = jnp.concatenate([jnp.full((1,), -1, jnp.int32), req_c])
    hit = (rows_at[None, :, None] == own_row[:, None, None]) & (
        slot_ids[None, None, :] == own_slot[:, None, None]
    )
    coef = coef + hit[:, :, :, None].astype(jnp.float32)
    coef = coef.reshape(wanted.shape[0], seq_count * groups_dev, heads_local)
    coef_hi = coef.astype(jnp.bfloat16)
    coef_lo = (coef - coef_hi.astype(jnp.float32)).astype(jnp.bfloat16)
    summed_states = jnp.einsum(
        "rjh,jhpn->rhpn", coef_hi, every, preferred_element_type=jnp.float32
    ) + jnp.einsum("rjh,jhpn->rhpn", coef_lo, every, preferred_element_type=jnp.float32)
    carried = summed_states[0, :, :head_width]
    request_states = summed_states[1:, :, :head_width]

    group_in = before_group[:, :, None, None] * carried[None] + local_in
    state_low = group_in.astype(jnp.bfloat16)
    carry_keep = jnp.where((segments == seg_before[:, None])[:, None, :], jnp.exp(cumul_heads), 0.0)
    carry_out = jnp.einsum(
        "cin,chpn->cihp", c_matrix, state_low, preferred_element_type=jnp.float32
    )
    carry_out = carry_out * carry_keep.transpose(0, 2, 1)[:, :, :, None]
    y_local = diag_out + carry_out + skip[None, None, :, None] * inputs.astype(jnp.float32)
    y_local = y_local.reshape(tok_dev, inner_local)
    gated = y_local * jax.nn.silu(gate_z.astype(jnp.float32))
    square_sum = jnp.sum(gated * gated, axis=1)
    scaled = (gated * norm_weight[None, :]).astype(jnp.bfloat16)
    partial = lax.dot_general(
        scaled, gathered[:, width:], (((1,), (1,)), ((), ())), preferred_element_type=jnp.float32
    )
    side = jnp.zeros((tok_dev, 128), jnp.float32).at[:, 0].set(square_sum)
    summed = scatter_sum(jnp.concatenate([partial, side], axis=1).astype(jnp.bfloat16), tp_count)
    mean_square = summed[:, d_model] / INNER
    mixed = (summed[:, :d_model] * lax.rsqrt(mean_square + epsilon)[:, None]).astype(jnp.bfloat16)
    return (mixed, request_states)


def solution(mesh):
    return jax.shard_map(
        on_device,
        mesh=mesh,
        in_specs=(
            P(SEQ, None),
            P((SEQ, "tp"), None),
            P((SEQ, "tp"), None),
            P((SEQ, "tp"), None),
            P(None, "tp"),
            P("tp"),
            P(),
            P(),
            P("tp"),
            P("tp"),
            P("tp"),
            P("tp"),
            P("tp", SEQ),
            P(),
            P(),
        ),
        out_specs=(P((SEQ, "tp"), None), P(SEQ, "tp", None, None)),
        check_vma=False,
    )
```

```python
import functools

import jax
import jax.numpy as jnp
from jax import lax
from jax.experimental import pallas as pl
from jax.experimental.pallas import tpu as pltpu
from jax.sharding import PartitionSpec as P

INNER = 4096
GROUP = 256
SEQ = "seq"


epsilon = 1e-05


def from_behind(x, by):
    count = lax.axis_size(SEQ)
    pairs = [(i, i + by) for i in range(count) if 0 <= i + by < count]
    return lax.ppermute(x, SEQ, pairs)


def gather_seq(x):
    return lax.all_gather(x, SEQ, axis=0, tiled=False)


def segment_of(position, lengths):
    prompt_ends = jnp.cumsum(lengths)
    return jnp.sum((position[:, None] >= prompt_ends[None, :]).astype(jnp.int32), axis=1)


def scatter_sum_kernel(count, rows, x_ref, o_ref, recv, send_sem, recv_sem):
    me = lax.axis_index("tp")
    barrier = pltpu.get_barrier_semaphore()
    for d in range(1, count):
        peer = lax.rem(me + d, count)
        pl.semaphore_signal(barrier, inc=1, device_id={"tp": peer}, device_id_type=pl.DeviceIdType.MESH)
    pl.semaphore_wait(barrier, count - 1)
    copies = []
    for d in range(1, count):
        peer = lax.rem(me + d, count)
        copy = pltpu.make_async_remote_copy(
            src_ref=x_ref.at[pl.ds(pl.multiple_of(peer * rows, rows), rows)],
            dst_ref=recv.at[me],
            send_sem=send_sem.at[d],
            recv_sem=recv_sem.at[me],
            device_id={"tp": peer},
            device_id_type=pl.DeviceIdType.MESH,
        )
        copy.start()
        copies.append(copy)
    total = x_ref[pl.ds(pl.multiple_of(me * rows, rows), rows), :].astype(jnp.float32)
    for d in range(1, count):
        sender = lax.rem(me + count - d, count)
        arrival = pltpu.make_async_remote_copy(
            src_ref=x_ref.at[pl.ds(0, rows)],
            dst_ref=recv.at[sender],
            send_sem=send_sem.at[d],
            recv_sem=recv_sem.at[sender],
            device_id={"tp": sender},
            device_id_type=pl.DeviceIdType.MESH,
        )
        arrival.wait_recv()
        total = total + recv[sender].astype(jnp.float32)
    for copy in copies:
        copy.wait_send()
    o_ref[...] = total


def scatter_sum(x, count):
    rows = x.shape[0] // count
    cols = x.shape[1]
    return pl.pallas_call(
        functools.partial(scatter_sum_kernel, count, rows),
        out_shape=jax.ShapeDtypeStruct((rows, cols), jnp.float32),
        in_specs=[pl.BlockSpec(memory_space=pltpu.VMEM)],
        out_specs=pl.BlockSpec(memory_space=pltpu.VMEM),
        scratch_shapes=[
            pltpu.VMEM((count, rows, cols), x.dtype),
            pltpu.SemaphoreType.DMA((count,)),
            pltpu.SemaphoreType.DMA((count,)),
        ],
        compiler_params=pltpu.CompilerParams(collective_id=0, has_side_effects=True),
    )(x)


def carry_kernel(count, width, mine_ref, out_ref, recv, acc, send_sem, recv_sem):
    me = lax.axis_index(SEQ)
    barrier = pltpu.get_barrier_semaphore()
    for d in range(1, count):
        peer = lax.rem(me + d, count)
        pl.semaphore_signal(barrier, inc=1, device_id={SEQ: peer}, device_id_type=pl.DeviceIdType.MESH)
    pl.semaphore_wait(barrier, count - 1)

    def send_to(d):
        return pltpu.make_async_remote_copy(
            src_ref=mine_ref,
            dst_ref=recv.at[me],
            send_sem=send_sem.at[d],
            recv_sem=recv_sem.at[me],
            device_id={SEQ: me + d},
            device_id_type=pl.DeviceIdType.MESH,
        )

    for d in range(1, count):
        @pl.when(me + d < count)
        def _():
            send_to(d).start()

    acc[...] = jnp.zeros_like(acc)
    for j in range(count - 1):
        @pl.when(j < me)
        def _():
            pltpu.make_async_remote_copy(
                src_ref=mine_ref,
                dst_ref=recv.at[j],
                send_sem=send_sem.at[0],
                recv_sem=recv_sem.at[j],
                device_id={SEQ: j},
                device_id_type=pl.DeviceIdType.MESH,
            ).wait_recv()
            tail = recv[j, :, width : width + 16, :].astype(jnp.float32)
            gate = tail[:, 0:1, :] + tail[:, 1:2, :]
            acc[...] = gate * acc[...] + recv[j, :, :width, :].astype(jnp.float32)

    for d in range(1, count):
        @pl.when(me + d < count)
        def _():
            send_to(d).wait_send()
    out_ref[...] = acc[...]


def carry_in(mine, width):
    count = lax.axis_size(SEQ)
    heads, _, lanes = mine.shape
    return pl.pallas_call(
        functools.partial(carry_kernel, count, width),
        out_shape=jax.ShapeDtypeStruct((heads, width, lanes), jnp.float32),
        in_specs=[pl.BlockSpec(memory_space=pltpu.VMEM)],
        out_specs=pl.BlockSpec(memory_space=pltpu.VMEM),
        scratch_shapes=[
            pltpu.VMEM((count,) + mine.shape, mine.dtype),
            pltpu.VMEM((heads, width, lanes), jnp.float32),
            pltpu.SemaphoreType.DMA((count,)),
            pltpu.SemaphoreType.DMA((count,)),
        ],
        compiler_params=pltpu.CompilerParams(collective_id=1, has_side_effects=True),
    )(mine)


def round_up(n, m):
    return (n + m - 1) // m * m


def on_device(
    tokens,
    w_zx,
    w_dt,
    w_bc,
    conv_x_weight,
    conv_x_bias,
    conv_bc_weight,
    conv_bc_bias,
    dt_bias,
    a_log,
    skip,
    norm_weight,
    w_out,
    lengths,
    request_group,
):
    tp_count = lax.axis_size("tp")
    seq_count = lax.axis_size(SEQ)
    seq_index = lax.axis_index(SEQ)
    tok_dev = tokens.shape[0]
    d_model = tokens.shape[1]
    local_rows = w_zx.shape[0]
    inner_local = conv_x_weight.shape[1]
    heads_local = dt_bias.shape[0]
    head_width = inner_local // heads_local
    bc_width = conv_bc_weight.shape[1]
    state_width = bc_width // 2
    taps = conv_x_weight.shape[0]
    groups_dev = tok_dev // GROUP

    zx_part = w_zx.astype(jnp.bfloat16).reshape(local_rows, 2, tp_count, inner_local)
    zx_part = zx_part.transpose(0, 2, 1, 3).reshape(local_rows, tp_count, 2 * inner_local)
    bc_part = jnp.broadcast_to(
        w_bc.astype(jnp.bfloat16)[:, None, :], (local_rows, tp_count, bc_width)
    )
    dt_part = w_dt.astype(jnp.bfloat16).reshape(local_rows, tp_count, heads_local)
    used = 2 * inner_local + bc_width + heads_local
    width = round_up(used, 128)
    pad_part = jnp.zeros((local_rows, tp_count, width - used), jnp.bfloat16)
    packed = jnp.concatenate([zx_part, bc_part, dt_part, pad_part], axis=2)
    packed = packed.reshape(local_rows, tp_count * width)
    block = lax.all_to_all(packed, "tp", split_axis=1, concat_axis=0, tiled=True)
    block_rows = block.shape[0]
    out_rows, out_cols = w_out.shape
    out_piece = w_out.astype(jnp.bfloat16).T
    gathered = gather_seq(jnp.concatenate([block, out_piece], axis=1))
    gathered = gathered.reshape(seq_count * block_rows, width + out_rows)
    proj = jnp.dot(tokens, gathered[:, :width], preferred_element_type=jnp.float32)
    zx_low = proj[:, : 2 * inner_local].astype(jnp.bfloat16)
    gate_z = zx_low[:, :inner_local]
    x_raw = zx_low[:, inner_local:]
    bc_raw = proj[:, 2 * inner_local : 2 * inner_local + bc_width].astype(jnp.bfloat16)
    dt_pre = proj[:, 2 * inner_local + bc_width : used]

    raw_mix = jnp.concatenate([x_raw, bc_raw], axis=1)
    conv_weight = jnp.concatenate([conv_x_weight, conv_bc_weight], axis=1)
    conv_bias = jnp.concatenate([conv_x_bias, conv_bc_bias], axis=0)
    rim_rows = from_behind(raw_mix[tok_dev - (taps - 1) :], 1)
    padded = jnp.concatenate([rim_rows, raw_mix], axis=0)
    offset = seq_index * tok_dev
    seg_pad = segment_of(
        offset - (taps - 1) + jnp.arange(tok_dev + taps - 1, dtype=jnp.int32), lengths
    )
    seg_tok = seg_pad[taps - 1 :]
    conv_sum = jnp.zeros((tok_dev, raw_mix.shape[1]), jnp.float32) + conv_bias[None, :]
    for offset_tap in range(taps):
        rows_wide = padded[offset_tap : offset_tap + tok_dev].astype(jnp.float32)
        keep_tap = seg_pad[offset_tap : offset_tap + tok_dev] == seg_tok
        conv_sum = conv_sum + jnp.where(
            keep_tap[:, None], rows_wide * conv_weight[offset_tap][None, :], 0.0
        )
    convolved = jax.nn.silu(conv_sum).astype(jnp.bfloat16)
    inputs = convolved[:, :inner_local].reshape(groups_dev, GROUP, heads_local, head_width)
    b_matrix = convolved[:, inner_local : inner_local + state_width].reshape(
        groups_dev, GROUP, state_width
    )
    c_matrix = convolved[:, inner_local + state_width :].reshape(groups_dev, GROUP, state_width)
    step_size = jax.nn.softplus(dt_pre + dt_bias[None, :]).reshape(groups_dev, GROUP, heads_local)
    step_heads = step_size.transpose(0, 2, 1)
    decay_rate = -jnp.exp(a_log)
    cumul_heads = jnp.cumsum(step_size * decay_rate[None, None, :], axis=1).transpose(0, 2, 1)
    segments = seg_tok.reshape(groups_dev, GROUP)
    seg_before = segment_of(offset + jnp.arange(groups_dev, dtype=jnp.int32) * GROUP - 1, lengths)
    within = jnp.arange(GROUP, dtype=jnp.int32)
    same_prompt = (segments[:, :, None] == segments[:, None, :]) & (
        within[:, None] >= within[None, :]
    )[None]
    log_decay = cumul_heads[:, :, :, None] - cumul_heads[:, :, None, :]
    decay_matrix = jnp.where(
        same_prompt[:, None], jnp.exp(jnp.where(same_prompt[:, None], log_decay, 0.0)), 0.0
    )
    scores = jnp.einsum("cin,cjn->cij", c_matrix, b_matrix, preferred_element_type=jnp.float32)
    mix_weights = (decay_matrix * scores[:, None] * step_heads[:, :, None, :]).astype(jnp.bfloat16)
    diag_out = jnp.einsum(
        "chij,cjhp->cihp", mix_weights, inputs, preferred_element_type=jnp.float32
    )
    last_segment = segments[:, -1]
    tail_weight = (
        jnp.where(
            (segments == last_segment[:, None])[:, None, :],
            jnp.exp(cumul_heads[:, :, -1:] - cumul_heads),
            0.0,
        )
        * step_heads
    )
    b_weighted = (b_matrix.astype(jnp.float32)[:, None] * tail_weight[:, :, :, None]).astype(
        jnp.bfloat16
    )
    contrib = jnp.einsum("cjhp,chjn->chpn", inputs, b_weighted, preferred_element_type=jnp.float32)
    pass_gate = jnp.where(
        (last_segment == seg_before)[:, None], jnp.exp(cumul_heads[:, :, -1]), 0.0
    )

    ends = [contrib[0]]
    for c in range(1, groups_dev):
        ends.append(pass_gate[c][:, None, None] * ends[-1] + contrib[c])
    local_end = jnp.stack(ends)
    local_in = jnp.concatenate([jnp.zeros_like(local_end[:1]), local_end[:-1]], axis=0)
    through_group = jnp.cumprod(pass_gate, axis=0)
    before_group = jnp.concatenate(
        [jnp.ones((1, heads_local), jnp.float32), through_group[:-1]], axis=0
    )

    gate_hi = through_group.astype(jnp.bfloat16)
    gate_lo = (through_group - gate_hi.astype(jnp.float32)).astype(jnp.bfloat16)
    extra = jnp.zeros((groups_dev, heads_local, 16, state_width), jnp.bfloat16)
    extra = extra.at[:, :, 0, :].set(jnp.broadcast_to(gate_hi[:, :, None], gate_hi.shape + (state_width,)))
    extra = extra.at[:, :, 1, :].set(jnp.broadcast_to(gate_lo[:, :, None], gate_lo.shape + (state_width,)))
    sendable = jnp.concatenate([local_end.astype(jnp.bfloat16), extra], axis=2)
    carried = carry_in(sendable[-1], head_width)
    every = gather_seq(sendable).reshape(
        (seq_count * groups_dev, heads_local, head_width + 16, state_width)
    )
    gate_rows = every[:, :, head_width : head_width + 2, :].astype(jnp.float32)
    every_gate = (gate_rows[:, :, 0, 0] + gate_rows[:, :, 1, 0]).reshape(
        seq_count, groups_dev, heads_local
    )
    dev_gate = every_gate[:, -1]
    rows_at = jnp.arange(seq_count, dtype=jnp.int32)
    dev_of = rows_at

    def carry_weights(k):
        between = (dev_of[:, None] < dev_of[None, :]) & (dev_of[None, :] < k)
        factors = jnp.where(between[:, :, None], dev_gate[None, :, :], 1.0)
        return jnp.where((dev_of < k)[:, None], jnp.prod(factors, axis=1), 0.0)

    req_dev = request_group.shape[0] // seq_count
    mine = lax.dynamic_slice_in_dim(request_group, seq_index * req_dev, req_dev)
    req_k = mine // groups_dev
    req_c = mine % groups_dev
    req_row = req_k
    req_gate = every_gate[req_row, req_c]
    wanted = req_k
    weights_all = jax.vmap(carry_weights)(wanted)
    weights_all = weights_all * req_gate[:, None, :]
    slot_ids = jnp.arange(groups_dev, dtype=jnp.int32)
    last_slot = (slot_ids == groups_dev - 1).astype(jnp.float32)
    coef = weights_all[:, :, None, :] * last_slot[None, None, :, None]
    own_row = req_row
    own_slot = req_c
    hit = (rows_at[None, :, None] == own_row[:, None, None]) & (
        slot_ids[None, None, :] == own_slot[:, None, None]
    )
    coef = coef + hit[:, :, :, None].astype(jnp.float32)
    coef = coef.reshape(wanted.shape[0], seq_count * groups_dev, heads_local)
    coef_hi = coef.astype(jnp.bfloat16)
    coef_lo = (coef - coef_hi.astype(jnp.float32)).astype(jnp.bfloat16)
    summed_states = jnp.einsum(
        "rjh,jhpn->rhpn", coef_hi, every, preferred_element_type=jnp.float32
    ) + jnp.einsum("rjh,jhpn->rhpn", coef_lo, every, preferred_element_type=jnp.float32)
    request_states = summed_states[:, :, :head_width]

    group_in = before_group[:, :, None, None] * carried[None] + local_in
    state_low = group_in.astype(jnp.bfloat16)
    carry_keep = jnp.where((segments == seg_before[:, None])[:, None, :], jnp.exp(cumul_heads), 0.0)
    carry_out = jnp.einsum(
        "cin,chpn->cihp", c_matrix, state_low, preferred_element_type=jnp.float32
    )
    carry_out = carry_out * carry_keep.transpose(0, 2, 1)[:, :, :, None]
    y_local = diag_out + carry_out + skip[None, None, :, None] * inputs.astype(jnp.float32)
    y_local = y_local.reshape(tok_dev, inner_local)
    gated = y_local * jax.nn.silu(gate_z.astype(jnp.float32))
    square_sum = jnp.sum(gated * gated, axis=1)
    scaled = (gated * norm_weight[None, :]).astype(jnp.bfloat16)
    partial = lax.dot_general(
        scaled, gathered[:, width:], (((1,), (1,)), ((), ())), preferred_element_type=jnp.float32
    )
    side = jnp.zeros((tok_dev, 128), jnp.float32).at[:, 0].set(square_sum)
    summed = scatter_sum(jnp.concatenate([partial, side], axis=1).astype(jnp.bfloat16), tp_count)
    mean_square = summed[:, d_model] / INNER
    mixed = (summed[:, :d_model] * lax.rsqrt(mean_square + epsilon)[:, None]).astype(jnp.bfloat16)
    return (mixed, request_states)


def solution(mesh):
    return jax.shard_map(
        on_device,
        mesh=mesh,
        in_specs=(
            P(SEQ, None),
            P((SEQ, "tp"), None),
            P((SEQ, "tp"), None),
            P((SEQ, "tp"), None),
            P(None, "tp"),
            P("tp"),
            P(),
            P(),
            P("tp"),
            P("tp"),
            P("tp"),
            P("tp"),
            P("tp", SEQ),
            P(),
            P(),
        ),
        out_specs=(P((SEQ, "tp"), None), P(SEQ, "tp", None, None)),
        check_vma=False,
    )
```

```python
import functools

import jax
import jax.numpy as jnp
from jax import lax
from jax.experimental import pallas as pl
from jax.experimental.pallas import tpu as pltpu
from jax.sharding import PartitionSpec as P

INNER = 4096
GROUP = 256
SEQ = "seq"


epsilon = 1e-05


def from_behind(x, by):
    count = lax.axis_size(SEQ)
    pairs = [(i, i + by) for i in range(count) if 0 <= i + by < count]
    return lax.ppermute(x, SEQ, pairs)


def gather_seq(x):
    return lax.all_gather(x, SEQ, axis=0, tiled=False)


def segment_of(position, lengths):
    prompt_ends = jnp.cumsum(lengths)
    return jnp.sum((position[:, None] >= prompt_ends[None, :]).astype(jnp.int32), axis=1)


def scatter_sum_kernel(count, rows, x_ref, o_ref, recv, send_sem, recv_sem):
    me = lax.axis_index("tp")
    barrier = pltpu.get_barrier_semaphore()
    for d in range(1, count):
        peer = lax.rem(me + d, count)
        pl.semaphore_signal(barrier, inc=1, device_id={"tp": peer}, device_id_type=pl.DeviceIdType.MESH)
    pl.semaphore_wait(barrier, count - 1)
    copies = []
    for d in range(1, count):
        peer = lax.rem(me + d, count)
        copy = pltpu.make_async_remote_copy(
            src_ref=x_ref.at[pl.ds(pl.multiple_of(peer * rows, rows), rows)],
            dst_ref=recv.at[me],
            send_sem=send_sem.at[d],
            recv_sem=recv_sem.at[me],
            device_id={"tp": peer},
            device_id_type=pl.DeviceIdType.MESH,
        )
        copy.start()
        copies.append(copy)
    total = x_ref[pl.ds(pl.multiple_of(me * rows, rows), rows), :].astype(jnp.float32)
    for d in range(1, count):
        sender = lax.rem(me + count - d, count)
        arrival = pltpu.make_async_remote_copy(
            src_ref=x_ref.at[pl.ds(0, rows)],
            dst_ref=recv.at[sender],
            send_sem=send_sem.at[d],
            recv_sem=recv_sem.at[sender],
            device_id={"tp": sender},
            device_id_type=pl.DeviceIdType.MESH,
        )
        arrival.wait_recv()
        total = total + recv[sender].astype(jnp.float32)
    for copy in copies:
        copy.wait_send()
    o_ref[...] = total


def scatter_sum(x, count):
    rows = x.shape[0] // count
    cols = x.shape[1]
    return pl.pallas_call(
        functools.partial(scatter_sum_kernel, count, rows),
        out_shape=jax.ShapeDtypeStruct((rows, cols), jnp.float32),
        in_specs=[pl.BlockSpec(memory_space=pltpu.VMEM)],
        out_specs=pl.BlockSpec(memory_space=pltpu.VMEM),
        scratch_shapes=[
            pltpu.VMEM((count, rows, cols), x.dtype),
            pltpu.SemaphoreType.DMA((count,)),
            pltpu.SemaphoreType.DMA((count,)),
        ],
        compiler_params=pltpu.CompilerParams(collective_id=0, has_side_effects=True),
    )(x)


def carry_kernel(count, width, mine_ref, out_ref, recv, acc, send_sem, recv_sem):
    me = lax.axis_index(SEQ)
    barrier = pltpu.get_barrier_semaphore()
    for d in range(1, count):
        peer = lax.rem(me + d, count)
        pl.semaphore_signal(barrier, inc=1, device_id={SEQ: peer}, device_id_type=pl.DeviceIdType.MESH)
    pl.semaphore_wait(barrier, count - 1)

    def send_to(d):
        return pltpu.make_async_remote_copy(
            src_ref=mine_ref,
            dst_ref=recv.at[me],
            send_sem=send_sem.at[d],
            recv_sem=recv_sem.at[me],
            device_id={SEQ: me + d},
            device_id_type=pl.DeviceIdType.MESH,
        )

    for d in range(1, count):
        @pl.when(me + d < count)
        def _():
            send_to(d).start()

    acc[...] = jnp.zeros_like(acc)
    for j in range(count - 1):
        @pl.when(j < me)
        def _():
            pltpu.make_async_remote_copy(
                src_ref=mine_ref,
                dst_ref=recv.at[j],
                send_sem=send_sem.at[0],
                recv_sem=recv_sem.at[j],
                device_id={SEQ: j},
                device_id_type=pl.DeviceIdType.MESH,
            ).wait_recv()
            tail = recv[j, :, width : width + 16, :].astype(jnp.float32)
            gate = tail[:, 0:1, :] + tail[:, 1:2, :]
            acc[...] = gate * acc[...] + recv[j, :, :width, :].astype(jnp.float32)

    for d in range(1, count):
        @pl.when(me + d < count)
        def _():
            send_to(d).wait_send()
    out_ref[...] = acc[...]


def carry_in(mine, width):
    count = lax.axis_size(SEQ)
    heads, _, lanes = mine.shape
    return pl.pallas_call(
        functools.partial(carry_kernel, count, width),
        out_shape=jax.ShapeDtypeStruct((heads, width, lanes), jnp.float32),
        in_specs=[pl.BlockSpec(memory_space=pltpu.VMEM)],
        out_specs=pl.BlockSpec(memory_space=pltpu.VMEM),
        scratch_shapes=[
            pltpu.VMEM((count,) + mine.shape, mine.dtype),
            pltpu.VMEM((heads, width, lanes), jnp.float32),
            pltpu.SemaphoreType.DMA((count,)),
            pltpu.SemaphoreType.DMA((count,)),
        ],
        compiler_params=pltpu.CompilerParams(collective_id=1, has_side_effects=True),
    )(mine)


def round_up(n, m):
    return (n + m - 1) // m * m


def on_device(
    tokens,
    w_zx,
    w_dt,
    w_bc,
    conv_x_weight,
    conv_x_bias,
    conv_bc_weight,
    conv_bc_bias,
    dt_bias,
    a_log,
    skip,
    norm_weight,
    w_out,
    lengths,
    request_group,
):
    tp_count = lax.axis_size("tp")
    seq_count = lax.axis_size(SEQ)
    seq_index = lax.axis_index(SEQ)
    tok_dev = tokens.shape[0]
    d_model = tokens.shape[1]
    local_rows = w_zx.shape[0]
    inner_local = conv_x_weight.shape[1]
    heads_local = dt_bias.shape[0]
    head_width = inner_local // heads_local
    bc_width = conv_bc_weight.shape[1]
    state_width = bc_width // 2
    taps = conv_x_weight.shape[0]
    groups_dev = tok_dev // GROUP

    zx_part = w_zx.astype(jnp.bfloat16).reshape(local_rows, 2, tp_count, inner_local)
    zx_part = zx_part.transpose(0, 2, 1, 3).reshape(local_rows, tp_count, 2 * inner_local)
    bc_part = jnp.broadcast_to(
        w_bc.astype(jnp.bfloat16)[:, None, :], (local_rows, tp_count, bc_width)
    )
    dt_part = w_dt.astype(jnp.bfloat16).reshape(local_rows, tp_count, heads_local)
    used = 2 * inner_local + bc_width + heads_local
    width = round_up(used, 128)
    pad_part = jnp.zeros((local_rows, tp_count, width - used), jnp.bfloat16)
    packed = jnp.concatenate([zx_part, bc_part, dt_part, pad_part], axis=2)
    packed = packed.reshape(local_rows, tp_count * width)
    block = lax.all_to_all(packed, "tp", split_axis=1, concat_axis=0, tiled=True)
    block_rows = block.shape[0]
    out_rows, out_cols = w_out.shape
    out_piece = w_out.astype(jnp.bfloat16).T
    gathered = gather_seq(jnp.concatenate([block, out_piece], axis=1))
    gathered = gathered.reshape(seq_count * block_rows, width + out_rows)
    proj = jnp.dot(tokens, gathered[:, :width], preferred_element_type=jnp.float32)
    zx_low = proj[:, : 2 * inner_local].astype(jnp.bfloat16)
    gate_z = zx_low[:, :inner_local]
    x_raw = zx_low[:, inner_local:]
    bc_raw = proj[:, 2 * inner_local : 2 * inner_local + bc_width].astype(jnp.bfloat16)
    dt_pre = proj[:, 2 * inner_local + bc_width : used]

    raw_mix = jnp.concatenate([x_raw, bc_raw], axis=1)
    conv_weight = jnp.concatenate([conv_x_weight, conv_bc_weight], axis=1)
    conv_bias = jnp.concatenate([conv_x_bias, conv_bc_bias], axis=0)
    rim_rows = from_behind(raw_mix[tok_dev - (taps - 1) :], 1)
    padded = jnp.concatenate([rim_rows, raw_mix], axis=0)
    offset = seq_index * tok_dev
    seg_pad = segment_of(
        offset - (taps - 1) + jnp.arange(tok_dev + taps - 1, dtype=jnp.int32), lengths
    )
    seg_tok = seg_pad[taps - 1 :]
    conv_sum = jnp.zeros((tok_dev, raw_mix.shape[1]), jnp.float32) + conv_bias[None, :]
    for offset_tap in range(taps):
        rows_wide = padded[offset_tap : offset_tap + tok_dev].astype(jnp.float32)
        keep_tap = seg_pad[offset_tap : offset_tap + tok_dev] == seg_tok
        conv_sum = conv_sum + jnp.where(
            keep_tap[:, None], rows_wide * conv_weight[offset_tap][None, :], 0.0
        )
    convolved = jax.nn.silu(conv_sum).astype(jnp.bfloat16)
    inputs = convolved[:, :inner_local].reshape(groups_dev, GROUP, heads_local, head_width)
    b_matrix = convolved[:, inner_local : inner_local + state_width].reshape(
        groups_dev, GROUP, state_width
    )
    c_matrix = convolved[:, inner_local + state_width :].reshape(groups_dev, GROUP, state_width)
    step_size = jax.nn.softplus(dt_pre + dt_bias[None, :]).reshape(groups_dev, GROUP, heads_local)
    step_heads = step_size.transpose(0, 2, 1)
    decay_rate = -jnp.exp(a_log)
    cumul_heads = jnp.cumsum(step_size * decay_rate[None, None, :], axis=1).transpose(0, 2, 1)
    segments = seg_tok.reshape(groups_dev, GROUP)
    seg_before = segment_of(offset + jnp.arange(groups_dev, dtype=jnp.int32) * GROUP - 1, lengths)
    within = jnp.arange(GROUP, dtype=jnp.int32)
    same_prompt = (segments[:, :, None] == segments[:, None, :]) & (
        within[:, None] >= within[None, :]
    )[None]
    log_decay = cumul_heads[:, :, :, None] - cumul_heads[:, :, None, :]
    decay_matrix = jnp.where(
        same_prompt[:, None], jnp.exp(jnp.where(same_prompt[:, None], log_decay, 0.0)), 0.0
    )
    scores = jnp.einsum("cin,cjn->cij", c_matrix, b_matrix, preferred_element_type=jnp.float32)
    mix_weights = (decay_matrix * scores[:, None] * step_heads[:, :, None, :]).astype(jnp.bfloat16)
    diag_out = jnp.einsum(
        "chij,cjhp->cihp", mix_weights, inputs, preferred_element_type=jnp.float32
    )
    last_segment = segments[:, -1]
    tail_weight = (
        jnp.where(
            (segments == last_segment[:, None])[:, None, :],
            jnp.exp(cumul_heads[:, :, -1:] - cumul_heads),
            0.0,
        )
        * step_heads
    )
    b_weighted = (b_matrix.astype(jnp.float32)[:, None] * tail_weight[:, :, :, None]).astype(
        jnp.bfloat16
    )
    contrib = jnp.einsum("cjhp,chjn->chpn", inputs, b_weighted, preferred_element_type=jnp.float32)
    pass_gate = jnp.where(
        (last_segment == seg_before)[:, None], jnp.exp(cumul_heads[:, :, -1]), 0.0
    )

    ends = [contrib[0]]
    for c in range(1, groups_dev):
        ends.append(pass_gate[c][:, None, None] * ends[-1] + contrib[c])
    local_end = jnp.stack(ends)
    local_in = jnp.concatenate([jnp.zeros_like(local_end[:1]), local_end[:-1]], axis=0)
    through_group = jnp.cumprod(pass_gate, axis=0)
    before_group = jnp.concatenate(
        [jnp.ones((1, heads_local), jnp.float32), through_group[:-1]], axis=0
    )

    gate_hi = through_group.astype(jnp.bfloat16)
    gate_lo = (through_group - gate_hi.astype(jnp.float32)).astype(jnp.bfloat16)
    extra = jnp.zeros((groups_dev, heads_local, 16, state_width), jnp.bfloat16)
    extra = extra.at[:, :, 0, :].set(jnp.broadcast_to(gate_hi[:, :, None], gate_hi.shape + (state_width,)))
    extra = extra.at[:, :, 1, :].set(jnp.broadcast_to(gate_lo[:, :, None], gate_lo.shape + (state_width,)))
    sendable = jnp.concatenate([local_end.astype(jnp.bfloat16), extra], axis=2)
    carried = carry_in(sendable[-1], head_width)
    carried, later = lax.optimization_barrier((carried, sendable))
    every = gather_seq(later).reshape(
        (seq_count * groups_dev, heads_local, head_width + 16, state_width)
    )
    gate_rows = every[:, :, head_width : head_width + 2, :].astype(jnp.float32)
    every_gate = (gate_rows[:, :, 0, 0] + gate_rows[:, :, 1, 0]).reshape(
        seq_count, groups_dev, heads_local
    )
    dev_gate = every_gate[:, -1]
    rows_at = jnp.arange(seq_count, dtype=jnp.int32)
    dev_of = rows_at

    def carry_weights(k):
        between = (dev_of[:, None] < dev_of[None, :]) & (dev_of[None, :] < k)
        factors = jnp.where(between[:, :, None], dev_gate[None, :, :], 1.0)
        return jnp.where((dev_of < k)[:, None], jnp.prod(factors, axis=1), 0.0)

    req_dev = request_group.shape[0] // seq_count
    mine = lax.dynamic_slice_in_dim(request_group, seq_index * req_dev, req_dev)
    req_k = mine // groups_dev
    req_c = mine % groups_dev
    req_row = req_k
    req_gate = every_gate[req_row, req_c]
    wanted = req_k
    weights_all = jax.vmap(carry_weights)(wanted)
    weights_all = weights_all * req_gate[:, None, :]
    slot_ids = jnp.arange(groups_dev, dtype=jnp.int32)
    last_slot = (slot_ids == groups_dev - 1).astype(jnp.float32)
    coef = weights_all[:, :, None, :] * last_slot[None, None, :, None]
    own_row = req_row
    own_slot = req_c
    hit = (rows_at[None, :, None] == own_row[:, None, None]) & (
        slot_ids[None, None, :] == own_slot[:, None, None]
    )
    coef = coef + hit[:, :, :, None].astype(jnp.float32)
    coef = coef.reshape(wanted.shape[0], seq_count * groups_dev, heads_local)
    coef_hi = coef.astype(jnp.bfloat16)
    coef_lo = (coef - coef_hi.astype(jnp.float32)).astype(jnp.bfloat16)
    summed_states = jnp.einsum(
        "rjh,jhpn->rhpn", coef_hi, every, preferred_element_type=jnp.float32
    ) + jnp.einsum("rjh,jhpn->rhpn", coef_lo, every, preferred_element_type=jnp.float32)
    request_states = summed_states[:, :, :head_width]

    group_in = before_group[:, :, None, None] * carried[None] + local_in
    state_low = group_in.astype(jnp.bfloat16)
    carry_keep = jnp.where((segments == seg_before[:, None])[:, None, :], jnp.exp(cumul_heads), 0.0)
    carry_out = jnp.einsum(
        "cin,chpn->cihp", c_matrix, state_low, preferred_element_type=jnp.float32
    )
    carry_out = carry_out * carry_keep.transpose(0, 2, 1)[:, :, :, None]
    y_local = diag_out + carry_out + skip[None, None, :, None] * inputs.astype(jnp.float32)
    y_local = y_local.reshape(tok_dev, inner_local)
    gated = y_local * jax.nn.silu(gate_z.astype(jnp.float32))
    square_sum = jnp.sum(gated * gated, axis=1)
    scaled = (gated * norm_weight[None, :]).astype(jnp.bfloat16)
    partial = lax.dot_general(
        scaled, gathered[:, width:], (((1,), (1,)), ((), ())), preferred_element_type=jnp.float32
    )
    side = jnp.zeros((tok_dev, 128), jnp.float32).at[:, 0].set(square_sum)
    summed = scatter_sum(jnp.concatenate([partial, side], axis=1).astype(jnp.bfloat16), tp_count)
    mean_square = summed[:, d_model] / INNER
    mixed = (summed[:, :d_model] * lax.rsqrt(mean_square + epsilon)[:, None]).astype(jnp.bfloat16)
    return (mixed, request_states)


def solution(mesh):
    return jax.shard_map(
        on_device,
        mesh=mesh,
        in_specs=(
            P(SEQ, None),
            P((SEQ, "tp"), None),
            P((SEQ, "tp"), None),
            P((SEQ, "tp"), None),
            P(None, "tp"),
            P("tp"),
            P(),
            P(),
            P("tp"),
            P("tp"),
            P("tp"),
            P("tp"),
            P("tp", SEQ),
            P(),
            P(),
        ),
        out_specs=(P((SEQ, "tp"), None), P(SEQ, "tp", None, None)),
        check_vma=False,
    )
```

```python
import functools

import jax
import jax.numpy as jnp
from jax import lax
from jax.experimental import pallas as pl
from jax.experimental.pallas import tpu as pltpu
from jax.sharding import PartitionSpec as P

INNER = 4096
GROUP = 256
SEQ = "seq"


epsilon = 1e-05


def from_behind(x, by):
    count = lax.axis_size(SEQ)
    pairs = [(i, i + by) for i in range(count) if 0 <= i + by < count]
    return lax.ppermute(x, SEQ, pairs)


def gather_seq(x):
    return lax.all_gather(x, SEQ, axis=0, tiled=False)


def segment_of(position, lengths):
    prompt_ends = jnp.cumsum(lengths)
    return jnp.sum((position[:, None] >= prompt_ends[None, :]).astype(jnp.int32), axis=1)


def scatter_sum_kernel(count, rows, x_ref, o_ref, recv, send_sem, recv_sem):
    me = lax.axis_index("tp")
    barrier = pltpu.get_barrier_semaphore()
    for d in range(1, count):
        peer = lax.rem(me + d, count)
        pl.semaphore_signal(barrier, inc=1, device_id={"tp": peer}, device_id_type=pl.DeviceIdType.MESH)
    pl.semaphore_wait(barrier, count - 1)
    copies = []
    for d in range(1, count):
        peer = lax.rem(me + d, count)
        copy = pltpu.make_async_remote_copy(
            src_ref=x_ref.at[pl.ds(pl.multiple_of(peer * rows, rows), rows)],
            dst_ref=recv.at[me],
            send_sem=send_sem.at[d],
            recv_sem=recv_sem.at[me],
            device_id={"tp": peer},
            device_id_type=pl.DeviceIdType.MESH,
        )
        copy.start()
        copies.append(copy)
    total = x_ref[pl.ds(pl.multiple_of(me * rows, rows), rows), :].astype(jnp.float32)
    for d in range(1, count):
        sender = lax.rem(me + count - d, count)
        arrival = pltpu.make_async_remote_copy(
            src_ref=x_ref.at[pl.ds(0, rows)],
            dst_ref=recv.at[sender],
            send_sem=send_sem.at[d],
            recv_sem=recv_sem.at[sender],
            device_id={"tp": sender},
            device_id_type=pl.DeviceIdType.MESH,
        )
        arrival.wait_recv()
        total = total + recv[sender].astype(jnp.float32)
    for copy in copies:
        copy.wait_send()
    o_ref[...] = total


def scatter_sum(x, count):
    rows = x.shape[0] // count
    cols = x.shape[1]
    return pl.pallas_call(
        functools.partial(scatter_sum_kernel, count, rows),
        out_shape=jax.ShapeDtypeStruct((rows, cols), jnp.float32),
        in_specs=[pl.BlockSpec(memory_space=pltpu.VMEM)],
        out_specs=pl.BlockSpec(memory_space=pltpu.VMEM),
        scratch_shapes=[
            pltpu.VMEM((count, rows, cols), x.dtype),
            pltpu.SemaphoreType.DMA((count,)),
            pltpu.SemaphoreType.DMA((count,)),
        ],
        compiler_params=pltpu.CompilerParams(collective_id=0, has_side_effects=True),
    )(x)


def carry_kernel(count, width, mine_ref, out_ref, recv, acc, send_sem, recv_sem):
    me = lax.axis_index(SEQ)
    barrier = pltpu.get_barrier_semaphore()
    for d in range(1, count):
        peer = lax.rem(me + d, count)
        pl.semaphore_signal(barrier, inc=1, device_id={SEQ: peer}, device_id_type=pl.DeviceIdType.MESH)
    pl.semaphore_wait(barrier, count - 1)

    def send_to(d):
        return pltpu.make_async_remote_copy(
            src_ref=mine_ref,
            dst_ref=recv.at[me],
            send_sem=send_sem.at[d],
            recv_sem=recv_sem.at[me],
            device_id={SEQ: me + d},
            device_id_type=pl.DeviceIdType.MESH,
        )

    for d in range(1, count):
        @pl.when(me + d < count)
        def _():
            send_to(d).start()

    acc[...] = jnp.zeros_like(acc)
    for j in range(count - 1):
        @pl.when(j < me)
        def _():
            pltpu.make_async_remote_copy(
                src_ref=mine_ref,
                dst_ref=recv.at[j],
                send_sem=send_sem.at[0],
                recv_sem=recv_sem.at[j],
                device_id={SEQ: j},
                device_id_type=pl.DeviceIdType.MESH,
            ).wait_recv()
            tail = recv[j, :, width : width + 16, :].astype(jnp.float32)
            gate = tail[:, 0:1, :] + tail[:, 1:2, :]
            acc[...] = gate * acc[...] + recv[j, :, :width, :].astype(jnp.float32)

    for d in range(1, count):
        @pl.when(me + d < count)
        def _():
            send_to(d).wait_send()
    out_ref[...] = acc[...]


def carry_in(mine, width):
    count = lax.axis_size(SEQ)
    heads, _, lanes = mine.shape
    return pl.pallas_call(
        functools.partial(carry_kernel, count, width),
        out_shape=jax.ShapeDtypeStruct((heads, width, lanes), jnp.float32),
        in_specs=[pl.BlockSpec(memory_space=pltpu.VMEM)],
        out_specs=pl.BlockSpec(memory_space=pltpu.VMEM),
        scratch_shapes=[
            pltpu.VMEM((count,) + mine.shape, mine.dtype),
            pltpu.VMEM((heads, width, lanes), jnp.float32),
            pltpu.SemaphoreType.DMA((count,)),
            pltpu.SemaphoreType.DMA((count,)),
        ],
        compiler_params=pltpu.CompilerParams(collective_id=1, has_side_effects=True),
    )(mine)


def exchange_kernel(count, rows, width, x_ref, o_ref, recv, send_sem, recv_sem):
    me = lax.axis_index("tp")
    barrier = pltpu.get_barrier_semaphore()
    for d in range(1, count):
        peer = lax.rem(me + d, count)
        pl.semaphore_signal(barrier, inc=1, device_id={"tp": peer}, device_id_type=pl.DeviceIdType.MESH)
    pl.semaphore_wait(barrier, count - 1)
    copies = []
    for d in range(1, count):
        peer = lax.rem(me + d, count)
        copy = pltpu.make_async_remote_copy(
            src_ref=x_ref.at[:, pl.ds(pl.multiple_of(peer * width, 128), width)],
            dst_ref=recv.at[me],
            send_sem=send_sem.at[d],
            recv_sem=recv_sem.at[me],
            device_id={"tp": peer},
            device_id_type=pl.DeviceIdType.MESH,
        )
        copy.start()
        copies.append(copy)
    o_ref[pl.ds(pl.multiple_of(me * rows, rows), rows), :] = x_ref[
        :, pl.ds(pl.multiple_of(me * width, 128), width)
    ]
    for d in range(1, count):
        sender = lax.rem(me + count - d, count)
        pltpu.make_async_remote_copy(
            src_ref=x_ref.at[:, pl.ds(0, width)],
            dst_ref=recv.at[sender],
            send_sem=send_sem.at[0],
            recv_sem=recv_sem.at[sender],
            device_id={"tp": sender},
            device_id_type=pl.DeviceIdType.MESH,
        ).wait_recv()
        o_ref[pl.ds(pl.multiple_of(sender * rows, rows), rows), :] = recv[sender]
    for copy in copies:
        copy.wait_send()


def exchange(x, count):
    rows = x.shape[0]
    width = x.shape[1] // count
    return pl.pallas_call(
        functools.partial(exchange_kernel, count, rows, width),
        out_shape=jax.ShapeDtypeStruct((count * rows, width), x.dtype),
        in_specs=[pl.BlockSpec(memory_space=pltpu.VMEM)],
        out_specs=pl.BlockSpec(memory_space=pltpu.VMEM),
        scratch_shapes=[
            pltpu.VMEM((count, rows, width), x.dtype),
            pltpu.SemaphoreType.DMA((count,)),
            pltpu.SemaphoreType.DMA((count,)),
        ],
        compiler_params=pltpu.CompilerParams(collective_id=2, has_side_effects=True),
    )(x)


def round_up(n, m):
    return (n + m - 1) // m * m


def on_device(
    tokens,
    w_zx,
    w_dt,
    w_bc,
    conv_x_weight,
    conv_x_bias,
    conv_bc_weight,
    conv_bc_bias,
    dt_bias,
    a_log,
    skip,
    norm_weight,
    w_out,
    lengths,
    request_group,
):
    tp_count = lax.axis_size("tp")
    seq_count = lax.axis_size(SEQ)
    seq_index = lax.axis_index(SEQ)
    tok_dev = tokens.shape[0]
    d_model = tokens.shape[1]
    local_rows = w_zx.shape[0]
    inner_local = conv_x_weight.shape[1]
    heads_local = dt_bias.shape[0]
    head_width = inner_local // heads_local
    bc_width = conv_bc_weight.shape[1]
    state_width = bc_width // 2
    taps = conv_x_weight.shape[0]
    groups_dev = tok_dev // GROUP

    zx_part = w_zx.astype(jnp.bfloat16).reshape(local_rows, 2, tp_count, inner_local)
    zx_part = zx_part.transpose(0, 2, 1, 3).reshape(local_rows, tp_count, 2 * inner_local)
    bc_part = jnp.broadcast_to(
        w_bc.astype(jnp.bfloat16)[:, None, :], (local_rows, tp_count, bc_width)
    )
    dt_part = w_dt.astype(jnp.bfloat16).reshape(local_rows, tp_count, heads_local)
    used = 2 * inner_local + bc_width + heads_local
    width = round_up(used, 128)
    pad_part = jnp.zeros((local_rows, tp_count, width - used), jnp.bfloat16)
    packed = jnp.concatenate([zx_part, bc_part, dt_part, pad_part], axis=2)
    packed = packed.reshape(local_rows, tp_count * width)
    block = exchange(packed, tp_count)
    block_rows = block.shape[0]
    out_rows, out_cols = w_out.shape
    out_piece = w_out.astype(jnp.bfloat16).T
    gathered = gather_seq(jnp.concatenate([block, out_piece], axis=1))
    gathered = gathered.reshape(seq_count * block_rows, width + out_rows)
    proj = jnp.dot(tokens, gathered[:, :width], preferred_element_type=jnp.float32)
    zx_low = proj[:, : 2 * inner_local].astype(jnp.bfloat16)
    gate_z = zx_low[:, :inner_local]
    x_raw = zx_low[:, inner_local:]
    bc_raw = proj[:, 2 * inner_local : 2 * inner_local + bc_width].astype(jnp.bfloat16)
    dt_pre = proj[:, 2 * inner_local + bc_width : used]

    raw_mix = jnp.concatenate([x_raw, bc_raw], axis=1)
    conv_weight = jnp.concatenate([conv_x_weight, conv_bc_weight], axis=1)
    conv_bias = jnp.concatenate([conv_x_bias, conv_bc_bias], axis=0)
    rim_rows = from_behind(raw_mix[tok_dev - (taps - 1) :], 1)
    padded = jnp.concatenate([rim_rows, raw_mix], axis=0)
    offset = seq_index * tok_dev
    seg_pad = segment_of(
        offset - (taps - 1) + jnp.arange(tok_dev + taps - 1, dtype=jnp.int32), lengths
    )
    seg_tok = seg_pad[taps - 1 :]
    conv_sum = jnp.zeros((tok_dev, raw_mix.shape[1]), jnp.float32) + conv_bias[None, :]
    for offset_tap in range(taps):
        rows_wide = padded[offset_tap : offset_tap + tok_dev].astype(jnp.float32)
        keep_tap = seg_pad[offset_tap : offset_tap + tok_dev] == seg_tok
        conv_sum = conv_sum + jnp.where(
            keep_tap[:, None], rows_wide * conv_weight[offset_tap][None, :], 0.0
        )
    convolved = jax.nn.silu(conv_sum).astype(jnp.bfloat16)
    inputs = convolved[:, :inner_local].reshape(groups_dev, GROUP, heads_local, head_width)
    b_matrix = convolved[:, inner_local : inner_local + state_width].reshape(
        groups_dev, GROUP, state_width
    )
    c_matrix = convolved[:, inner_local + state_width :].reshape(groups_dev, GROUP, state_width)
    step_size = jax.nn.softplus(dt_pre + dt_bias[None, :]).reshape(groups_dev, GROUP, heads_local)
    step_heads = step_size.transpose(0, 2, 1)
    decay_rate = -jnp.exp(a_log)
    cumul_heads = jnp.cumsum(step_size * decay_rate[None, None, :], axis=1).transpose(0, 2, 1)
    segments = seg_tok.reshape(groups_dev, GROUP)
    seg_before = segment_of(offset + jnp.arange(groups_dev, dtype=jnp.int32) * GROUP - 1, lengths)
    within = jnp.arange(GROUP, dtype=jnp.int32)
    same_prompt = (segments[:, :, None] == segments[:, None, :]) & (
        within[:, None] >= within[None, :]
    )[None]
    log_decay = cumul_heads[:, :, :, None] - cumul_heads[:, :, None, :]
    decay_matrix = jnp.where(
        same_prompt[:, None], jnp.exp(jnp.where(same_prompt[:, None], log_decay, 0.0)), 0.0
    )
    scores = jnp.einsum("cin,cjn->cij", c_matrix, b_matrix, preferred_element_type=jnp.float32)
    mix_weights = (decay_matrix * scores[:, None] * step_heads[:, :, None, :]).astype(jnp.bfloat16)
    diag_out = jnp.einsum(
        "chij,cjhp->cihp", mix_weights, inputs, preferred_element_type=jnp.float32
    )
    last_segment = segments[:, -1]
    tail_weight = (
        jnp.where(
            (segments == last_segment[:, None])[:, None, :],
            jnp.exp(cumul_heads[:, :, -1:] - cumul_heads),
            0.0,
        )
        * step_heads
    )
    b_weighted = (b_matrix.astype(jnp.float32)[:, None] * tail_weight[:, :, :, None]).astype(
        jnp.bfloat16
    )
    contrib = jnp.einsum("cjhp,chjn->chpn", inputs, b_weighted, preferred_element_type=jnp.float32)
    pass_gate = jnp.where(
        (last_segment == seg_before)[:, None], jnp.exp(cumul_heads[:, :, -1]), 0.0
    )

    ends = [contrib[0]]
    for c in range(1, groups_dev):
        ends.append(pass_gate[c][:, None, None] * ends[-1] + contrib[c])
    local_end = jnp.stack(ends)
    local_in = jnp.concatenate([jnp.zeros_like(local_end[:1]), local_end[:-1]], axis=0)
    through_group = jnp.cumprod(pass_gate, axis=0)
    before_group = jnp.concatenate(
        [jnp.ones((1, heads_local), jnp.float32), through_group[:-1]], axis=0
    )

    gate_hi = through_group.astype(jnp.bfloat16)
    gate_lo = (through_group - gate_hi.astype(jnp.float32)).astype(jnp.bfloat16)
    extra = jnp.zeros((groups_dev, heads_local, 16, state_width), jnp.bfloat16)
    extra = extra.at[:, :, 0, :].set(jnp.broadcast_to(gate_hi[:, :, None], gate_hi.shape + (state_width,)))
    extra = extra.at[:, :, 1, :].set(jnp.broadcast_to(gate_lo[:, :, None], gate_lo.shape + (state_width,)))
    sendable = jnp.concatenate([local_end.astype(jnp.bfloat16), extra], axis=2)
    carried = carry_in(sendable[-1], head_width)
    carried, later = lax.optimization_barrier((carried, sendable))
    every = gather_seq(later).reshape(
        (seq_count * groups_dev, heads_local, head_width + 16, state_width)
    )
    gate_rows = every[:, :, head_width : head_width + 2, :].astype(jnp.float32)
    every_gate = (gate_rows[:, :, 0, 0] + gate_rows[:, :, 1, 0]).reshape(
        seq_count, groups_dev, heads_local
    )
    dev_gate = every_gate[:, -1]
    rows_at = jnp.arange(seq_count, dtype=jnp.int32)
    dev_of = rows_at

    def carry_weights(k):
        between = (dev_of[:, None] < dev_of[None, :]) & (dev_of[None, :] < k)
        factors = jnp.where(between[:, :, None], dev_gate[None, :, :], 1.0)
        return jnp.where((dev_of < k)[:, None], jnp.prod(factors, axis=1), 0.0)

    req_dev = request_group.shape[0] // seq_count
    mine = lax.dynamic_slice_in_dim(request_group, seq_index * req_dev, req_dev)
    req_k = mine // groups_dev
    req_c = mine % groups_dev
    req_row = req_k
    req_gate = every_gate[req_row, req_c]
    wanted = req_k
    weights_all = jax.vmap(carry_weights)(wanted)
    weights_all = weights_all * req_gate[:, None, :]
    slot_ids = jnp.arange(groups_dev, dtype=jnp.int32)
    last_slot = (slot_ids == groups_dev - 1).astype(jnp.float32)
    coef = weights_all[:, :, None, :] * last_slot[None, None, :, None]
    own_row = req_row
    own_slot = req_c
    hit = (rows_at[None, :, None] == own_row[:, None, None]) & (
        slot_ids[None, None, :] == own_slot[:, None, None]
    )
    coef = coef + hit[:, :, :, None].astype(jnp.float32)
    coef = coef.reshape(wanted.shape[0], seq_count * groups_dev, heads_local)
    coef_hi = coef.astype(jnp.bfloat16)
    coef_lo = (coef - coef_hi.astype(jnp.float32)).astype(jnp.bfloat16)
    summed_states = jnp.einsum(
        "rjh,jhpn->rhpn", coef_hi, every, preferred_element_type=jnp.float32
    ) + jnp.einsum("rjh,jhpn->rhpn", coef_lo, every, preferred_element_type=jnp.float32)
    request_states = summed_states[:, :, :head_width]

    group_in = before_group[:, :, None, None] * carried[None] + local_in
    state_low = group_in.astype(jnp.bfloat16)
    carry_keep = jnp.where((segments == seg_before[:, None])[:, None, :], jnp.exp(cumul_heads), 0.0)
    carry_out = jnp.einsum(
        "cin,chpn->cihp", c_matrix, state_low, preferred_element_type=jnp.float32
    )
    carry_out = carry_out * carry_keep.transpose(0, 2, 1)[:, :, :, None]
    y_local = diag_out + carry_out + skip[None, None, :, None] * inputs.astype(jnp.float32)
    y_local = y_local.reshape(tok_dev, inner_local)
    gated = y_local * jax.nn.silu(gate_z.astype(jnp.float32))
    square_sum = jnp.sum(gated * gated, axis=1)
    scaled = (gated * norm_weight[None, :]).astype(jnp.bfloat16)
    partial = lax.dot_general(
        scaled, gathered[:, width:], (((1,), (1,)), ((), ())), preferred_element_type=jnp.float32
    )
    side = jnp.zeros((tok_dev, 128), jnp.float32).at[:, 0].set(square_sum)
    summed = scatter_sum(jnp.concatenate([partial, side], axis=1).astype(jnp.bfloat16), tp_count)
    mean_square = summed[:, d_model] / INNER
    mixed = (summed[:, :d_model] * lax.rsqrt(mean_square + epsilon)[:, None]).astype(jnp.bfloat16)
    return (mixed, request_states)


def solution(mesh):
    return jax.shard_map(
        on_device,
        mesh=mesh,
        in_specs=(
            P(SEQ, None),
            P((SEQ, "tp"), None),
            P((SEQ, "tp"), None),
            P((SEQ, "tp"), None),
            P(None, "tp"),
            P("tp"),
            P(),
            P(),
            P("tp"),
            P("tp"),
            P("tp"),
            P("tp"),
            P("tp", SEQ),
            P(),
            P(),
        ),
        out_specs=(P((SEQ, "tp"), None), P(SEQ, "tp", None, None)),
        check_vma=False,
    )
```

```python
import functools

import jax
import jax.numpy as jnp
from jax import lax
from jax.experimental import pallas as pl
from jax.experimental.pallas import tpu as pltpu
from jax.sharding import PartitionSpec as P

INNER = 4096
GROUP = 256
SEQ = "seq"


epsilon = 1e-05


def from_behind(x, by):
    count = lax.axis_size(SEQ)
    pairs = [(i, i + by) for i in range(count) if 0 <= i + by < count]
    return lax.ppermute(x, SEQ, pairs)


def gather_seq(x):
    return lax.all_gather(x, SEQ, axis=0, tiled=False)


def segment_of(position, lengths):
    prompt_ends = jnp.cumsum(lengths)
    return jnp.sum((position[:, None] >= prompt_ends[None, :]).astype(jnp.int32), axis=1)


def scatter_sum_kernel(count, rows, x_ref, o_ref, recv, send_sem, recv_sem):
    me = lax.axis_index("tp")
    barrier = pltpu.get_barrier_semaphore()
    for d in range(1, count):
        peer = lax.rem(me + d, count)
        pl.semaphore_signal(barrier, inc=1, device_id={"tp": peer}, device_id_type=pl.DeviceIdType.MESH)
    pl.semaphore_wait(barrier, count - 1)
    copies = []
    for d in range(1, count):
        peer = lax.rem(me + d, count)
        copy = pltpu.make_async_remote_copy(
            src_ref=x_ref.at[pl.ds(pl.multiple_of(peer * rows, rows), rows)],
            dst_ref=recv.at[me],
            send_sem=send_sem.at[d],
            recv_sem=recv_sem.at[me],
            device_id={"tp": peer},
            device_id_type=pl.DeviceIdType.MESH,
        )
        copy.start()
        copies.append(copy)
    total = x_ref[pl.ds(pl.multiple_of(me * rows, rows), rows), :].astype(jnp.float32)
    for d in range(1, count):
        sender = lax.rem(me + count - d, count)
        arrival = pltpu.make_async_remote_copy(
            src_ref=x_ref.at[pl.ds(0, rows)],
            dst_ref=recv.at[sender],
            send_sem=send_sem.at[d],
            recv_sem=recv_sem.at[sender],
            device_id={"tp": sender},
            device_id_type=pl.DeviceIdType.MESH,
        )
        arrival.wait_recv()
        total = total + recv[sender].astype(jnp.float32)
    for copy in copies:
        copy.wait_send()
    o_ref[...] = total


def scatter_sum(x, count):
    rows = x.shape[0] // count
    cols = x.shape[1]
    return pl.pallas_call(
        functools.partial(scatter_sum_kernel, count, rows),
        out_shape=jax.ShapeDtypeStruct((rows, cols), jnp.float32),
        in_specs=[pl.BlockSpec(memory_space=pltpu.VMEM)],
        out_specs=pl.BlockSpec(memory_space=pltpu.VMEM),
        scratch_shapes=[
            pltpu.VMEM((count, rows, cols), x.dtype),
            pltpu.SemaphoreType.DMA((count,)),
            pltpu.SemaphoreType.DMA((count,)),
        ],
        compiler_params=pltpu.CompilerParams(collective_id=0, has_side_effects=True),
    )(x)


def scan_kernel(count, width, mine_ref, out_ref, acc, send_buf, recv, send_sem, recv_sem):
    me = lax.axis_index(SEQ)
    barrier = pltpu.get_barrier_semaphore()
    for d in range(1, count):
        peer = lax.rem(me + d, count)
        pl.semaphore_signal(barrier, inc=1, device_id={SEQ: peer}, device_id_type=pl.DeviceIdType.MESH)
    pl.semaphore_wait(barrier, count - 1)
    distances = [1]
    while distances[-1] * 2 < count:
        distances.append(distances[-1] * 2)
    rounds = [1] + distances

    def link(r, dist, target):
        return pltpu.make_async_remote_copy(
            src_ref=mine_ref if r == 0 else send_buf.at[r],
            dst_ref=recv.at[r],
            send_sem=send_sem.at[r],
            recv_sem=recv_sem.at[r],
            device_id={SEQ: target},
            device_id_type=pl.DeviceIdType.MESH,
        )

    rows = acc.shape[1]
    is_gate_row = lax.broadcasted_iota(jnp.int32, acc.shape, 1) == width
    acc[...] = jnp.where(is_gate_row, 1.0, 0.0).astype(acc.dtype)
    for r, dist in enumerate(rounds):
        if r > 0:
            send_buf[r] = acc[...]

        @pl.when(me + dist < count)
        def _():
            link(r, dist, me + dist).start()

        @pl.when(me >= dist)
        def _():
            link(r, dist, me - dist).wait_recv()
            if r == 0:
                acc[...] = recv[0]
            else:
                came = recv[r]
                mine_gate = acc[:, width : width + 8, :][:, 0:1, :]
                came_gate = came[:, width : width + 8, :][:, 0:1, :]
                state = mine_gate * came + acc[...]
                acc[...] = jnp.where(is_gate_row, mine_gate * came_gate, state)

    for r, dist in enumerate(rounds):
        @pl.when(me + dist < count)
        def _():
            link(r, dist, me + dist).wait_send()
    out_ref[...] = acc[:, :width, :]


def carry_in(mine, width):
    count = lax.axis_size(SEQ)
    heads, rows, lanes = mine.shape
    steps = 1
    while (1 << (steps - 1)) < count:
        steps += 1
    return pl.pallas_call(
        functools.partial(scan_kernel, count, width),
        out_shape=jax.ShapeDtypeStruct((heads, width, lanes), jnp.float32),
        in_specs=[pl.BlockSpec(memory_space=pltpu.VMEM)],
        out_specs=pl.BlockSpec(memory_space=pltpu.VMEM),
        scratch_shapes=[
            pltpu.VMEM(mine.shape, jnp.float32),
            pltpu.VMEM((steps,) + mine.shape, jnp.float32),
            pltpu.VMEM((steps,) + mine.shape, jnp.float32),
            pltpu.SemaphoreType.DMA((steps,)),
            pltpu.SemaphoreType.DMA((steps,)),
        ],
        compiler_params=pltpu.CompilerParams(collective_id=1, has_side_effects=True),
    )(mine)


def round_up(n, m):
    return (n + m - 1) // m * m


def on_device(
    tokens,
    w_zx,
    w_dt,
    w_bc,
    conv_x_weight,
    conv_x_bias,
    conv_bc_weight,
    conv_bc_bias,
    dt_bias,
    a_log,
    skip,
    norm_weight,
    w_out,
    lengths,
    request_group,
):
    tp_count = lax.axis_size("tp")
    seq_count = lax.axis_size(SEQ)
    seq_index = lax.axis_index(SEQ)
    tok_dev = tokens.shape[0]
    d_model = tokens.shape[1]
    local_rows = w_zx.shape[0]
    inner_local = conv_x_weight.shape[1]
    heads_local = dt_bias.shape[0]
    head_width = inner_local // heads_local
    bc_width = conv_bc_weight.shape[1]
    state_width = bc_width // 2
    taps = conv_x_weight.shape[0]
    groups_dev = tok_dev // GROUP

    zx_part = w_zx.astype(jnp.bfloat16).reshape(local_rows, 2, tp_count, inner_local)
    zx_part = zx_part.transpose(0, 2, 1, 3).reshape(local_rows, tp_count, 2 * inner_local)
    bc_part = jnp.broadcast_to(
        w_bc.astype(jnp.bfloat16)[:, None, :], (local_rows, tp_count, bc_width)
    )
    dt_part = w_dt.astype(jnp.bfloat16).reshape(local_rows, tp_count, heads_local)
    used = 2 * inner_local + bc_width + heads_local
    width = round_up(used, 128)
    pad_part = jnp.zeros((local_rows, tp_count, width - used), jnp.bfloat16)
    packed = jnp.concatenate([zx_part, bc_part, dt_part, pad_part], axis=2)
    packed = packed.reshape(local_rows, tp_count * width)
    block = lax.all_to_all(packed, "tp", split_axis=1, concat_axis=0, tiled=True)
    block_rows = block.shape[0]
    out_rows, out_cols = w_out.shape
    out_piece = w_out.astype(jnp.bfloat16).T
    gathered = gather_seq(jnp.concatenate([block, out_piece], axis=1))
    gathered = gathered.reshape(seq_count * block_rows, width + out_rows)
    proj = jnp.dot(tokens, gathered[:, :width], preferred_element_type=jnp.float32)
    zx_low = proj[:, : 2 * inner_local].astype(jnp.bfloat16)
    gate_z = zx_low[:, :inner_local]
    x_raw = zx_low[:, inner_local:]
    bc_raw = proj[:, 2 * inner_local : 2 * inner_local + bc_width].astype(jnp.bfloat16)
    dt_pre = proj[:, 2 * inner_local + bc_width : used]

    raw_mix = jnp.concatenate([x_raw, bc_raw], axis=1)
    conv_weight = jnp.concatenate([conv_x_weight, conv_bc_weight], axis=1)
    conv_bias = jnp.concatenate([conv_x_bias, conv_bc_bias], axis=0)
    rim_rows = from_behind(raw_mix[tok_dev - (taps - 1) :], 1)
    padded = jnp.concatenate([rim_rows, raw_mix], axis=0)
    offset = seq_index * tok_dev
    seg_pad = segment_of(
        offset - (taps - 1) + jnp.arange(tok_dev + taps - 1, dtype=jnp.int32), lengths
    )
    seg_tok = seg_pad[taps - 1 :]
    conv_sum = jnp.zeros((tok_dev, raw_mix.shape[1]), jnp.float32) + conv_bias[None, :]
    for offset_tap in range(taps):
        rows_wide = padded[offset_tap : offset_tap + tok_dev].astype(jnp.float32)
        keep_tap = seg_pad[offset_tap : offset_tap + tok_dev] == seg_tok
        conv_sum = conv_sum + jnp.where(
            keep_tap[:, None], rows_wide * conv_weight[offset_tap][None, :], 0.0
        )
    convolved = jax.nn.silu(conv_sum).astype(jnp.bfloat16)
    inputs = convolved[:, :inner_local].reshape(groups_dev, GROUP, heads_local, head_width)
    b_matrix = convolved[:, inner_local : inner_local + state_width].reshape(
        groups_dev, GROUP, state_width
    )
    c_matrix = convolved[:, inner_local + state_width :].reshape(groups_dev, GROUP, state_width)
    step_size = jax.nn.softplus(dt_pre + dt_bias[None, :]).reshape(groups_dev, GROUP, heads_local)
    step_heads = step_size.transpose(0, 2, 1)
    decay_rate = -jnp.exp(a_log)
    cumul_heads = jnp.cumsum(step_size * decay_rate[None, None, :], axis=1).transpose(0, 2, 1)
    segments = seg_tok.reshape(groups_dev, GROUP)
    seg_before = segment_of(offset + jnp.arange(groups_dev, dtype=jnp.int32) * GROUP - 1, lengths)
    within = jnp.arange(GROUP, dtype=jnp.int32)
    same_prompt = (segments[:, :, None] == segments[:, None, :]) & (
        within[:, None] >= within[None, :]
    )[None]
    log_decay = cumul_heads[:, :, :, None] - cumul_heads[:, :, None, :]
    decay_matrix = jnp.where(
        same_prompt[:, None], jnp.exp(jnp.where(same_prompt[:, None], log_decay, 0.0)), 0.0
    )
    scores = jnp.einsum("cin,cjn->cij", c_matrix, b_matrix, preferred_element_type=jnp.float32)
    mix_weights = (decay_matrix * scores[:, None] * step_heads[:, :, None, :]).astype(jnp.bfloat16)
    diag_out = jnp.einsum(
        "chij,cjhp->cihp", mix_weights, inputs, preferred_element_type=jnp.float32
    )
    last_segment = segments[:, -1]
    tail_weight = (
        jnp.where(
            (segments == last_segment[:, None])[:, None, :],
            jnp.exp(cumul_heads[:, :, -1:] - cumul_heads),
            0.0,
        )
        * step_heads
    )
    b_weighted = (b_matrix.astype(jnp.float32)[:, None] * tail_weight[:, :, :, None]).astype(
        jnp.bfloat16
    )
    contrib = jnp.einsum("cjhp,chjn->chpn", inputs, b_weighted, preferred_element_type=jnp.float32)
    pass_gate = jnp.where(
        (last_segment == seg_before)[:, None], jnp.exp(cumul_heads[:, :, -1]), 0.0
    )

    ends = [contrib[0]]
    for c in range(1, groups_dev):
        ends.append(pass_gate[c][:, None, None] * ends[-1] + contrib[c])
    local_end = jnp.stack(ends)
    local_in = jnp.concatenate([jnp.zeros_like(local_end[:1]), local_end[:-1]], axis=0)
    through_group = jnp.cumprod(pass_gate, axis=0)
    before_group = jnp.concatenate(
        [jnp.ones((1, heads_local), jnp.float32), through_group[:-1]], axis=0
    )

    gate_hi = through_group.astype(jnp.bfloat16)
    gate_lo = (through_group - gate_hi.astype(jnp.float32)).astype(jnp.bfloat16)
    extra = jnp.zeros((groups_dev, heads_local, 16, state_width), jnp.bfloat16)
    extra = extra.at[:, :, 0, :].set(jnp.broadcast_to(gate_hi[:, :, None], gate_hi.shape + (state_width,)))
    extra = extra.at[:, :, 1, :].set(jnp.broadcast_to(gate_lo[:, :, None], gate_lo.shape + (state_width,)))
    sendable = jnp.concatenate([local_end.astype(jnp.bfloat16), extra], axis=2)
    dev_row = jnp.zeros((heads_local, 8, state_width), jnp.float32)
    dev_row = dev_row.at[:, 0, :].set(
        jnp.broadcast_to(through_group[-1][:, None], (heads_local, state_width))
    )
    carried = carry_in(jnp.concatenate([local_end[-1], dev_row], axis=1), head_width)
    carried, later = lax.optimization_barrier((carried, sendable))
    every = gather_seq(later).reshape(
        (seq_count * groups_dev, heads_local, head_width + 16, state_width)
    )
    gate_rows = every[:, :, head_width : head_width + 2, :].astype(jnp.float32)
    every_gate = (gate_rows[:, :, 0, 0] + gate_rows[:, :, 1, 0]).reshape(
        seq_count, groups_dev, heads_local
    )
    dev_gate = every_gate[:, -1]
    rows_at = jnp.arange(seq_count, dtype=jnp.int32)
    dev_of = rows_at

    def carry_weights(k):
        between = (dev_of[:, None] < dev_of[None, :]) & (dev_of[None, :] < k)
        factors = jnp.where(between[:, :, None], dev_gate[None, :, :], 1.0)
        return jnp.where((dev_of < k)[:, None], jnp.prod(factors, axis=1), 0.0)

    req_dev = request_group.shape[0] // seq_count
    mine = lax.dynamic_slice_in_dim(request_group, seq_index * req_dev, req_dev)
    req_k = mine // groups_dev
    req_c = mine % groups_dev
    req_row = req_k
    req_gate = every_gate[req_row, req_c]
    wanted = req_k
    weights_all = jax.vmap(carry_weights)(wanted)
    weights_all = weights_all * req_gate[:, None, :]
    slot_ids = jnp.arange(groups_dev, dtype=jnp.int32)
    last_slot = (slot_ids == groups_dev - 1).astype(jnp.float32)
    coef = weights_all[:, :, None, :] * last_slot[None, None, :, None]
    own_row = req_row
    own_slot = req_c
    hit = (rows_at[None, :, None] == own_row[:, None, None]) & (
        slot_ids[None, None, :] == own_slot[:, None, None]
    )
    coef = coef + hit[:, :, :, None].astype(jnp.float32)
    coef = coef.reshape(wanted.shape[0], seq_count * groups_dev, heads_local)
    coef_hi = coef.astype(jnp.bfloat16)
    coef_lo = (coef - coef_hi.astype(jnp.float32)).astype(jnp.bfloat16)
    summed_states = jnp.einsum(
        "rjh,jhpn->rhpn", coef_hi, every, preferred_element_type=jnp.float32
    ) + jnp.einsum("rjh,jhpn->rhpn", coef_lo, every, preferred_element_type=jnp.float32)
    request_states = summed_states[:, :, :head_width]

    group_in = before_group[:, :, None, None] * carried[None] + local_in
    state_low = group_in.astype(jnp.bfloat16)
    carry_keep = jnp.where((segments == seg_before[:, None])[:, None, :], jnp.exp(cumul_heads), 0.0)
    carry_out = jnp.einsum(
        "cin,chpn->cihp", c_matrix, state_low, preferred_element_type=jnp.float32
    )
    carry_out = carry_out * carry_keep.transpose(0, 2, 1)[:, :, :, None]
    y_local = diag_out + carry_out + skip[None, None, :, None] * inputs.astype(jnp.float32)
    y_local = y_local.reshape(tok_dev, inner_local)
    gated = y_local * jax.nn.silu(gate_z.astype(jnp.float32))
    square_sum = jnp.sum(gated * gated, axis=1)
    scaled = (gated * norm_weight[None, :]).astype(jnp.bfloat16)
    partial = lax.dot_general(
        scaled, gathered[:, width:], (((1,), (1,)), ((), ())), preferred_element_type=jnp.float32
    )
    side = jnp.zeros((tok_dev, 128), jnp.float32).at[:, 0].set(square_sum)
    summed = scatter_sum(jnp.concatenate([partial, side], axis=1).astype(jnp.bfloat16), tp_count)
    mean_square = summed[:, d_model] / INNER
    mixed = (summed[:, :d_model] * lax.rsqrt(mean_square + epsilon)[:, None]).astype(jnp.bfloat16)
    return (mixed, request_states)


def solution(mesh):
    return jax.shard_map(
        on_device,
        mesh=mesh,
        in_specs=(
            P(SEQ, None),
            P((SEQ, "tp"), None),
            P((SEQ, "tp"), None),
            P((SEQ, "tp"), None),
            P(None, "tp"),
            P("tp"),
            P(),
            P(),
            P("tp"),
            P("tp"),
            P("tp"),
            P("tp"),
            P("tp", SEQ),
            P(),
            P(),
        ),
        out_specs=(P((SEQ, "tp"), None), P(SEQ, "tp", None, None)),
        check_vma=False,
    )
```

```python
import functools

import jax
import jax.numpy as jnp
from jax import lax
from jax.experimental import pallas as pl
from jax.experimental.pallas import tpu as pltpu
from jax.sharding import PartitionSpec as P

INNER = 4096
GROUP = 256
SEQ = "seq"


epsilon = 1e-05


def from_behind(x, by):
    count = lax.axis_size(SEQ)
    pairs = [(i, i + by) for i in range(count) if 0 <= i + by < count]
    return lax.ppermute(x, SEQ, pairs)


def gather_seq(x):
    return lax.all_gather(x, SEQ, axis=0, tiled=False)


def segment_of(position, lengths):
    prompt_ends = jnp.cumsum(lengths)
    return jnp.sum((position[:, None] >= prompt_ends[None, :]).astype(jnp.int32), axis=1)


def scatter_sum_kernel(count, rows, x_ref, o_ref, recv, send_sem, recv_sem):
    me = lax.axis_index("tp")
    barrier = pltpu.get_barrier_semaphore()
    for d in range(1, count):
        peer = lax.rem(me + d, count)
        pl.semaphore_signal(barrier, inc=1, device_id={"tp": peer}, device_id_type=pl.DeviceIdType.MESH)
    pl.semaphore_wait(barrier, count - 1)
    copies = []
    for d in range(1, count):
        peer = lax.rem(me + d, count)
        copy = pltpu.make_async_remote_copy(
            src_ref=x_ref.at[pl.ds(pl.multiple_of(peer * rows, rows), rows)],
            dst_ref=recv.at[me],
            send_sem=send_sem.at[d],
            recv_sem=recv_sem.at[me],
            device_id={"tp": peer},
            device_id_type=pl.DeviceIdType.MESH,
        )
        copy.start()
        copies.append(copy)
    total = x_ref[pl.ds(pl.multiple_of(me * rows, rows), rows), :].astype(jnp.float32)
    for d in range(1, count):
        sender = lax.rem(me + count - d, count)
        arrival = pltpu.make_async_remote_copy(
            src_ref=x_ref.at[pl.ds(0, rows)],
            dst_ref=recv.at[sender],
            send_sem=send_sem.at[d],
            recv_sem=recv_sem.at[sender],
            device_id={"tp": sender},
            device_id_type=pl.DeviceIdType.MESH,
        )
        arrival.wait_recv()
        total = total + recv[sender].astype(jnp.float32)
    for copy in copies:
        copy.wait_send()
    o_ref[...] = total


def scatter_sum(x, count):
    rows = x.shape[0] // count
    cols = x.shape[1]
    return pl.pallas_call(
        functools.partial(scatter_sum_kernel, count, rows),
        out_shape=jax.ShapeDtypeStruct((rows, cols), jnp.float32),
        in_specs=[pl.BlockSpec(memory_space=pltpu.VMEM)],
        out_specs=pl.BlockSpec(memory_space=pltpu.VMEM),
        scratch_shapes=[
            pltpu.VMEM((count, rows, cols), x.dtype),
            pltpu.SemaphoreType.DMA((count,)),
            pltpu.SemaphoreType.DMA((count,)),
        ],
        compiler_params=pltpu.CompilerParams(collective_id=0, has_side_effects=True),
    )(x)


def scan_kernel(count, width, mine_ref, out_ref, acc, send_buf, recv, send_sem, recv_sem):
    me = lax.axis_index(SEQ)
    barrier = pltpu.get_barrier_semaphore()
    for d in range(1, count):
        peer = lax.rem(me + d, count)
        pl.semaphore_signal(barrier, inc=1, device_id={SEQ: peer}, device_id_type=pl.DeviceIdType.MESH)
    pl.semaphore_wait(barrier, count - 1)
    distances = [1]
    while distances[-1] * 2 < count:
        distances.append(distances[-1] * 2)
    rounds = [1] + distances

    def link(r, dist, target):
        return pltpu.make_async_remote_copy(
            src_ref=mine_ref if r == 0 else send_buf.at[r],
            dst_ref=recv.at[r],
            send_sem=send_sem.at[r],
            recv_sem=recv_sem.at[r],
            device_id={SEQ: target},
            device_id_type=pl.DeviceIdType.MESH,
        )

    rows = acc.shape[1]
    is_gate_row = lax.broadcasted_iota(jnp.int32, acc.shape, 1) == width
    acc[...] = jnp.where(is_gate_row, 1.0, 0.0).astype(acc.dtype)
    for r, dist in enumerate(rounds):
        if r > 0:
            send_buf[r] = acc[...]

        @pl.when(me + dist < count)
        def _():
            link(r, dist, me + dist).start()

        @pl.when(me >= dist)
        def _():
            link(r, dist, me - dist).wait_recv()
            if r == 0:
                acc[...] = recv[0]
            else:
                came = recv[r]
                mine_gate = acc[:, width : width + 8, :][:, 0:1, :]
                came_gate = came[:, width : width + 8, :][:, 0:1, :]
                state = mine_gate * came + acc[...]
                acc[...] = jnp.where(is_gate_row, mine_gate * came_gate, state)

    for r, dist in enumerate(rounds):
        @pl.when(me + dist < count)
        def _():
            link(r, dist, me + dist).wait_send()
    out_ref[...] = acc[:, :width, :]


def carry_in(mine, width):
    count = lax.axis_size(SEQ)
    heads, rows, lanes = mine.shape
    steps = 1
    while (1 << (steps - 1)) < count:
        steps += 1
    return pl.pallas_call(
        functools.partial(scan_kernel, count, width),
        out_shape=jax.ShapeDtypeStruct((heads, width, lanes), jnp.float32),
        in_specs=[pl.BlockSpec(memory_space=pltpu.VMEM)],
        out_specs=pl.BlockSpec(memory_space=pltpu.VMEM),
        scratch_shapes=[
            pltpu.VMEM(mine.shape, jnp.float32),
            pltpu.VMEM((steps,) + mine.shape, jnp.float32),
            pltpu.VMEM((steps,) + mine.shape, jnp.float32),
            pltpu.SemaphoreType.DMA((steps,)),
            pltpu.SemaphoreType.DMA((steps,)),
        ],
        compiler_params=pltpu.CompilerParams(collective_id=1, has_side_effects=True),
    )(mine)


def round_up(n, m):
    return (n + m - 1) // m * m


def on_device(
    tokens,
    w_zx,
    w_dt,
    w_bc,
    conv_x_weight,
    conv_x_bias,
    conv_bc_weight,
    conv_bc_bias,
    dt_bias,
    a_log,
    skip,
    norm_weight,
    w_out,
    lengths,
    request_group,
):
    tp_count = lax.axis_size("tp")
    seq_count = lax.axis_size(SEQ)
    seq_index = lax.axis_index(SEQ)
    tok_dev = tokens.shape[0]
    d_model = tokens.shape[1]
    local_rows = w_zx.shape[0]
    inner_local = conv_x_weight.shape[1]
    heads_local = dt_bias.shape[0]
    head_width = inner_local // heads_local
    bc_width = conv_bc_weight.shape[1]
    state_width = bc_width // 2
    taps = conv_x_weight.shape[0]
    groups_dev = tok_dev // GROUP

    zx_part = w_zx.astype(jnp.bfloat16).reshape(local_rows, 2, tp_count, inner_local)
    zx_part = zx_part.transpose(0, 2, 1, 3).reshape(local_rows, tp_count, 2 * inner_local)
    bc_part = jnp.broadcast_to(
        w_bc.astype(jnp.bfloat16)[:, None, :], (local_rows, tp_count, bc_width)
    )
    dt_part = w_dt.astype(jnp.bfloat16).reshape(local_rows, tp_count, heads_local)
    used = 2 * inner_local + bc_width + heads_local
    width = round_up(used, 128)
    pad_part = jnp.zeros((local_rows, tp_count, width - used), jnp.bfloat16)
    packed = jnp.concatenate([zx_part, bc_part, dt_part, pad_part], axis=2)
    packed = packed.reshape(local_rows, tp_count * width)
    block = lax.all_to_all(packed, "tp", split_axis=1, concat_axis=0, tiled=True)
    block_rows = block.shape[0]
    out_rows, out_cols = w_out.shape
    out_piece = w_out.astype(jnp.bfloat16).T
    gathered = gather_seq(jnp.concatenate([block, out_piece], axis=1))
    gathered = gathered.reshape(seq_count * block_rows, width + out_rows)
    proj = jnp.dot(tokens, gathered[:, :width], preferred_element_type=jnp.float32)
    zx_low = proj[:, : 2 * inner_local].astype(jnp.bfloat16)
    gate_z = zx_low[:, :inner_local]
    x_raw = zx_low[:, inner_local:]
    bc_raw = proj[:, 2 * inner_local : 2 * inner_local + bc_width].astype(jnp.bfloat16)
    dt_pre = proj[:, 2 * inner_local + bc_width : used]

    raw_mix = jnp.concatenate([x_raw, bc_raw], axis=1)
    conv_weight = jnp.concatenate([conv_x_weight, conv_bc_weight], axis=1)
    conv_bias = jnp.concatenate([conv_x_bias, conv_bc_bias], axis=0)
    rim_rows = from_behind(raw_mix[tok_dev - (taps - 1) :], 1)
    padded = jnp.concatenate([rim_rows, raw_mix], axis=0)
    offset = seq_index * tok_dev
    seg_pad = segment_of(
        offset - (taps - 1) + jnp.arange(tok_dev + taps - 1, dtype=jnp.int32), lengths
    )
    seg_tok = seg_pad[taps - 1 :]
    conv_sum = jnp.zeros((tok_dev, raw_mix.shape[1]), jnp.float32) + conv_bias[None, :]
    for offset_tap in range(taps):
        rows_wide = padded[offset_tap : offset_tap + tok_dev].astype(jnp.float32)
        keep_tap = seg_pad[offset_tap : offset_tap + tok_dev] == seg_tok
        conv_sum = conv_sum + jnp.where(
            keep_tap[:, None], rows_wide * conv_weight[offset_tap][None, :], 0.0
        )
    convolved = jax.nn.silu(conv_sum).astype(jnp.bfloat16)
    inputs = convolved[:, :inner_local].reshape(groups_dev, GROUP, heads_local, head_width)
    b_matrix = convolved[:, inner_local : inner_local + state_width].reshape(
        groups_dev, GROUP, state_width
    )
    c_matrix = convolved[:, inner_local + state_width :].reshape(groups_dev, GROUP, state_width)
    step_size = jax.nn.softplus(dt_pre + dt_bias[None, :]).reshape(groups_dev, GROUP, heads_local)
    step_heads = step_size.transpose(0, 2, 1)
    decay_rate = -jnp.exp(a_log)
    cumul_heads = jnp.cumsum(step_size * decay_rate[None, None, :], axis=1).transpose(0, 2, 1)
    segments = seg_tok.reshape(groups_dev, GROUP)
    seg_before = segment_of(offset + jnp.arange(groups_dev, dtype=jnp.int32) * GROUP - 1, lengths)
    within = jnp.arange(GROUP, dtype=jnp.int32)
    same_prompt = (segments[:, :, None] == segments[:, None, :]) & (
        within[:, None] >= within[None, :]
    )[None]
    log_decay = cumul_heads[:, :, :, None] - cumul_heads[:, :, None, :]
    decay_matrix = jnp.where(
        same_prompt[:, None], jnp.exp(jnp.where(same_prompt[:, None], log_decay, 0.0)), 0.0
    )
    scores = jnp.einsum("cin,cjn->cij", c_matrix, b_matrix, preferred_element_type=jnp.float32)
    mix_weights = (decay_matrix * scores[:, None] * step_heads[:, :, None, :]).astype(jnp.bfloat16)
    diag_out = jnp.einsum(
        "chij,cjhp->cihp", mix_weights, inputs, preferred_element_type=jnp.float32
    )
    last_segment = segments[:, -1]
    tail_weight = (
        jnp.where(
            (segments == last_segment[:, None])[:, None, :],
            jnp.exp(cumul_heads[:, :, -1:] - cumul_heads),
            0.0,
        )
        * step_heads
    )
    b_weighted = (b_matrix.astype(jnp.float32)[:, None] * tail_weight[:, :, :, None]).astype(
        jnp.bfloat16
    )
    contrib = jnp.einsum("cjhp,chjn->chpn", inputs, b_weighted, preferred_element_type=jnp.float32)
    pass_gate = jnp.where(
        (last_segment == seg_before)[:, None], jnp.exp(cumul_heads[:, :, -1]), 0.0
    )

    ends = [contrib[0]]
    for c in range(1, groups_dev):
        ends.append(pass_gate[c][:, None, None] * ends[-1] + contrib[c])
    local_end = jnp.stack(ends)
    local_in = jnp.concatenate([jnp.zeros_like(local_end[:1]), local_end[:-1]], axis=0)
    through_group = jnp.cumprod(pass_gate, axis=0)
    before_group = jnp.concatenate(
        [jnp.ones((1, heads_local), jnp.float32), through_group[:-1]], axis=0
    )

    gate_hi = through_group.astype(jnp.bfloat16)
    gate_lo = (through_group - gate_hi.astype(jnp.float32)).astype(jnp.bfloat16)
    extra = jnp.zeros((groups_dev, heads_local, 16, state_width), jnp.bfloat16)
    extra = extra.at[:, :, 0, :].set(jnp.broadcast_to(gate_hi[:, :, None], gate_hi.shape + (state_width,)))
    extra = extra.at[:, :, 1, :].set(jnp.broadcast_to(gate_lo[:, :, None], gate_lo.shape + (state_width,)))
    sendable = jnp.concatenate([local_end.astype(jnp.bfloat16), extra], axis=2)
    dev_row = jnp.zeros((heads_local, 8, state_width), jnp.float32)
    dev_row = dev_row.at[:, 0, :].set(
        jnp.broadcast_to(through_group[-1][:, None], (heads_local, state_width))
    )
    carried = carry_in(jnp.concatenate([local_end[-1], dev_row], axis=1), head_width)
    every = gather_seq(sendable).reshape(
        (seq_count * groups_dev, heads_local, head_width + 16, state_width)
    )
    gate_rows = every[:, :, head_width : head_width + 2, :].astype(jnp.float32)
    every_gate = (gate_rows[:, :, 0, 0] + gate_rows[:, :, 1, 0]).reshape(
        seq_count, groups_dev, heads_local
    )
    dev_gate = every_gate[:, -1]
    rows_at = jnp.arange(seq_count, dtype=jnp.int32)
    dev_of = rows_at

    def carry_weights(k):
        between = (dev_of[:, None] < dev_of[None, :]) & (dev_of[None, :] < k)
        factors = jnp.where(between[:, :, None], dev_gate[None, :, :], 1.0)
        return jnp.where((dev_of < k)[:, None], jnp.prod(factors, axis=1), 0.0)

    req_dev = request_group.shape[0] // seq_count
    mine = lax.dynamic_slice_in_dim(request_group, seq_index * req_dev, req_dev)
    req_k = mine // groups_dev
    req_c = mine % groups_dev
    req_row = req_k
    req_gate = every_gate[req_row, req_c]
    wanted = req_k
    weights_all = jax.vmap(carry_weights)(wanted)
    weights_all = weights_all * req_gate[:, None, :]
    slot_ids = jnp.arange(groups_dev, dtype=jnp.int32)
    last_slot = (slot_ids == groups_dev - 1).astype(jnp.float32)
    coef = weights_all[:, :, None, :] * last_slot[None, None, :, None]
    own_row = req_row
    own_slot = req_c
    hit = (rows_at[None, :, None] == own_row[:, None, None]) & (
        slot_ids[None, None, :] == own_slot[:, None, None]
    )
    coef = coef + hit[:, :, :, None].astype(jnp.float32)
    coef = coef.reshape(wanted.shape[0], seq_count * groups_dev, heads_local)
    coef_hi = coef.astype(jnp.bfloat16)
    coef_lo = (coef - coef_hi.astype(jnp.float32)).astype(jnp.bfloat16)
    summed_states = jnp.einsum(
        "rjh,jhpn->rhpn", coef_hi, every, preferred_element_type=jnp.float32
    ) + jnp.einsum("rjh,jhpn->rhpn", coef_lo, every, preferred_element_type=jnp.float32)
    request_states = summed_states[:, :, :head_width]

    group_in = before_group[:, :, None, None] * carried[None] + local_in
    state_low = group_in.astype(jnp.bfloat16)
    carry_keep = jnp.where((segments == seg_before[:, None])[:, None, :], jnp.exp(cumul_heads), 0.0)
    carry_out = jnp.einsum(
        "cin,chpn->cihp", c_matrix, state_low, preferred_element_type=jnp.float32
    )
    carry_out = carry_out * carry_keep.transpose(0, 2, 1)[:, :, :, None]
    y_local = diag_out + carry_out + skip[None, None, :, None] * inputs.astype(jnp.float32)
    y_local = y_local.reshape(tok_dev, inner_local)
    gated = y_local * jax.nn.silu(gate_z.astype(jnp.float32))
    square_sum = jnp.sum(gated * gated, axis=1)
    scaled = (gated * norm_weight[None, :]).astype(jnp.bfloat16)
    partial = lax.dot_general(
        scaled, gathered[:, width:], (((1,), (1,)), ((), ())), preferred_element_type=jnp.float32
    )
    side = jnp.zeros((tok_dev, 128), jnp.float32).at[:, 0].set(square_sum)
    summed = scatter_sum(jnp.concatenate([partial, side], axis=1).astype(jnp.bfloat16), tp_count)
    mean_square = summed[:, d_model] / INNER
    mixed = (summed[:, :d_model] * lax.rsqrt(mean_square + epsilon)[:, None]).astype(jnp.bfloat16)
    return (mixed, request_states)


def solution(mesh):
    return jax.shard_map(
        on_device,
        mesh=mesh,
        in_specs=(
            P(SEQ, None),
            P((SEQ, "tp"), None),
            P((SEQ, "tp"), None),
            P((SEQ, "tp"), None),
            P(None, "tp"),
            P("tp"),
            P(),
            P(),
            P("tp"),
            P("tp"),
            P("tp"),
            P("tp"),
            P("tp", SEQ),
            P(),
            P(),
        ),
        out_specs=(P((SEQ, "tp"), None), P(SEQ, "tp", None, None)),
        check_vma=False,
    )
```

```python
import functools

import jax
import jax.numpy as jnp
from jax import lax
from jax.experimental import pallas as pl
from jax.experimental.pallas import tpu as pltpu
from jax.sharding import PartitionSpec as P

INNER = 4096
GROUP = 256
SEQ = "seq"


epsilon = 1e-05


def from_behind(x, by):
    count = lax.axis_size(SEQ)
    pairs = [(i, i + by) for i in range(count) if 0 <= i + by < count]
    return lax.ppermute(x, SEQ, pairs)


def gather_seq(x):
    return lax.all_gather(x, SEQ, axis=0, tiled=False)


def segment_of(position, lengths):
    prompt_ends = jnp.cumsum(lengths)
    return jnp.sum((position[:, None] >= prompt_ends[None, :]).astype(jnp.int32), axis=1)


def scatter_sum_kernel(count, rows, x_ref, o_ref, recv, send_sem, recv_sem):
    me = lax.axis_index("tp")
    barrier = pltpu.get_barrier_semaphore()
    for d in range(1, count):
        peer = lax.rem(me + d, count)
        pl.semaphore_signal(barrier, inc=1, device_id={"tp": peer}, device_id_type=pl.DeviceIdType.MESH)
    pl.semaphore_wait(barrier, count - 1)
    copies = []
    half = count // 2
    order = [(1, k) for k in range(half)] + [(0, k) for k in range(1, half)]
    for d, (other, k) in enumerate(order, start=1):
        peer = lax.rem(me // half + other, 2) * half + lax.rem(me + k, half)
        copy = pltpu.make_async_remote_copy(
            src_ref=x_ref.at[pl.ds(pl.multiple_of(peer * rows, rows), rows)],
            dst_ref=recv.at[me],
            send_sem=send_sem.at[d],
            recv_sem=recv_sem.at[me],
            device_id={"tp": peer},
            device_id_type=pl.DeviceIdType.MESH,
        )
        copy.start()
        copies.append(copy)
    total = x_ref[pl.ds(pl.multiple_of(me * rows, rows), rows), :].astype(jnp.float32)
    for d in range(1, count):
        sender = lax.rem(me + count - d, count)
        arrival = pltpu.make_async_remote_copy(
            src_ref=x_ref.at[pl.ds(0, rows)],
            dst_ref=recv.at[sender],
            send_sem=send_sem.at[d],
            recv_sem=recv_sem.at[sender],
            device_id={"tp": sender},
            device_id_type=pl.DeviceIdType.MESH,
        )
        arrival.wait_recv()
        total = total + recv[sender].astype(jnp.float32)
    for copy in copies:
        copy.wait_send()
    o_ref[...] = total


def scatter_sum(x, count):
    rows = x.shape[0] // count
    cols = x.shape[1]
    return pl.pallas_call(
        functools.partial(scatter_sum_kernel, count, rows),
        out_shape=jax.ShapeDtypeStruct((rows, cols), jnp.float32),
        in_specs=[pl.BlockSpec(memory_space=pltpu.VMEM)],
        out_specs=pl.BlockSpec(memory_space=pltpu.VMEM),
        scratch_shapes=[
            pltpu.VMEM((count, rows, cols), x.dtype),
            pltpu.SemaphoreType.DMA((count,)),
            pltpu.SemaphoreType.DMA((count,)),
        ],
        compiler_params=pltpu.CompilerParams(collective_id=0, has_side_effects=True),
    )(x)


def scan_kernel(count, width, mine_ref, out_ref, acc, send_buf, recv, send_sem, recv_sem):
    me = lax.axis_index(SEQ)
    barrier = pltpu.get_barrier_semaphore()
    for d in range(1, count):
        peer = lax.rem(me + d, count)
        pl.semaphore_signal(barrier, inc=1, device_id={SEQ: peer}, device_id_type=pl.DeviceIdType.MESH)
    pl.semaphore_wait(barrier, count - 1)
    distances = [1]
    while distances[-1] * 2 < count:
        distances.append(distances[-1] * 2)
    rounds = [1] + distances

    def link(r, dist, target):
        return pltpu.make_async_remote_copy(
            src_ref=mine_ref if r == 0 else send_buf.at[r],
            dst_ref=recv.at[r],
            send_sem=send_sem.at[r],
            recv_sem=recv_sem.at[r],
            device_id={SEQ: target},
            device_id_type=pl.DeviceIdType.MESH,
        )

    rows = acc.shape[1]
    is_gate_row = lax.broadcasted_iota(jnp.int32, acc.shape, 1) == width
    acc[...] = jnp.where(is_gate_row, 1.0, 0.0).astype(acc.dtype)
    for r, dist in enumerate(rounds):
        if r > 0:
            send_buf[r] = acc[...]

        @pl.when(me + dist < count)
        def _():
            link(r, dist, me + dist).start()

        @pl.when(me >= dist)
        def _():
            link(r, dist, me - dist).wait_recv()
            if r == 0:
                acc[...] = recv[0]
            else:
                came = recv[r]
                mine_gate = acc[:, width : width + 8, :][:, 0:1, :]
                came_gate = came[:, width : width + 8, :][:, 0:1, :]
                state = mine_gate * came + acc[...]
                acc[...] = jnp.where(is_gate_row, mine_gate * came_gate, state)

    for r, dist in enumerate(rounds):
        @pl.when(me + dist < count)
        def _():
            link(r, dist, me + dist).wait_send()
    out_ref[...] = acc[:, :width, :]


def carry_in(mine, width):
    count = lax.axis_size(SEQ)
    heads, rows, lanes = mine.shape
    steps = 1
    while (1 << (steps - 1)) < count:
        steps += 1
    return pl.pallas_call(
        functools.partial(scan_kernel, count, width),
        out_shape=jax.ShapeDtypeStruct((heads, width, lanes), jnp.float32),
        in_specs=[pl.BlockSpec(memory_space=pltpu.VMEM)],
        out_specs=pl.BlockSpec(memory_space=pltpu.VMEM),
        scratch_shapes=[
            pltpu.VMEM(mine.shape, jnp.float32),
            pltpu.VMEM((steps,) + mine.shape, jnp.float32),
            pltpu.VMEM((steps,) + mine.shape, jnp.float32),
            pltpu.SemaphoreType.DMA((steps,)),
            pltpu.SemaphoreType.DMA((steps,)),
        ],
        compiler_params=pltpu.CompilerParams(collective_id=1, has_side_effects=True),
    )(mine)


def round_up(n, m):
    return (n + m - 1) // m * m


def on_device(
    tokens,
    w_zx,
    w_dt,
    w_bc,
    conv_x_weight,
    conv_x_bias,
    conv_bc_weight,
    conv_bc_bias,
    dt_bias,
    a_log,
    skip,
    norm_weight,
    w_out,
    lengths,
    request_group,
):
    tp_count = lax.axis_size("tp")
    seq_count = lax.axis_size(SEQ)
    seq_index = lax.axis_index(SEQ)
    tok_dev = tokens.shape[0]
    d_model = tokens.shape[1]
    local_rows = w_zx.shape[0]
    inner_local = conv_x_weight.shape[1]
    heads_local = dt_bias.shape[0]
    head_width = inner_local // heads_local
    bc_width = conv_bc_weight.shape[1]
    state_width = bc_width // 2
    taps = conv_x_weight.shape[0]
    groups_dev = tok_dev // GROUP

    zx_part = w_zx.astype(jnp.bfloat16).reshape(local_rows, 2, tp_count, inner_local)
    zx_part = zx_part.transpose(0, 2, 1, 3).reshape(local_rows, tp_count, 2 * inner_local)
    bc_part = jnp.broadcast_to(
        w_bc.astype(jnp.bfloat16)[:, None, :], (local_rows, tp_count, bc_width)
    )
    dt_part = w_dt.astype(jnp.bfloat16).reshape(local_rows, tp_count, heads_local)
    used = 2 * inner_local + bc_width + heads_local
    width = round_up(used, 128)
    pad_part = jnp.zeros((local_rows, tp_count, width - used), jnp.bfloat16)
    packed = jnp.concatenate([zx_part, bc_part, dt_part, pad_part], axis=2)
    packed = packed.reshape(local_rows, tp_count * width)
    block = lax.all_to_all(packed, "tp", split_axis=1, concat_axis=0, tiled=True)
    block_rows = block.shape[0]
    out_rows, out_cols = w_out.shape
    out_piece = w_out.astype(jnp.bfloat16).T
    gathered = gather_seq(jnp.concatenate([block, out_piece], axis=1))
    gathered = gathered.reshape(seq_count * block_rows, width + out_rows)
    proj = jnp.dot(tokens, gathered[:, :width], preferred_element_type=jnp.float32)
    zx_low = proj[:, : 2 * inner_local].astype(jnp.bfloat16)
    gate_z = zx_low[:, :inner_local]
    x_raw = zx_low[:, inner_local:]
    bc_raw = proj[:, 2 * inner_local : 2 * inner_local + bc_width].astype(jnp.bfloat16)
    dt_pre = proj[:, 2 * inner_local + bc_width : used]

    raw_mix = jnp.concatenate([x_raw, bc_raw], axis=1)
    conv_weight = jnp.concatenate([conv_x_weight, conv_bc_weight], axis=1)
    conv_bias = jnp.concatenate([conv_x_bias, conv_bc_bias], axis=0)
    rim_rows = from_behind(raw_mix[tok_dev - (taps - 1) :], 1)
    padded = jnp.concatenate([rim_rows, raw_mix], axis=0)
    offset = seq_index * tok_dev
    seg_pad = segment_of(
        offset - (taps - 1) + jnp.arange(tok_dev + taps - 1, dtype=jnp.int32), lengths
    )
    seg_tok = seg_pad[taps - 1 :]
    conv_sum = jnp.zeros((tok_dev, raw_mix.shape[1]), jnp.float32) + conv_bias[None, :]
    for offset_tap in range(taps):
        rows_wide = padded[offset_tap : offset_tap + tok_dev].astype(jnp.float32)
        keep_tap = seg_pad[offset_tap : offset_tap + tok_dev] == seg_tok
        conv_sum = conv_sum + jnp.where(
            keep_tap[:, None], rows_wide * conv_weight[offset_tap][None, :], 0.0
        )
    convolved = jax.nn.silu(conv_sum).astype(jnp.bfloat16)
    inputs = convolved[:, :inner_local].reshape(groups_dev, GROUP, heads_local, head_width)
    b_matrix = convolved[:, inner_local : inner_local + state_width].reshape(
        groups_dev, GROUP, state_width
    )
    c_matrix = convolved[:, inner_local + state_width :].reshape(groups_dev, GROUP, state_width)
    step_size = jax.nn.softplus(dt_pre + dt_bias[None, :]).reshape(groups_dev, GROUP, heads_local)
    step_heads = step_size.transpose(0, 2, 1)
    decay_rate = -jnp.exp(a_log)
    cumul_heads = jnp.cumsum(step_size * decay_rate[None, None, :], axis=1).transpose(0, 2, 1)
    segments = seg_tok.reshape(groups_dev, GROUP)
    seg_before = segment_of(offset + jnp.arange(groups_dev, dtype=jnp.int32) * GROUP - 1, lengths)
    within = jnp.arange(GROUP, dtype=jnp.int32)
    same_prompt = (segments[:, :, None] == segments[:, None, :]) & (
        within[:, None] >= within[None, :]
    )[None]
    log_decay = cumul_heads[:, :, :, None] - cumul_heads[:, :, None, :]
    decay_matrix = jnp.where(
        same_prompt[:, None], jnp.exp(jnp.where(same_prompt[:, None], log_decay, 0.0)), 0.0
    )
    scores = jnp.einsum("cin,cjn->cij", c_matrix, b_matrix, preferred_element_type=jnp.float32)
    mix_weights = (decay_matrix * scores[:, None] * step_heads[:, :, None, :]).astype(jnp.bfloat16)
    diag_out = jnp.einsum(
        "chij,cjhp->cihp", mix_weights, inputs, preferred_element_type=jnp.float32
    )
    last_segment = segments[:, -1]
    tail_weight = (
        jnp.where(
            (segments == last_segment[:, None])[:, None, :],
            jnp.exp(cumul_heads[:, :, -1:] - cumul_heads),
            0.0,
        )
        * step_heads
    )
    b_weighted = (b_matrix.astype(jnp.float32)[:, None] * tail_weight[:, :, :, None]).astype(
        jnp.bfloat16
    )
    contrib = jnp.einsum("cjhp,chjn->chpn", inputs, b_weighted, preferred_element_type=jnp.float32)
    pass_gate = jnp.where(
        (last_segment == seg_before)[:, None], jnp.exp(cumul_heads[:, :, -1]), 0.0
    )

    ends = [contrib[0]]
    for c in range(1, groups_dev):
        ends.append(pass_gate[c][:, None, None] * ends[-1] + contrib[c])
    local_end = jnp.stack(ends)
    local_in = jnp.concatenate([jnp.zeros_like(local_end[:1]), local_end[:-1]], axis=0)
    through_group = jnp.cumprod(pass_gate, axis=0)
    before_group = jnp.concatenate(
        [jnp.ones((1, heads_local), jnp.float32), through_group[:-1]], axis=0
    )

    gate_hi = through_group.astype(jnp.bfloat16)
    gate_lo = (through_group - gate_hi.astype(jnp.float32)).astype(jnp.bfloat16)
    extra = jnp.zeros((groups_dev, heads_local, 16, state_width), jnp.bfloat16)
    extra = extra.at[:, :, 0, :].set(jnp.broadcast_to(gate_hi[:, :, None], gate_hi.shape + (state_width,)))
    extra = extra.at[:, :, 1, :].set(jnp.broadcast_to(gate_lo[:, :, None], gate_lo.shape + (state_width,)))
    sendable = jnp.concatenate([local_end.astype(jnp.bfloat16), extra], axis=2)
    dev_row = jnp.zeros((heads_local, 8, state_width), jnp.float32)
    dev_row = dev_row.at[:, 0, :].set(
        jnp.broadcast_to(through_group[-1][:, None], (heads_local, state_width))
    )
    carried = carry_in(jnp.concatenate([local_end[-1], dev_row], axis=1), head_width)
    carried, later = lax.optimization_barrier((carried, sendable))
    every = gather_seq(later).reshape(
        (seq_count * groups_dev, heads_local, head_width + 16, state_width)
    )
    gate_rows = every[:, :, head_width : head_width + 2, :].astype(jnp.float32)
    every_gate = (gate_rows[:, :, 0, 0] + gate_rows[:, :, 1, 0]).reshape(
        seq_count, groups_dev, heads_local
    )
    dev_gate = every_gate[:, -1]
    rows_at = jnp.arange(seq_count, dtype=jnp.int32)
    dev_of = rows_at

    def carry_weights(k):
        between = (dev_of[:, None] < dev_of[None, :]) & (dev_of[None, :] < k)
        factors = jnp.where(between[:, :, None], dev_gate[None, :, :], 1.0)
        return jnp.where((dev_of < k)[:, None], jnp.prod(factors, axis=1), 0.0)

    req_dev = request_group.shape[0] // seq_count
    mine = lax.dynamic_slice_in_dim(request_group, seq_index * req_dev, req_dev)
    req_k = mine // groups_dev
    req_c = mine % groups_dev
    req_row = req_k
    req_gate = every_gate[req_row, req_c]
    wanted = req_k
    weights_all = jax.vmap(carry_weights)(wanted)
    weights_all = weights_all * req_gate[:, None, :]
    slot_ids = jnp.arange(groups_dev, dtype=jnp.int32)
    last_slot = (slot_ids == groups_dev - 1).astype(jnp.float32)
    coef = weights_all[:, :, None, :] * last_slot[None, None, :, None]
    own_row = req_row
    own_slot = req_c
    hit = (rows_at[None, :, None] == own_row[:, None, None]) & (
        slot_ids[None, None, :] == own_slot[:, None, None]
    )
    coef = coef + hit[:, :, :, None].astype(jnp.float32)
    coef = coef.reshape(wanted.shape[0], seq_count * groups_dev, heads_local)
    coef_hi = coef.astype(jnp.bfloat16)
    coef_lo = (coef - coef_hi.astype(jnp.float32)).astype(jnp.bfloat16)
    summed_states = jnp.einsum(
        "rjh,jhpn->rhpn", coef_hi, every, preferred_element_type=jnp.float32
    ) + jnp.einsum("rjh,jhpn->rhpn", coef_lo, every, preferred_element_type=jnp.float32)
    request_states = summed_states[:, :, :head_width]

    group_in = before_group[:, :, None, None] * carried[None] + local_in
    state_low = group_in.astype(jnp.bfloat16)
    carry_keep = jnp.where((segments == seg_before[:, None])[:, None, :], jnp.exp(cumul_heads), 0.0)
    carry_out = jnp.einsum(
        "cin,chpn->cihp", c_matrix, state_low, preferred_element_type=jnp.float32
    )
    carry_out = carry_out * carry_keep.transpose(0, 2, 1)[:, :, :, None]
    y_local = diag_out + carry_out + skip[None, None, :, None] * inputs.astype(jnp.float32)
    y_local = y_local.reshape(tok_dev, inner_local)
    gated = y_local * jax.nn.silu(gate_z.astype(jnp.float32))
    square_sum = jnp.sum(gated * gated, axis=1)
    scaled = (gated * norm_weight[None, :]).astype(jnp.bfloat16)
    partial = lax.dot_general(
        scaled, gathered[:, width:], (((1,), (1,)), ((), ())), preferred_element_type=jnp.float32
    )
    side = jnp.zeros((tok_dev, 128), jnp.float32).at[:, 0].set(square_sum)
    summed = scatter_sum(jnp.concatenate([partial, side], axis=1).astype(jnp.bfloat16), tp_count)
    mean_square = summed[:, d_model] / INNER
    mixed = (summed[:, :d_model] * lax.rsqrt(mean_square + epsilon)[:, None]).astype(jnp.bfloat16)
    return (mixed, request_states)


def solution(mesh):
    return jax.shard_map(
        on_device,
        mesh=mesh,
        in_specs=(
            P(SEQ, None),
            P((SEQ, "tp"), None),
            P((SEQ, "tp"), None),
            P((SEQ, "tp"), None),
            P(None, "tp"),
            P("tp"),
            P(),
            P(),
            P("tp"),
            P("tp"),
            P("tp"),
            P("tp"),
            P("tp", SEQ),
            P(),
            P(),
        ),
        out_specs=(P((SEQ, "tp"), None), P(SEQ, "tp", None, None)),
        check_vma=False,
    )
```

```python
import functools

import jax
import jax.numpy as jnp
from jax import lax
from jax.experimental import pallas as pl
from jax.experimental.pallas import tpu as pltpu
from jax.sharding import PartitionSpec as P

INNER = 4096
GROUP = 256
SEQ = "seq"


epsilon = 1e-05


def from_behind(x, by):
    count = lax.axis_size(SEQ)
    pairs = [(i, i + by) for i in range(count) if 0 <= i + by < count]
    return lax.ppermute(x, SEQ, pairs)


def gather_seq(x):
    return lax.all_gather(x, SEQ, axis=0, tiled=False)


def segment_of(position, lengths):
    prompt_ends = jnp.cumsum(lengths)
    return jnp.sum((position[:, None] >= prompt_ends[None, :]).astype(jnp.int32), axis=1)


def scatter_sum_kernel(count, rows, x_ref, o_ref, recv, send_sem, recv_sem):
    me = lax.axis_index("tp")
    barrier = pltpu.get_barrier_semaphore()
    for d in range(1, count):
        peer = lax.rem(me + d, count)
        pl.semaphore_signal(barrier, inc=1, device_id={"tp": peer}, device_id_type=pl.DeviceIdType.MESH)
    pl.semaphore_wait(barrier, count - 1)
    copies = []
    for d in range(1, count):
        peer = lax.rem(me + d, count)
        copy = pltpu.make_async_remote_copy(
            src_ref=x_ref.at[pl.ds(pl.multiple_of(peer * rows, rows), rows)],
            dst_ref=recv.at[me],
            send_sem=send_sem.at[d],
            recv_sem=recv_sem.at[me],
            device_id={"tp": peer},
            device_id_type=pl.DeviceIdType.MESH,
        )
        copy.start()
        copies.append(copy)
    total = x_ref[pl.ds(pl.multiple_of(me * rows, rows), rows), :].astype(jnp.float32)
    for d in range(1, count):
        sender = lax.rem(me + count - d, count)
        arrival = pltpu.make_async_remote_copy(
            src_ref=x_ref.at[pl.ds(0, rows)],
            dst_ref=recv.at[sender],
            send_sem=send_sem.at[d],
            recv_sem=recv_sem.at[sender],
            device_id={"tp": sender},
            device_id_type=pl.DeviceIdType.MESH,
        )
        arrival.wait_recv()
        total = total + recv[sender].astype(jnp.float32)
    for copy in copies:
        copy.wait_send()
    o_ref[...] = total


def scatter_sum(x, count):
    rows = x.shape[0] // count
    cols = x.shape[1]
    return pl.pallas_call(
        functools.partial(scatter_sum_kernel, count, rows),
        out_shape=jax.ShapeDtypeStruct((rows, cols), jnp.float32),
        in_specs=[pl.BlockSpec(memory_space=pltpu.VMEM)],
        out_specs=pl.BlockSpec(memory_space=pltpu.VMEM),
        scratch_shapes=[
            pltpu.VMEM((count, rows, cols), x.dtype),
            pltpu.SemaphoreType.DMA((count,)),
            pltpu.SemaphoreType.DMA((count,)),
        ],
        compiler_params=pltpu.CompilerParams(collective_id=0, has_side_effects=True),
    )(x)


def scan_kernel(count, width, mine_ref, out_ref, acc, send_buf, recv, send_sem, recv_sem):
    me = lax.axis_index(SEQ)
    barrier = pltpu.get_barrier_semaphore()
    for d in range(1, count):
        peer = lax.rem(me + d, count)
        pl.semaphore_signal(barrier, inc=1, device_id={SEQ: peer}, device_id_type=pl.DeviceIdType.MESH)
    pl.semaphore_wait(barrier, count - 1)
    distances = [1]
    while distances[-1] * 2 < count:
        distances.append(distances[-1] * 2)
    rounds = [1] + distances

    def link(r, dist, target):
        return pltpu.make_async_remote_copy(
            src_ref=mine_ref if r == 0 else send_buf.at[r],
            dst_ref=recv.at[r],
            send_sem=send_sem.at[r],
            recv_sem=recv_sem.at[r],
            device_id={SEQ: target},
            device_id_type=pl.DeviceIdType.MESH,
        )

    rows = acc.shape[1]
    is_gate_row = lax.broadcasted_iota(jnp.int32, acc.shape, 1) == width
    acc[...] = jnp.where(is_gate_row, 1.0, 0.0).astype(acc.dtype)
    for r, dist in enumerate(rounds):
        if r > 0:
            send_buf[r] = acc[...]

        @pl.when(me + dist < count)
        def _():
            link(r, dist, me + dist).start()

        @pl.when(me >= dist)
        def _():
            link(r, dist, me - dist).wait_recv()
            if r == 0:
                acc[...] = recv[0]
            else:
                came = recv[r]
                mine_gate = acc[:, width : width + 8, :][:, 0:1, :]
                came_gate = came[:, width : width + 8, :][:, 0:1, :]
                state = mine_gate * came + acc[...]
                acc[...] = jnp.where(is_gate_row, mine_gate * came_gate, state)

    for r, dist in enumerate(rounds):
        @pl.when(me + dist < count)
        def _():
            link(r, dist, me + dist).wait_send()
    out_ref[...] = acc[:, :width, :]


def carry_in(mine, width):
    count = lax.axis_size(SEQ)
    heads, rows, lanes = mine.shape
    steps = 1
    while (1 << (steps - 1)) < count:
        steps += 1
    return pl.pallas_call(
        functools.partial(scan_kernel, count, width),
        out_shape=jax.ShapeDtypeStruct((heads, width, lanes), jnp.float32),
        in_specs=[pl.BlockSpec(memory_space=pltpu.VMEM)],
        out_specs=pl.BlockSpec(memory_space=pltpu.VMEM),
        scratch_shapes=[
            pltpu.VMEM(mine.shape, jnp.float32),
            pltpu.VMEM((steps,) + mine.shape, jnp.float32),
            pltpu.VMEM((steps,) + mine.shape, jnp.float32),
            pltpu.SemaphoreType.DMA((steps,)),
            pltpu.SemaphoreType.DMA((steps,)),
        ],
        compiler_params=pltpu.CompilerParams(collective_id=1, has_side_effects=True),
    )(mine)


def round_up(n, m):
    return (n + m - 1) // m * m


def on_device(
    tokens,
    w_zx,
    w_dt,
    w_bc,
    conv_x_weight,
    conv_x_bias,
    conv_bc_weight,
    conv_bc_bias,
    dt_bias,
    a_log,
    skip,
    norm_weight,
    w_out,
    lengths,
    request_group,
):
    tp_count = lax.axis_size("tp")
    seq_count = lax.axis_size(SEQ)
    seq_index = lax.axis_index(SEQ)
    tok_dev = tokens.shape[0]
    d_model = tokens.shape[1]
    local_rows = w_zx.shape[0]
    inner_local = conv_x_weight.shape[1]
    heads_local = dt_bias.shape[0]
    head_width = inner_local // heads_local
    bc_width = conv_bc_weight.shape[1]
    state_width = bc_width // 2
    taps = conv_x_weight.shape[0]
    groups_dev = tok_dev // GROUP

    zx_part = w_zx.astype(jnp.bfloat16).reshape(local_rows, 2, tp_count, inner_local)
    zx_part = zx_part.transpose(0, 2, 1, 3).reshape(local_rows, tp_count, 2 * inner_local)
    bc_part = jnp.broadcast_to(
        w_bc.astype(jnp.bfloat16)[:, None, :], (local_rows, tp_count, bc_width)
    )
    dt_part = w_dt.astype(jnp.bfloat16).reshape(local_rows, tp_count, heads_local)
    used = 2 * inner_local + bc_width + heads_local
    width = round_up(used, 128)
    pad_part = jnp.zeros((local_rows, tp_count, width - used), jnp.bfloat16)
    packed = jnp.concatenate([zx_part, bc_part, dt_part, pad_part], axis=2)
    packed = packed.reshape(local_rows, tp_count * width)
    block = lax.all_to_all(packed, "tp", split_axis=1, concat_axis=0, tiled=True)
    block_rows = block.shape[0]
    out_rows, out_cols = w_out.shape
    out_piece = w_out.astype(jnp.bfloat16).T
    gathered = gather_seq(jnp.concatenate([block, out_piece], axis=1))
    gathered = gathered.reshape(seq_count * block_rows, width + out_rows)
    proj = jnp.dot(tokens, gathered[:, :width], preferred_element_type=jnp.float32)
    zx_low = proj[:, : 2 * inner_local].astype(jnp.bfloat16)
    gate_z = zx_low[:, :inner_local]
    x_raw = zx_low[:, inner_local:]
    bc_raw = proj[:, 2 * inner_local : 2 * inner_local + bc_width].astype(jnp.bfloat16)
    dt_pre = proj[:, 2 * inner_local + bc_width : used]

    raw_mix = jnp.concatenate([x_raw, bc_raw], axis=1)
    conv_weight = jnp.concatenate([conv_x_weight, conv_bc_weight], axis=1)
    conv_bias = jnp.concatenate([conv_x_bias, conv_bc_bias], axis=0)
    rim_rows = from_behind(raw_mix[tok_dev - (taps - 1) :], 1)
    padded = jnp.concatenate([rim_rows, raw_mix], axis=0)
    offset = seq_index * tok_dev
    seg_pad = segment_of(
        offset - (taps - 1) + jnp.arange(tok_dev + taps - 1, dtype=jnp.int32), lengths
    )
    seg_tok = seg_pad[taps - 1 :]
    conv_sum = jnp.zeros((tok_dev, raw_mix.shape[1]), jnp.float32) + conv_bias[None, :]
    for offset_tap in range(taps):
        rows_wide = padded[offset_tap : offset_tap + tok_dev].astype(jnp.float32)
        keep_tap = seg_pad[offset_tap : offset_tap + tok_dev] == seg_tok
        conv_sum = conv_sum + jnp.where(
            keep_tap[:, None], rows_wide * conv_weight[offset_tap][None, :], 0.0
        )
    convolved = jax.nn.silu(conv_sum).astype(jnp.bfloat16)
    inputs = convolved[:, :inner_local].reshape(groups_dev, GROUP, heads_local, head_width)
    b_matrix = convolved[:, inner_local : inner_local + state_width].reshape(
        groups_dev, GROUP, state_width
    )
    c_matrix = convolved[:, inner_local + state_width :].reshape(groups_dev, GROUP, state_width)
    step_size = jax.nn.softplus(dt_pre + dt_bias[None, :]).reshape(groups_dev, GROUP, heads_local)
    step_heads = step_size.transpose(0, 2, 1)
    decay_rate = -jnp.exp(a_log)
    cumul_heads = jnp.cumsum(step_size * decay_rate[None, None, :], axis=1).transpose(0, 2, 1)
    segments = seg_tok.reshape(groups_dev, GROUP)
    seg_before = segment_of(offset + jnp.arange(groups_dev, dtype=jnp.int32) * GROUP - 1, lengths)
    within = jnp.arange(GROUP, dtype=jnp.int32)
    same_prompt = (segments[:, :, None] == segments[:, None, :]) & (
        within[:, None] >= within[None, :]
    )[None]
    log_decay = cumul_heads[:, :, :, None] - cumul_heads[:, :, None, :]
    decay_matrix = jnp.where(
        same_prompt[:, None], jnp.exp(jnp.where(same_prompt[:, None], log_decay, 0.0)), 0.0
    )
    scores = jnp.einsum("cin,cjn->cij", c_matrix, b_matrix, preferred_element_type=jnp.float32)
    mix_weights = (decay_matrix * scores[:, None] * step_heads[:, :, None, :]).astype(jnp.bfloat16)
    diag_out = jnp.einsum(
        "chij,cjhp->cihp", mix_weights, inputs, preferred_element_type=jnp.float32
    )
    last_segment = segments[:, -1]
    tail_weight = (
        jnp.where(
            (segments == last_segment[:, None])[:, None, :],
            jnp.exp(cumul_heads[:, :, -1:] - cumul_heads),
            0.0,
        )
        * step_heads
    )
    b_weighted = (b_matrix.astype(jnp.float32)[:, None] * tail_weight[:, :, :, None]).astype(
        jnp.bfloat16
    )
    contrib = jnp.einsum("cjhp,chjn->chpn", inputs, b_weighted, preferred_element_type=jnp.float32)
    pass_gate = jnp.where(
        (last_segment == seg_before)[:, None], jnp.exp(cumul_heads[:, :, -1]), 0.0
    )

    ends = [contrib[0]]
    for c in range(1, groups_dev):
        ends.append(pass_gate[c][:, None, None] * ends[-1] + contrib[c])
    local_end = jnp.stack(ends)
    local_in = jnp.concatenate([jnp.zeros_like(local_end[:1]), local_end[:-1]], axis=0)
    through_group = jnp.cumprod(pass_gate, axis=0)
    before_group = jnp.concatenate(
        [jnp.ones((1, heads_local), jnp.float32), through_group[:-1]], axis=0
    )

    dev_row = jnp.zeros((heads_local, 8, state_width), jnp.float32)
    dev_row = dev_row.at[:, 0, :].set(
        jnp.broadcast_to(through_group[-1][:, None], (heads_local, state_width))
    )
    carried = carry_in(jnp.concatenate([local_end[-1], dev_row], axis=1), head_width)
    group_end = through_group[:, :, None, None] * carried[None] + local_end
    every = gather_seq(group_end.astype(jnp.bfloat16)).reshape(
        (seq_count * groups_dev,) + group_end.shape[1:]
    )
    req_dev = request_group.shape[0] // seq_count
    mine = lax.dynamic_slice_in_dim(request_group, seq_index * req_dev, req_dev)
    request_states = jnp.stack(
        [lax.dynamic_index_in_dim(every, mine[i], 0, keepdims=False) for i in range(req_dev)]
    ).astype(jnp.float32)

    group_in = before_group[:, :, None, None] * carried[None] + local_in
    state_low = group_in.astype(jnp.bfloat16)
    carry_keep = jnp.where((segments == seg_before[:, None])[:, None, :], jnp.exp(cumul_heads), 0.0)
    carry_out = jnp.einsum(
        "cin,chpn->cihp", c_matrix, state_low, preferred_element_type=jnp.float32
    )
    carry_out = carry_out * carry_keep.transpose(0, 2, 1)[:, :, :, None]
    y_local = diag_out + carry_out + skip[None, None, :, None] * inputs.astype(jnp.float32)
    y_local = y_local.reshape(tok_dev, inner_local)
    gated = y_local * jax.nn.silu(gate_z.astype(jnp.float32))
    square_sum = jnp.sum(gated * gated, axis=1)
    scaled = (gated * norm_weight[None, :]).astype(jnp.bfloat16)
    partial = lax.dot_general(
        scaled, gathered[:, width:], (((1,), (1,)), ((), ())), preferred_element_type=jnp.float32
    )
    side = jnp.zeros((tok_dev, 128), jnp.float32).at[:, 0].set(square_sum)
    summed = scatter_sum(jnp.concatenate([partial, side], axis=1).astype(jnp.bfloat16), tp_count)
    mean_square = summed[:, d_model] / INNER
    mixed = (summed[:, :d_model] * lax.rsqrt(mean_square + epsilon)[:, None]).astype(jnp.bfloat16)
    return (mixed, request_states)


def solution(mesh):
    return jax.shard_map(
        on_device,
        mesh=mesh,
        in_specs=(
            P(SEQ, None),
            P((SEQ, "tp"), None),
            P((SEQ, "tp"), None),
            P((SEQ, "tp"), None),
            P(None, "tp"),
            P("tp"),
            P(),
            P(),
            P("tp"),
            P("tp"),
            P("tp"),
            P("tp"),
            P("tp", SEQ),
            P(),
            P(),
        ),
        out_specs=(P((SEQ, "tp"), None), P(SEQ, "tp", None, None)),
        check_vma=False,
    )
```

```python
import functools

import jax
import jax.numpy as jnp
from jax import lax
from jax.experimental import pallas as pl
from jax.experimental.pallas import tpu as pltpu
from jax.sharding import PartitionSpec as P

INNER = 4096
GROUP = 256
SEQ = "seq"


epsilon = 1e-05


def from_behind(x, by):
    count = lax.axis_size(SEQ)
    pairs = [(i, i + by) for i in range(count) if 0 <= i + by < count]
    return lax.ppermute(x, SEQ, pairs)


def gather_seq(x):
    return lax.all_gather(x, SEQ, axis=0, tiled=False)


def segment_of(position, lengths):
    prompt_ends = jnp.cumsum(lengths)
    return jnp.sum((position[:, None] >= prompt_ends[None, :]).astype(jnp.int32), axis=1)


def scatter_sum_kernel(count, rows, x_ref, o_ref, recv, send_sem, recv_sem):
    me = lax.axis_index("tp")
    barrier = pltpu.get_barrier_semaphore()
    for d in range(1, count):
        peer = lax.rem(me + d, count)
        pl.semaphore_signal(barrier, inc=1, device_id={"tp": peer}, device_id_type=pl.DeviceIdType.MESH)
    pl.semaphore_wait(barrier, count - 1)
    copies = []
    for d in range(1, count):
        peer = lax.rem(me + d, count)
        copy = pltpu.make_async_remote_copy(
            src_ref=x_ref.at[pl.ds(pl.multiple_of(peer * rows, rows), rows)],
            dst_ref=recv.at[me],
            send_sem=send_sem.at[d],
            recv_sem=recv_sem.at[me],
            device_id={"tp": peer},
            device_id_type=pl.DeviceIdType.MESH,
        )
        copy.start()
        copies.append(copy)
    total = x_ref[pl.ds(pl.multiple_of(me * rows, rows), rows), :].astype(jnp.float32)
    for d in range(1, count):
        sender = lax.rem(me + count - d, count)
        arrival = pltpu.make_async_remote_copy(
            src_ref=x_ref.at[pl.ds(0, rows)],
            dst_ref=recv.at[sender],
            send_sem=send_sem.at[d],
            recv_sem=recv_sem.at[sender],
            device_id={"tp": sender},
            device_id_type=pl.DeviceIdType.MESH,
        )
        arrival.wait_recv()
        total = total + recv[sender].astype(jnp.float32)
    for copy in copies:
        copy.wait_send()
    o_ref[...] = total


def scatter_sum(x, count):
    rows = x.shape[0] // count
    cols = x.shape[1]
    return pl.pallas_call(
        functools.partial(scatter_sum_kernel, count, rows),
        out_shape=jax.ShapeDtypeStruct((rows, cols), jnp.float32),
        in_specs=[pl.BlockSpec(memory_space=pltpu.VMEM)],
        out_specs=pl.BlockSpec(memory_space=pltpu.VMEM),
        scratch_shapes=[
            pltpu.VMEM((count, rows, cols), x.dtype),
            pltpu.SemaphoreType.DMA((count,)),
            pltpu.SemaphoreType.DMA((count,)),
        ],
        compiler_params=pltpu.CompilerParams(collective_id=0, has_side_effects=True),
    )(x)


def scan_kernel(count, width, mine_ref, out_ref, acc, send_buf, recv, send_sem, recv_sem):
    me = lax.axis_index(SEQ)
    barrier = pltpu.get_barrier_semaphore()
    for d in range(1, count):
        peer = lax.rem(me + d, count)
        pl.semaphore_signal(barrier, inc=1, device_id={SEQ: peer}, device_id_type=pl.DeviceIdType.MESH)
    pl.semaphore_wait(barrier, count - 1)
    distances = [1]
    while distances[-1] * 2 < count:
        distances.append(distances[-1] * 2)
    rounds = [1] + distances

    def link(r, dist, target):
        return pltpu.make_async_remote_copy(
            src_ref=mine_ref if r == 0 else send_buf.at[r],
            dst_ref=recv.at[r],
            send_sem=send_sem.at[r],
            recv_sem=recv_sem.at[r],
            device_id={SEQ: target},
            device_id_type=pl.DeviceIdType.MESH,
        )

    rows = acc.shape[1]
    is_gate_row = lax.broadcasted_iota(jnp.int32, acc.shape, 1) == width
    acc[...] = jnp.where(is_gate_row, 1.0, 0.0).astype(acc.dtype)
    for r, dist in enumerate(rounds):
        if r > 0:
            send_buf[r] = acc[...]

        @pl.when(me + dist < count)
        def _():
            link(r, dist, me + dist).start()

        @pl.when(me >= dist)
        def _():
            link(r, dist, me - dist).wait_recv()
            if r == 0:
                acc[...] = recv[0]
            else:
                came = recv[r]
                mine_gate = acc[:, width : width + 8, :][:, 0:1, :]
                came_gate = came[:, width : width + 8, :][:, 0:1, :]
                state = mine_gate * came + acc[...]
                acc[...] = jnp.where(is_gate_row, mine_gate * came_gate, state)

    for r, dist in enumerate(rounds):
        @pl.when(me + dist < count)
        def _():
            link(r, dist, me + dist).wait_send()
    out_ref[...] = acc[:, :width, :]


def carry_in(mine, width):
    count = lax.axis_size(SEQ)
    heads, rows, lanes = mine.shape
    steps = 1
    while (1 << (steps - 1)) < count:
        steps += 1
    return pl.pallas_call(
        functools.partial(scan_kernel, count, width),
        out_shape=jax.ShapeDtypeStruct((heads, width, lanes), jnp.float32),
        in_specs=[pl.BlockSpec(memory_space=pltpu.VMEM)],
        out_specs=pl.BlockSpec(memory_space=pltpu.VMEM),
        scratch_shapes=[
            pltpu.VMEM(mine.shape, jnp.float32),
            pltpu.VMEM((steps,) + mine.shape, jnp.float32),
            pltpu.VMEM((steps,) + mine.shape, jnp.float32),
            pltpu.SemaphoreType.DMA((steps,)),
            pltpu.SemaphoreType.DMA((steps,)),
        ],
        compiler_params=pltpu.CompilerParams(collective_id=1, has_side_effects=True),
    )(mine)


def round_up(n, m):
    return (n + m - 1) // m * m


def on_device(
    tokens,
    w_zx,
    w_dt,
    w_bc,
    conv_x_weight,
    conv_x_bias,
    conv_bc_weight,
    conv_bc_bias,
    dt_bias,
    a_log,
    skip,
    norm_weight,
    w_out,
    lengths,
    request_group,
):
    tp_count = lax.axis_size("tp")
    seq_count = lax.axis_size(SEQ)
    seq_index = lax.axis_index(SEQ)
    tok_dev = tokens.shape[0]
    d_model = tokens.shape[1]
    local_rows = w_zx.shape[0]
    inner_local = conv_x_weight.shape[1]
    heads_local = dt_bias.shape[0]
    head_width = inner_local // heads_local
    bc_width = conv_bc_weight.shape[1]
    state_width = bc_width // 2
    taps = conv_x_weight.shape[0]
    groups_dev = tok_dev // GROUP

    zx_part = w_zx.astype(jnp.bfloat16).reshape(local_rows, 2, tp_count, inner_local)
    zx_part = zx_part.transpose(0, 2, 1, 3).reshape(local_rows, tp_count, 2 * inner_local)
    bc_part = jnp.broadcast_to(
        w_bc.astype(jnp.bfloat16)[:, None, :], (local_rows, tp_count, bc_width)
    )
    dt_part = w_dt.astype(jnp.bfloat16).reshape(local_rows, tp_count, heads_local)
    used = 2 * inner_local + bc_width + heads_local
    width = round_up(used, 128)
    pad_part = jnp.zeros((local_rows, tp_count, width - used), jnp.bfloat16)
    packed = jnp.concatenate([zx_part, bc_part, dt_part, pad_part], axis=2)
    packed = packed.reshape(local_rows, tp_count * width)
    block = lax.all_to_all(packed, "tp", split_axis=1, concat_axis=0, tiled=True)
    block_rows = block.shape[0]
    out_rows, out_cols = w_out.shape
    out_piece = w_out.astype(jnp.bfloat16).T
    gathered = gather_seq(jnp.concatenate([block, out_piece], axis=1))
    gathered = gathered.reshape(seq_count * block_rows, width + out_rows)
    proj = jnp.dot(tokens, gathered[:, :width], preferred_element_type=jnp.float32)
    zx_low = proj[:, : 2 * inner_local].astype(jnp.bfloat16)
    gate_z = zx_low[:, :inner_local]
    x_raw = zx_low[:, inner_local:]
    bc_raw = proj[:, 2 * inner_local : 2 * inner_local + bc_width].astype(jnp.bfloat16)
    dt_pre = proj[:, 2 * inner_local + bc_width : used]

    raw_mix = jnp.concatenate([x_raw, bc_raw], axis=1)
    conv_weight = jnp.concatenate([conv_x_weight, conv_bc_weight], axis=1)
    conv_bias = jnp.concatenate([conv_x_bias, conv_bc_bias], axis=0)
    rim_rows = from_behind(raw_mix[tok_dev - (taps - 1) :], 1)
    padded = jnp.concatenate([rim_rows, raw_mix], axis=0)
    offset = seq_index * tok_dev
    seg_pad = segment_of(
        offset - (taps - 1) + jnp.arange(tok_dev + taps - 1, dtype=jnp.int32), lengths
    )
    seg_tok = seg_pad[taps - 1 :]
    conv_sum = jnp.zeros((tok_dev, raw_mix.shape[1]), jnp.float32) + conv_bias[None, :]
    for offset_tap in range(taps):
        rows_wide = padded[offset_tap : offset_tap + tok_dev].astype(jnp.float32)
        keep_tap = seg_pad[offset_tap : offset_tap + tok_dev] == seg_tok
        conv_sum = conv_sum + jnp.where(
            keep_tap[:, None], rows_wide * conv_weight[offset_tap][None, :], 0.0
        )
    convolved = jax.nn.silu(conv_sum).astype(jnp.bfloat16)
    inputs = convolved[:, :inner_local].reshape(groups_dev, GROUP, heads_local, head_width)
    b_matrix = convolved[:, inner_local : inner_local + state_width].reshape(
        groups_dev, GROUP, state_width
    )
    c_matrix = convolved[:, inner_local + state_width :].reshape(groups_dev, GROUP, state_width)
    step_size = jax.nn.softplus(dt_pre + dt_bias[None, :]).reshape(groups_dev, GROUP, heads_local)
    step_heads = step_size.transpose(0, 2, 1)
    decay_rate = -jnp.exp(a_log)
    within_group = jnp.arange(GROUP, dtype=jnp.int32)
    lower = (within_group[:, None] >= within_group[None, :]).astype(jnp.float32)
    cumul_heads = jnp.einsum(
        "ij,cjh->chi",
        lower,
        step_size * decay_rate[None, None, :],
        precision=lax.Precision.HIGHEST,
        preferred_element_type=jnp.float32,
    )
    segments = seg_tok.reshape(groups_dev, GROUP)
    seg_before = segment_of(offset + jnp.arange(groups_dev, dtype=jnp.int32) * GROUP - 1, lengths)
    within = jnp.arange(GROUP, dtype=jnp.int32)
    same_prompt = (segments[:, :, None] == segments[:, None, :]) & (
        within[:, None] >= within[None, :]
    )[None]
    log_decay = cumul_heads[:, :, :, None] - cumul_heads[:, :, None, :]
    decay_matrix = jnp.where(
        same_prompt[:, None], jnp.exp(jnp.where(same_prompt[:, None], log_decay, 0.0)), 0.0
    )
    scores = jnp.einsum("cin,cjn->cij", c_matrix, b_matrix, preferred_element_type=jnp.float32)
    mix_weights = (decay_matrix * scores[:, None] * step_heads[:, :, None, :]).astype(jnp.bfloat16)
    diag_out = jnp.einsum(
        "chij,cjhp->cihp", mix_weights, inputs, preferred_element_type=jnp.float32
    )
    last_segment = segments[:, -1]
    tail_weight = (
        jnp.where(
            (segments == last_segment[:, None])[:, None, :],
            jnp.exp(cumul_heads[:, :, -1:] - cumul_heads),
            0.0,
        )
        * step_heads
    )
    b_weighted = (b_matrix.astype(jnp.float32)[:, None] * tail_weight[:, :, :, None]).astype(
        jnp.bfloat16
    )
    contrib = jnp.einsum("cjhp,chjn->chpn", inputs, b_weighted, preferred_element_type=jnp.float32)
    pass_gate = jnp.where(
        (last_segment == seg_before)[:, None], jnp.exp(cumul_heads[:, :, -1]), 0.0
    )

    ends = [contrib[0]]
    for c in range(1, groups_dev):
        ends.append(pass_gate[c][:, None, None] * ends[-1] + contrib[c])
    local_end = jnp.stack(ends)
    local_in = jnp.concatenate([jnp.zeros_like(local_end[:1]), local_end[:-1]], axis=0)
    through_group = jnp.cumprod(pass_gate, axis=0)
    before_group = jnp.concatenate(
        [jnp.ones((1, heads_local), jnp.float32), through_group[:-1]], axis=0
    )

    dev_row = jnp.zeros((heads_local, 8, state_width), jnp.float32)
    dev_row = dev_row.at[:, 0, :].set(
        jnp.broadcast_to(through_group[-1][:, None], (heads_local, state_width))
    )
    carried = carry_in(jnp.concatenate([local_end[-1], dev_row], axis=1), head_width)
    group_end = through_group[:, :, None, None] * carried[None] + local_end
    every = gather_seq(group_end.astype(jnp.bfloat16)).reshape(
        (seq_count * groups_dev,) + group_end.shape[1:]
    )
    req_dev = request_group.shape[0] // seq_count
    mine = lax.dynamic_slice_in_dim(request_group, seq_index * req_dev, req_dev)
    request_states = jnp.stack(
        [lax.dynamic_index_in_dim(every, mine[i], 0, keepdims=False) for i in range(req_dev)]
    ).astype(jnp.float32)

    group_in = before_group[:, :, None, None] * carried[None] + local_in
    state_low = group_in.astype(jnp.bfloat16)
    carry_keep = jnp.where((segments == seg_before[:, None])[:, None, :], jnp.exp(cumul_heads), 0.0)
    carry_out = jnp.einsum(
        "cin,chpn->cihp", c_matrix, state_low, preferred_element_type=jnp.float32
    )
    carry_out = carry_out * carry_keep.transpose(0, 2, 1)[:, :, :, None]
    y_local = diag_out + carry_out + skip[None, None, :, None] * inputs.astype(jnp.float32)
    y_local = y_local.reshape(tok_dev, inner_local)
    gated = y_local * jax.nn.silu(gate_z.astype(jnp.float32))
    square_sum = jnp.sum(gated * gated, axis=1)
    scaled = (gated * norm_weight[None, :]).astype(jnp.bfloat16)
    partial = lax.dot_general(
        scaled, gathered[:, width:], (((1,), (1,)), ((), ())), preferred_element_type=jnp.float32
    )
    side = jnp.zeros((tok_dev, 128), jnp.float32).at[:, 0].set(square_sum)
    summed = scatter_sum(jnp.concatenate([partial, side], axis=1).astype(jnp.bfloat16), tp_count)
    mean_square = summed[:, d_model] / INNER
    mixed = (summed[:, :d_model] * lax.rsqrt(mean_square + epsilon)[:, None]).astype(jnp.bfloat16)
    return (mixed, request_states)


def solution(mesh):
    return jax.shard_map(
        on_device,
        mesh=mesh,
        in_specs=(
            P(SEQ, None),
            P((SEQ, "tp"), None),
            P((SEQ, "tp"), None),
            P((SEQ, "tp"), None),
            P(None, "tp"),
            P("tp"),
            P(),
            P(),
            P("tp"),
            P("tp"),
            P("tp"),
            P("tp"),
            P("tp", SEQ),
            P(),
            P(),
        ),
        out_specs=(P((SEQ, "tp"), None), P(SEQ, "tp", None, None)),
        check_vma=False,
    )
```

```python
import functools

import jax
import jax.numpy as jnp
from jax import lax
from jax.experimental import pallas as pl
from jax.experimental.pallas import tpu as pltpu
from jax.sharding import PartitionSpec as P

INNER = 4096
GROUP = 256
SEQ = "seq"


epsilon = 1e-05


def from_behind(x, by):
    count = lax.axis_size(SEQ)
    pairs = [(i, i + by) for i in range(count) if 0 <= i + by < count]
    return lax.ppermute(x, SEQ, pairs)


def gather_seq(x):
    return lax.all_gather(x, SEQ, axis=0, tiled=False)


def segment_of(position, lengths):
    prompt_ends = jnp.cumsum(lengths)
    return jnp.sum((position[:, None] >= prompt_ends[None, :]).astype(jnp.int32), axis=1)


def scatter_sum_kernel(count, rows, x_ref, q_ref, o_ref, qo_ref, recv, recv_q, send_sem, recv_sem):
    me = lax.axis_index("tp")
    barrier = pltpu.get_barrier_semaphore()
    for d in range(1, count):
        peer = lax.rem(me + d, count)
        pl.semaphore_signal(barrier, inc=1, device_id={"tp": peer}, device_id_type=pl.DeviceIdType.MESH)
    pl.semaphore_wait(barrier, count - 1)

    def pair(d, peer, slot):
        big = pltpu.make_async_remote_copy(
            src_ref=x_ref.at[pl.ds(pl.multiple_of(peer * rows, rows), rows)],
            dst_ref=recv.at[slot],
            send_sem=send_sem.at[0, d],
            recv_sem=recv_sem.at[0, slot],
            device_id={"tp": peer},
            device_id_type=pl.DeviceIdType.MESH,
        )
        small = pltpu.make_async_remote_copy(
            src_ref=q_ref.at[pl.ds(pl.multiple_of(peer * 8, 8), 8)],
            dst_ref=recv_q.at[slot],
            send_sem=send_sem.at[1, d],
            recv_sem=recv_sem.at[1, slot],
            device_id={"tp": peer},
            device_id_type=pl.DeviceIdType.MESH,
        )
        return big, small

    copies = []
    for d in range(1, count):
        peer = lax.rem(me + d, count)
        big, small = pair(d, peer, me)
        big.start()
        small.start()
        copies.append((big, small))
    total = x_ref[pl.ds(pl.multiple_of(me * rows, rows), rows), :].astype(jnp.float32)
    side = q_ref[pl.ds(pl.multiple_of(me * 8, 8), 8), :]
    for d in range(1, count):
        sender = lax.rem(me + count - d, count)
        big, small = pair(0, sender, sender)
        big.wait_recv()
        small.wait_recv()
        total = total + recv[sender].astype(jnp.float32)
        side = side + recv_q[sender]
    for big, small in copies:
        big.wait_send()
        small.wait_send()
    o_ref[...] = total
    qo_ref[...] = side


def scatter_sum(x, q, count):
    rows = x.shape[0] // count
    cols = x.shape[1]
    return pl.pallas_call(
        functools.partial(scatter_sum_kernel, count, rows),
        out_shape=(
            jax.ShapeDtypeStruct((rows, cols), jnp.float32),
            jax.ShapeDtypeStruct((8, q.shape[1]), jnp.float32),
        ),
        in_specs=[pl.BlockSpec(memory_space=pltpu.VMEM)] * 2,
        out_specs=(pl.BlockSpec(memory_space=pltpu.VMEM), pl.BlockSpec(memory_space=pltpu.VMEM)),
        scratch_shapes=[
            pltpu.VMEM((count, rows, cols), x.dtype),
            pltpu.VMEM((count, 8, q.shape[1]), jnp.float32),
            pltpu.SemaphoreType.DMA((2, count)),
            pltpu.SemaphoreType.DMA((2, count)),
        ],
        compiler_params=pltpu.CompilerParams(collective_id=0, has_side_effects=True),
    )(x, q)


def scan_kernel(count, width, mine_ref, out_ref, acc, send_buf, recv, send_sem, recv_sem):
    me = lax.axis_index(SEQ)
    barrier = pltpu.get_barrier_semaphore()
    for d in range(1, count):
        peer = lax.rem(me + d, count)
        pl.semaphore_signal(barrier, inc=1, device_id={SEQ: peer}, device_id_type=pl.DeviceIdType.MESH)
    pl.semaphore_wait(barrier, count - 1)
    distances = [1]
    while distances[-1] * 2 < count:
        distances.append(distances[-1] * 2)
    rounds = [1] + distances

    def link(r, dist, target):
        return pltpu.make_async_remote_copy(
            src_ref=mine_ref if r == 0 else send_buf.at[r],
            dst_ref=recv.at[r],
            send_sem=send_sem.at[r],
            recv_sem=recv_sem.at[r],
            device_id={SEQ: target},
            device_id_type=pl.DeviceIdType.MESH,
        )

    rows = acc.shape[1]
    is_gate_row = lax.broadcasted_iota(jnp.int32, acc.shape, 1) == width
    acc[...] = jnp.where(is_gate_row, 1.0, 0.0).astype(acc.dtype)
    for r, dist in enumerate(rounds):
        if r > 0:
            send_buf[r] = acc[...]

        @pl.when(me + dist < count)
        def _():
            link(r, dist, me + dist).start()

        @pl.when(me >= dist)
        def _():
            link(r, dist, me - dist).wait_recv()
            if r == 0:
                acc[...] = recv[0]
            else:
                came = recv[r]
                mine_gate = acc[:, width : width + 8, :][:, 0:1, :]
                came_gate = came[:, width : width + 8, :][:, 0:1, :]
                state = mine_gate * came + acc[...]
                acc[...] = jnp.where(is_gate_row, mine_gate * came_gate, state)

    for r, dist in enumerate(rounds):
        @pl.when(me + dist < count)
        def _():
            link(r, dist, me + dist).wait_send()
    out_ref[...] = acc[:, :width, :]


def carry_in(mine, width):
    count = lax.axis_size(SEQ)
    heads, rows, lanes = mine.shape
    steps = 1
    while (1 << (steps - 1)) < count:
        steps += 1
    return pl.pallas_call(
        functools.partial(scan_kernel, count, width),
        out_shape=jax.ShapeDtypeStruct((heads, width, lanes), jnp.float32),
        in_specs=[pl.BlockSpec(memory_space=pltpu.VMEM)],
        out_specs=pl.BlockSpec(memory_space=pltpu.VMEM),
        scratch_shapes=[
            pltpu.VMEM(mine.shape, jnp.float32),
            pltpu.VMEM((steps,) + mine.shape, jnp.float32),
            pltpu.VMEM((steps,) + mine.shape, jnp.float32),
            pltpu.SemaphoreType.DMA((steps,)),
            pltpu.SemaphoreType.DMA((steps,)),
        ],
        compiler_params=pltpu.CompilerParams(collective_id=1, has_side_effects=True),
    )(mine)


def round_up(n, m):
    return (n + m - 1) // m * m


def on_device(
    tokens,
    w_zx,
    w_dt,
    w_bc,
    conv_x_weight,
    conv_x_bias,
    conv_bc_weight,
    conv_bc_bias,
    dt_bias,
    a_log,
    skip,
    norm_weight,
    w_out,
    lengths,
    request_group,
):
    tp_count = lax.axis_size("tp")
    seq_count = lax.axis_size(SEQ)
    seq_index = lax.axis_index(SEQ)
    tok_dev = tokens.shape[0]
    d_model = tokens.shape[1]
    local_rows = w_zx.shape[0]
    inner_local = conv_x_weight.shape[1]
    heads_local = dt_bias.shape[0]
    head_width = inner_local // heads_local
    bc_width = conv_bc_weight.shape[1]
    state_width = bc_width // 2
    taps = conv_x_weight.shape[0]
    groups_dev = tok_dev // GROUP

    zx_part = w_zx.astype(jnp.bfloat16).reshape(local_rows, 2, tp_count, inner_local)
    zx_part = zx_part.transpose(0, 2, 1, 3).reshape(local_rows, tp_count, 2 * inner_local)
    bc_part = jnp.broadcast_to(
        w_bc.astype(jnp.bfloat16)[:, None, :], (local_rows, tp_count, bc_width)
    )
    dt_part = w_dt.astype(jnp.bfloat16).reshape(local_rows, tp_count, heads_local)
    used = 2 * inner_local + bc_width + heads_local
    width = round_up(used, 128)
    pad_part = jnp.zeros((local_rows, tp_count, width - used), jnp.bfloat16)
    packed = jnp.concatenate([zx_part, bc_part, dt_part, pad_part], axis=2)
    packed = packed.reshape(local_rows, tp_count * width)
    block = lax.all_to_all(packed, "tp", split_axis=1, concat_axis=0, tiled=True)
    block_rows = block.shape[0]
    out_rows, out_cols = w_out.shape
    out_piece = w_out.astype(jnp.bfloat16).T
    gathered = gather_seq(jnp.concatenate([block, out_piece], axis=1))
    gathered = gathered.reshape(seq_count * block_rows, width + out_rows)
    proj = jnp.dot(tokens, gathered[:, :width], preferred_element_type=jnp.float32)
    zx_low = proj[:, : 2 * inner_local].astype(jnp.bfloat16)
    gate_z = zx_low[:, :inner_local]
    x_raw = zx_low[:, inner_local:]
    bc_raw = proj[:, 2 * inner_local : 2 * inner_local + bc_width].astype(jnp.bfloat16)
    dt_pre = proj[:, 2 * inner_local + bc_width : used]

    raw_mix = jnp.concatenate([x_raw, bc_raw], axis=1)
    conv_weight = jnp.concatenate([conv_x_weight, conv_bc_weight], axis=1)
    conv_bias = jnp.concatenate([conv_x_bias, conv_bc_bias], axis=0)
    rim_rows = from_behind(raw_mix[tok_dev - (taps - 1) :], 1)
    padded = jnp.concatenate([rim_rows, raw_mix], axis=0)
    offset = seq_index * tok_dev
    seg_pad = segment_of(
        offset - (taps - 1) + jnp.arange(tok_dev + taps - 1, dtype=jnp.int32), lengths
    )
    seg_tok = seg_pad[taps - 1 :]
    conv_sum = jnp.zeros((tok_dev, raw_mix.shape[1]), jnp.float32) + conv_bias[None, :]
    for offset_tap in range(taps):
        rows_wide = padded[offset_tap : offset_tap + tok_dev].astype(jnp.float32)
        keep_tap = seg_pad[offset_tap : offset_tap + tok_dev] == seg_tok
        conv_sum = conv_sum + jnp.where(
            keep_tap[:, None], rows_wide * conv_weight[offset_tap][None, :], 0.0
        )
    convolved = jax.nn.silu(conv_sum).astype(jnp.bfloat16)
    inputs = convolved[:, :inner_local].reshape(groups_dev, GROUP, heads_local, head_width)
    b_matrix = convolved[:, inner_local : inner_local + state_width].reshape(
        groups_dev, GROUP, state_width
    )
    c_matrix = convolved[:, inner_local + state_width :].reshape(groups_dev, GROUP, state_width)
    step_size = jax.nn.softplus(dt_pre + dt_bias[None, :]).reshape(groups_dev, GROUP, heads_local)
    step_heads = step_size.transpose(0, 2, 1)
    decay_rate = -jnp.exp(a_log)
    within_group = jnp.arange(GROUP, dtype=jnp.int32)
    lower = (within_group[:, None] >= within_group[None, :]).astype(jnp.float32)
    cumul_heads = jnp.einsum(
        "ij,cjh->chi",
        lower,
        step_size * decay_rate[None, None, :],
        precision=lax.Precision.HIGHEST,
        preferred_element_type=jnp.float32,
    )
    segments = seg_tok.reshape(groups_dev, GROUP)
    seg_before = segment_of(offset + jnp.arange(groups_dev, dtype=jnp.int32) * GROUP - 1, lengths)
    within = jnp.arange(GROUP, dtype=jnp.int32)
    same_prompt = (segments[:, :, None] == segments[:, None, :]) & (
        within[:, None] >= within[None, :]
    )[None]
    log_decay = cumul_heads[:, :, :, None] - cumul_heads[:, :, None, :]
    decay_matrix = jnp.where(
        same_prompt[:, None], jnp.exp(jnp.where(same_prompt[:, None], log_decay, 0.0)), 0.0
    )
    scores = jnp.einsum("cin,cjn->cij", c_matrix, b_matrix, preferred_element_type=jnp.float32)
    mix_weights = (decay_matrix * scores[:, None] * step_heads[:, :, None, :]).astype(jnp.bfloat16)
    diag_out = jnp.einsum(
        "chij,cjhp->cihp", mix_weights, inputs, preferred_element_type=jnp.float32
    )
    last_segment = segments[:, -1]
    tail_weight = (
        jnp.where(
            (segments == last_segment[:, None])[:, None, :],
            jnp.exp(cumul_heads[:, :, -1:] - cumul_heads),
            0.0,
        )
        * step_heads
    )
    b_weighted = (b_matrix.astype(jnp.float32)[:, None] * tail_weight[:, :, :, None]).astype(
        jnp.bfloat16
    )
    contrib = jnp.einsum("cjhp,chjn->chpn", inputs, b_weighted, preferred_element_type=jnp.float32)
    pass_gate = jnp.where(
        (last_segment == seg_before)[:, None], jnp.exp(cumul_heads[:, :, -1]), 0.0
    )

    ends = [contrib[0]]
    for c in range(1, groups_dev):
        ends.append(pass_gate[c][:, None, None] * ends[-1] + contrib[c])
    local_end = jnp.stack(ends)
    local_in = jnp.concatenate([jnp.zeros_like(local_end[:1]), local_end[:-1]], axis=0)
    through_group = jnp.cumprod(pass_gate, axis=0)
    before_group = jnp.concatenate(
        [jnp.ones((1, heads_local), jnp.float32), through_group[:-1]], axis=0
    )

    dev_row = jnp.zeros((heads_local, 8, state_width), jnp.float32)
    dev_row = dev_row.at[:, 0, :].set(
        jnp.broadcast_to(through_group[-1][:, None], (heads_local, state_width))
    )
    carried = carry_in(jnp.concatenate([local_end[-1], dev_row], axis=1), head_width)
    group_end = through_group[:, :, None, None] * carried[None] + local_end
    every = gather_seq(group_end.astype(jnp.bfloat16)).reshape(
        (seq_count * groups_dev,) + group_end.shape[1:]
    )
    req_dev = request_group.shape[0] // seq_count
    mine = lax.dynamic_slice_in_dim(request_group, seq_index * req_dev, req_dev)
    request_states = jnp.stack(
        [lax.dynamic_index_in_dim(every, mine[i], 0, keepdims=False) for i in range(req_dev)]
    ).astype(jnp.float32)

    group_in = before_group[:, :, None, None] * carried[None] + local_in
    state_low = group_in.astype(jnp.bfloat16)
    carry_keep = jnp.where((segments == seg_before[:, None])[:, None, :], jnp.exp(cumul_heads), 0.0)
    carry_out = jnp.einsum(
        "cin,chpn->cihp", c_matrix, state_low, preferred_element_type=jnp.float32
    )
    carry_out = carry_out * carry_keep.transpose(0, 2, 1)[:, :, :, None]
    y_local = diag_out + carry_out + skip[None, None, :, None] * inputs.astype(jnp.float32)
    y_local = y_local.reshape(tok_dev, inner_local)
    gated = y_local * jax.nn.silu(gate_z.astype(jnp.float32))
    square_sum = jnp.sum(gated * gated, axis=1)
    scaled = (gated * norm_weight[None, :]).astype(jnp.bfloat16)
    partial = lax.dot_general(
        scaled, gathered[:, width:], (((1,), (1,)), ((), ())), preferred_element_type=jnp.float32
    )
    rows_out = tok_dev // tp_count
    side = square_sum.reshape(tp_count, 1, rows_out)
    side = jnp.concatenate(
        [side, jnp.zeros((tp_count, 1, 128 - rows_out), jnp.float32)], axis=2
    )
    side = jnp.concatenate([side, jnp.zeros((tp_count, 7, 128), jnp.float32)], axis=1)
    summed, side_sum = scatter_sum(
        partial.astype(jnp.bfloat16), side.reshape(tp_count * 8, 128), tp_count
    )
    mean_square = side_sum[0, :rows_out] / INNER
    mixed = (summed * lax.rsqrt(mean_square + epsilon)[:, None]).astype(jnp.bfloat16)
    return (mixed, request_states)


def solution(mesh):
    return jax.shard_map(
        on_device,
        mesh=mesh,
        in_specs=(
            P(SEQ, None),
            P((SEQ, "tp"), None),
            P((SEQ, "tp"), None),
            P((SEQ, "tp"), None),
            P(None, "tp"),
            P("tp"),
            P(),
            P(),
            P("tp"),
            P("tp"),
            P("tp"),
            P("tp"),
            P("tp", SEQ),
            P(),
            P(),
        ),
        out_specs=(P((SEQ, "tp"), None), P(SEQ, "tp", None, None)),
        check_vma=False,
    )
```

```python
import functools

import jax
import jax.numpy as jnp
from jax import lax
from jax.experimental import pallas as pl
from jax.experimental.pallas import tpu as pltpu
from jax.sharding import PartitionSpec as P

INNER = 4096
GROUP = 256
SEQ = "seq"


epsilon = 1e-05


def from_behind(x, by):
    count = lax.axis_size(SEQ)
    pairs = [(i, i + by) for i in range(count) if 0 <= i + by < count]
    return lax.ppermute(x, SEQ, pairs)


def gather_seq(x):
    return lax.all_gather(x, SEQ, axis=0, tiled=False)


def segment_of(position, lengths):
    prompt_ends = jnp.cumsum(lengths)
    return jnp.sum((position[:, None] >= prompt_ends[None, :]).astype(jnp.int32), axis=1)


def scatter_sum_kernel(count, rows, x_ref, q_ref, o_ref, recv, recv_q, send_sem, recv_sem):
    me = lax.axis_index("tp")
    barrier = pltpu.get_barrier_semaphore()
    for d in range(1, count):
        peer = lax.rem(me + d, count)
        pl.semaphore_signal(barrier, inc=1, device_id={"tp": peer}, device_id_type=pl.DeviceIdType.MESH)
    pl.semaphore_wait(barrier, count - 1)

    def pair(d, peer, slot):
        big = pltpu.make_async_remote_copy(
            src_ref=x_ref.at[pl.ds(pl.multiple_of(peer * rows, rows), rows)],
            dst_ref=recv.at[slot],
            send_sem=send_sem.at[0, d],
            recv_sem=recv_sem.at[0, slot],
            device_id={"tp": peer},
            device_id_type=pl.DeviceIdType.MESH,
        )
        small = pltpu.make_async_remote_copy(
            src_ref=q_ref.at[pl.ds(pl.multiple_of(peer * 8, 8), 8)],
            dst_ref=recv_q.at[slot],
            send_sem=send_sem.at[1, d],
            recv_sem=recv_sem.at[1, slot],
            device_id={"tp": peer},
            device_id_type=pl.DeviceIdType.MESH,
        )
        return big, small

    copies = []
    for d in range(1, count):
        peer = lax.rem(me + d, count)
        big, small = pair(d, peer, me)
        big.start()
        small.start()
        copies.append((big, small))
    total = x_ref[pl.ds(pl.multiple_of(me * rows, rows), rows), :].astype(jnp.float32)
    side = q_ref[pl.ds(pl.multiple_of(me * 8, 8), 8), :]
    for d in range(1, count):
        sender = lax.rem(me + count - d, count)
        big, small = pair(0, sender, sender)
        big.wait_recv()
        small.wait_recv()
        total = total + recv[sender].astype(jnp.float32)
        side = side + recv_q[sender]
    for big, small in copies:
        big.wait_send()
        small.wait_send()
    mean_square = jnp.transpose(side)[:rows, 0:1] / INNER
    o_ref[...] = (total * lax.rsqrt(mean_square + epsilon)).astype(o_ref.dtype)


def scatter_sum(x, q, count):
    rows = x.shape[0] // count
    cols = x.shape[1]
    return pl.pallas_call(
        functools.partial(scatter_sum_kernel, count, rows),
        out_shape=jax.ShapeDtypeStruct((rows, cols), jnp.bfloat16),
        in_specs=[pl.BlockSpec(memory_space=pltpu.VMEM)] * 2,
        out_specs=pl.BlockSpec(memory_space=pltpu.VMEM),
        scratch_shapes=[
            pltpu.VMEM((count, rows, cols), x.dtype),
            pltpu.VMEM((count, 8, q.shape[1]), jnp.float32),
            pltpu.SemaphoreType.DMA((2, count)),
            pltpu.SemaphoreType.DMA((2, count)),
        ],
        compiler_params=pltpu.CompilerParams(collective_id=0, has_side_effects=True),
    )(x, q)


def scan_kernel(count, width, mine_ref, out_ref, acc, send_buf, recv, send_sem, recv_sem):
    me = lax.axis_index(SEQ)
    barrier = pltpu.get_barrier_semaphore()
    for d in range(1, count):
        peer = lax.rem(me + d, count)
        pl.semaphore_signal(barrier, inc=1, device_id={SEQ: peer}, device_id_type=pl.DeviceIdType.MESH)
    pl.semaphore_wait(barrier, count - 1)
    distances = [1]
    while distances[-1] * 2 < count:
        distances.append(distances[-1] * 2)
    rounds = [1] + distances

    def link(r, dist, target):
        return pltpu.make_async_remote_copy(
            src_ref=mine_ref if r == 0 else send_buf.at[r],
            dst_ref=recv.at[r],
            send_sem=send_sem.at[r],
            recv_sem=recv_sem.at[r],
            device_id={SEQ: target},
            device_id_type=pl.DeviceIdType.MESH,
        )

    rows = acc.shape[1]
    is_gate_row = lax.broadcasted_iota(jnp.int32, acc.shape, 1) == width
    acc[...] = jnp.where(is_gate_row, 1.0, 0.0).astype(acc.dtype)
    for r, dist in enumerate(rounds):
        if r > 0:
            send_buf[r] = acc[...]

        @pl.when(me + dist < count)
        def _():
            link(r, dist, me + dist).start()

        @pl.when(me >= dist)
        def _():
            link(r, dist, me - dist).wait_recv()
            if r == 0:
                acc[...] = recv[0]
            else:
                came = recv[r]
                mine_gate = acc[:, width : width + 8, :][:, 0:1, :]
                came_gate = came[:, width : width + 8, :][:, 0:1, :]
                state = mine_gate * came + acc[...]
                acc[...] = jnp.where(is_gate_row, mine_gate * came_gate, state)

    for r, dist in enumerate(rounds):
        @pl.when(me + dist < count)
        def _():
            link(r, dist, me + dist).wait_send()
    out_ref[...] = acc[:, :width, :]


def carry_in(mine, width):
    count = lax.axis_size(SEQ)
    heads, rows, lanes = mine.shape
    steps = 1
    while (1 << (steps - 1)) < count:
        steps += 1
    return pl.pallas_call(
        functools.partial(scan_kernel, count, width),
        out_shape=jax.ShapeDtypeStruct((heads, width, lanes), jnp.float32),
        in_specs=[pl.BlockSpec(memory_space=pltpu.VMEM)],
        out_specs=pl.BlockSpec(memory_space=pltpu.VMEM),
        scratch_shapes=[
            pltpu.VMEM(mine.shape, jnp.float32),
            pltpu.VMEM((steps,) + mine.shape, jnp.float32),
            pltpu.VMEM((steps,) + mine.shape, jnp.float32),
            pltpu.SemaphoreType.DMA((steps,)),
            pltpu.SemaphoreType.DMA((steps,)),
        ],
        compiler_params=pltpu.CompilerParams(collective_id=1, has_side_effects=True),
    )(mine)


def round_up(n, m):
    return (n + m - 1) // m * m


def on_device(
    tokens,
    w_zx,
    w_dt,
    w_bc,
    conv_x_weight,
    conv_x_bias,
    conv_bc_weight,
    conv_bc_bias,
    dt_bias,
    a_log,
    skip,
    norm_weight,
    w_out,
    lengths,
    request_group,
):
    tp_count = lax.axis_size("tp")
    seq_count = lax.axis_size(SEQ)
    seq_index = lax.axis_index(SEQ)
    tok_dev = tokens.shape[0]
    d_model = tokens.shape[1]
    local_rows = w_zx.shape[0]
    inner_local = conv_x_weight.shape[1]
    heads_local = dt_bias.shape[0]
    head_width = inner_local // heads_local
    bc_width = conv_bc_weight.shape[1]
    state_width = bc_width // 2
    taps = conv_x_weight.shape[0]
    groups_dev = tok_dev // GROUP

    zx_part = w_zx.astype(jnp.bfloat16).reshape(local_rows, 2, tp_count, inner_local)
    zx_part = zx_part.transpose(0, 2, 1, 3).reshape(local_rows, tp_count, 2 * inner_local)
    bc_part = jnp.broadcast_to(
        w_bc.astype(jnp.bfloat16)[:, None, :], (local_rows, tp_count, bc_width)
    )
    dt_part = w_dt.astype(jnp.bfloat16).reshape(local_rows, tp_count, heads_local)
    used = 2 * inner_local + bc_width + heads_local
    width = round_up(used, 128)
    pad_part = jnp.zeros((local_rows, tp_count, width - used), jnp.bfloat16)
    packed = jnp.concatenate([zx_part, bc_part, dt_part, pad_part], axis=2)
    packed = packed.reshape(local_rows, tp_count * width)
    block = lax.all_to_all(packed, "tp", split_axis=1, concat_axis=0, tiled=True)
    block_rows = block.shape[0]
    out_rows, out_cols = w_out.shape
    out_piece = w_out.astype(jnp.bfloat16).T
    gathered = gather_seq(jnp.concatenate([block, out_piece], axis=1))
    gathered = gathered.reshape(seq_count * block_rows, width + out_rows)
    proj = jnp.dot(tokens, gathered[:, :width], preferred_element_type=jnp.float32)
    zx_low = proj[:, : 2 * inner_local].astype(jnp.bfloat16)
    gate_z = zx_low[:, :inner_local]
    x_raw = zx_low[:, inner_local:]
    bc_raw = proj[:, 2 * inner_local : 2 * inner_local + bc_width].astype(jnp.bfloat16)
    dt_pre = proj[:, 2 * inner_local + bc_width : used]

    raw_mix = jnp.concatenate([x_raw, bc_raw], axis=1)
    conv_weight = jnp.concatenate([conv_x_weight, conv_bc_weight], axis=1)
    conv_bias = jnp.concatenate([conv_x_bias, conv_bc_bias], axis=0)
    rim_rows = from_behind(raw_mix[tok_dev - (taps - 1) :], 1)
    padded = jnp.concatenate([rim_rows, raw_mix], axis=0)
    offset = seq_index * tok_dev
    seg_pad = segment_of(
        offset - (taps - 1) + jnp.arange(tok_dev + taps - 1, dtype=jnp.int32), lengths
    )
    seg_tok = seg_pad[taps - 1 :]
    conv_sum = jnp.zeros((tok_dev, raw_mix.shape[1]), jnp.float32) + conv_bias[None, :]
    for offset_tap in range(taps):
        rows_wide = padded[offset_tap : offset_tap + tok_dev].astype(jnp.float32)
        keep_tap = seg_pad[offset_tap : offset_tap + tok_dev] == seg_tok
        conv_sum = conv_sum + jnp.where(
            keep_tap[:, None], rows_wide * conv_weight[offset_tap][None, :], 0.0
        )
    convolved = jax.nn.silu(conv_sum).astype(jnp.bfloat16)
    inputs = convolved[:, :inner_local].reshape(groups_dev, GROUP, heads_local, head_width)
    b_matrix = convolved[:, inner_local : inner_local + state_width].reshape(
        groups_dev, GROUP, state_width
    )
    c_matrix = convolved[:, inner_local + state_width :].reshape(groups_dev, GROUP, state_width)
    step_size = jax.nn.softplus(dt_pre + dt_bias[None, :]).reshape(groups_dev, GROUP, heads_local)
    step_heads = step_size.transpose(0, 2, 1)
    decay_rate = -jnp.exp(a_log)
    within_group = jnp.arange(GROUP, dtype=jnp.int32)
    lower = (within_group[:, None] >= within_group[None, :]).astype(jnp.float32)
    cumul_heads = jnp.einsum(
        "ij,cjh->chi",
        lower,
        step_size * decay_rate[None, None, :],
        precision=lax.Precision.HIGHEST,
        preferred_element_type=jnp.float32,
    )
    segments = seg_tok.reshape(groups_dev, GROUP)
    seg_before = segment_of(offset + jnp.arange(groups_dev, dtype=jnp.int32) * GROUP - 1, lengths)
    within = jnp.arange(GROUP, dtype=jnp.int32)
    same_prompt = (segments[:, :, None] == segments[:, None, :]) & (
        within[:, None] >= within[None, :]
    )[None]
    log_decay = cumul_heads[:, :, :, None] - cumul_heads[:, :, None, :]
    decay_matrix = jnp.where(
        same_prompt[:, None], jnp.exp(jnp.where(same_prompt[:, None], log_decay, 0.0)), 0.0
    )
    scores = jnp.einsum("cin,cjn->cij", c_matrix, b_matrix, preferred_element_type=jnp.float32)
    mix_weights = (decay_matrix * scores[:, None] * step_heads[:, :, None, :]).astype(jnp.bfloat16)
    diag_out = jnp.einsum(
        "chij,cjhp->cihp", mix_weights, inputs, preferred_element_type=jnp.float32
    )
    last_segment = segments[:, -1]
    tail_weight = (
        jnp.where(
            (segments == last_segment[:, None])[:, None, :],
            jnp.exp(cumul_heads[:, :, -1:] - cumul_heads),
            0.0,
        )
        * step_heads
    )
    b_weighted = (b_matrix.astype(jnp.float32)[:, None] * tail_weight[:, :, :, None]).astype(
        jnp.bfloat16
    )
    contrib = jnp.einsum("cjhp,chjn->chpn", inputs, b_weighted, preferred_element_type=jnp.float32)
    pass_gate = jnp.where(
        (last_segment == seg_before)[:, None], jnp.exp(cumul_heads[:, :, -1]), 0.0
    )

    ends = [contrib[0]]
    for c in range(1, groups_dev):
        ends.append(pass_gate[c][:, None, None] * ends[-1] + contrib[c])
    local_end = jnp.stack(ends)
    local_in = jnp.concatenate([jnp.zeros_like(local_end[:1]), local_end[:-1]], axis=0)
    through_group = jnp.cumprod(pass_gate, axis=0)
    before_group = jnp.concatenate(
        [jnp.ones((1, heads_local), jnp.float32), through_group[:-1]], axis=0
    )

    dev_row = jnp.zeros((heads_local, 8, state_width), jnp.float32)
    dev_row = dev_row.at[:, 0, :].set(
        jnp.broadcast_to(through_group[-1][:, None], (heads_local, state_width))
    )
    carried = carry_in(jnp.concatenate([local_end[-1], dev_row], axis=1), head_width)
    group_end = through_group[:, :, None, None] * carried[None] + local_end
    every = gather_seq(group_end.astype(jnp.bfloat16)).reshape(
        (seq_count * groups_dev,) + group_end.shape[1:]
    )
    req_dev = request_group.shape[0] // seq_count
    mine = lax.dynamic_slice_in_dim(request_group, seq_index * req_dev, req_dev)
    request_states = jnp.stack(
        [lax.dynamic_index_in_dim(every, mine[i], 0, keepdims=False) for i in range(req_dev)]
    ).astype(jnp.float32)

    group_in = before_group[:, :, None, None] * carried[None] + local_in
    state_low = group_in.astype(jnp.bfloat16)
    carry_keep = jnp.where((segments == seg_before[:, None])[:, None, :], jnp.exp(cumul_heads), 0.0)
    carry_out = jnp.einsum(
        "cin,chpn->cihp", c_matrix, state_low, preferred_element_type=jnp.float32
    )
    carry_out = carry_out * carry_keep.transpose(0, 2, 1)[:, :, :, None]
    y_local = diag_out + carry_out + skip[None, None, :, None] * inputs.astype(jnp.float32)
    y_local = y_local.reshape(tok_dev, inner_local)
    gated = y_local * jax.nn.silu(gate_z.astype(jnp.float32))
    square_sum = jnp.sum(gated * gated, axis=1)
    scaled = (gated * norm_weight[None, :]).astype(jnp.bfloat16)
    partial = lax.dot_general(
        scaled, gathered[:, width:], (((1,), (1,)), ((), ())), preferred_element_type=jnp.float32
    )
    rows_out = tok_dev // tp_count
    side = square_sum.reshape(tp_count, 1, rows_out)
    side = jnp.concatenate(
        [side, jnp.zeros((tp_count, 1, 128 - rows_out), jnp.float32)], axis=2
    )
    side = jnp.concatenate([side, jnp.zeros((tp_count, 7, 128), jnp.float32)], axis=1)
    mixed = scatter_sum(partial.astype(jnp.bfloat16), side.reshape(tp_count * 8, 128), tp_count)
    return (mixed, request_states)


def solution(mesh):
    return jax.shard_map(
        on_device,
        mesh=mesh,
        in_specs=(
            P(SEQ, None),
            P((SEQ, "tp"), None),
            P((SEQ, "tp"), None),
            P((SEQ, "tp"), None),
            P(None, "tp"),
            P("tp"),
            P(),
            P(),
            P("tp"),
            P("tp"),
            P("tp"),
            P("tp"),
            P("tp", SEQ),
            P(),
            P(),
        ),
        out_specs=(P((SEQ, "tp"), None), P(SEQ, "tp", None, None)),
        check_vma=False,
    )
```

```python
import functools

import jax
import jax.numpy as jnp
from jax import lax
from jax.experimental import pallas as pl
from jax.experimental.pallas import tpu as pltpu
from jax.sharding import PartitionSpec as P

INNER = 4096
GROUP = 256
SEQ = "seq"


epsilon = 1e-05


def from_behind(x, by):
    count = lax.axis_size(SEQ)
    pairs = [(i, i + by) for i in range(count) if 0 <= i + by < count]
    return lax.ppermute(x, SEQ, pairs)


def gather_seq(x):
    return lax.all_gather(x, SEQ, axis=0, tiled=False)


def segment_of(position, lengths):
    count = lengths.shape[0]
    upto = jnp.arange(count)[:, None] >= jnp.arange(count)[None, :]
    prompt_ends = jnp.sum(jnp.where(upto, lengths[None, :], 0), axis=1)
    return jnp.sum((position[:, None] >= prompt_ends[None, :]).astype(jnp.int32), axis=1)


def scatter_sum_kernel(count, rows, x_ref, q_ref, o_ref, qo_ref, recv, recv_q, send_sem, recv_sem):
    me = lax.axis_index("tp")
    barrier = pltpu.get_barrier_semaphore()
    for d in range(1, count):
        peer = lax.rem(me + d, count)
        pl.semaphore_signal(barrier, inc=1, device_id={"tp": peer}, device_id_type=pl.DeviceIdType.MESH)
    pl.semaphore_wait(barrier, count - 1)

    def pair(d, peer, slot):
        big = pltpu.make_async_remote_copy(
            src_ref=x_ref.at[pl.ds(pl.multiple_of(peer * rows, rows), rows)],
            dst_ref=recv.at[slot],
            send_sem=send_sem.at[0, d],
            recv_sem=recv_sem.at[0, slot],
            device_id={"tp": peer},
            device_id_type=pl.DeviceIdType.MESH,
        )
        small = pltpu.make_async_remote_copy(
            src_ref=q_ref.at[pl.ds(pl.multiple_of(peer * 8, 8), 8)],
            dst_ref=recv_q.at[slot],
            send_sem=send_sem.at[1, d],
            recv_sem=recv_sem.at[1, slot],
            device_id={"tp": peer},
            device_id_type=pl.DeviceIdType.MESH,
        )
        return big, small

    copies = []
    for d in range(1, count):
        peer = lax.rem(me + d, count)
        big, small = pair(d, peer, me)
        big.start()
        small.start()
        copies.append((big, small))
    total = x_ref[pl.ds(pl.multiple_of(me * rows, rows), rows), :].astype(jnp.float32)
    side = q_ref[pl.ds(pl.multiple_of(me * 8, 8), 8), :]
    for d in range(1, count):
        sender = lax.rem(me + count - d, count)
        big, small = pair(0, sender, sender)
        big.wait_recv()
        small.wait_recv()
        total = total + recv[sender].astype(jnp.float32)
        side = side + recv_q[sender]
    for big, small in copies:
        big.wait_send()
        small.wait_send()
    o_ref[...] = total
    qo_ref[...] = side


def scatter_sum(x, q, count):
    rows = x.shape[0] // count
    cols = x.shape[1]
    return pl.pallas_call(
        functools.partial(scatter_sum_kernel, count, rows),
        out_shape=(
            jax.ShapeDtypeStruct((rows, cols), jnp.float32),
            jax.ShapeDtypeStruct((8, q.shape[1]), jnp.float32),
        ),
        in_specs=[pl.BlockSpec(memory_space=pltpu.VMEM)] * 2,
        out_specs=(pl.BlockSpec(memory_space=pltpu.VMEM), pl.BlockSpec(memory_space=pltpu.VMEM)),
        scratch_shapes=[
            pltpu.VMEM((count, rows, cols), x.dtype),
            pltpu.VMEM((count, 8, q.shape[1]), jnp.float32),
            pltpu.SemaphoreType.DMA((2, count)),
            pltpu.SemaphoreType.DMA((2, count)),
        ],
        compiler_params=pltpu.CompilerParams(collective_id=0, has_side_effects=True),
    )(x, q)


def scan_kernel(count, width, mine_ref, out_ref, acc, send_buf, recv, send_sem, recv_sem):
    me = lax.axis_index(SEQ)
    barrier = pltpu.get_barrier_semaphore()
    for d in range(1, count):
        peer = lax.rem(me + d, count)
        pl.semaphore_signal(barrier, inc=1, device_id={SEQ: peer}, device_id_type=pl.DeviceIdType.MESH)
    pl.semaphore_wait(barrier, count - 1)
    distances = [1]
    while distances[-1] * 2 < count:
        distances.append(distances[-1] * 2)
    rounds = [1] + distances

    def link(r, dist, target):
        return pltpu.make_async_remote_copy(
            src_ref=mine_ref if r == 0 else send_buf.at[r],
            dst_ref=recv.at[r],
            send_sem=send_sem.at[r],
            recv_sem=recv_sem.at[r],
            device_id={SEQ: target},
            device_id_type=pl.DeviceIdType.MESH,
        )

    rows = acc.shape[1]
    is_gate_row = lax.broadcasted_iota(jnp.int32, acc.shape, 1) == width
    acc[...] = jnp.where(is_gate_row, 1.0, 0.0).astype(acc.dtype)
    for r, dist in enumerate(rounds):
        if r > 0:
            send_buf[r] = acc[...]

        @pl.when(me + dist < count)
        def _():
            link(r, dist, me + dist).start()

        @pl.when(me >= dist)
        def _():
            link(r, dist, me - dist).wait_recv()
            if r == 0:
                acc[...] = recv[0]
            else:
                came = recv[r]
                mine_gate = acc[:, width : width + 8, :][:, 0:1, :]
                came_gate = came[:, width : width + 8, :][:, 0:1, :]
                state = mine_gate * came + acc[...]
                acc[...] = jnp.where(is_gate_row, mine_gate * came_gate, state)

    for r, dist in enumerate(rounds):
        @pl.when(me + dist < count)
        def _():
            link(r, dist, me + dist).wait_send()
    out_ref[...] = acc[:, :width, :]


def carry_in(mine, width):
    count = lax.axis_size(SEQ)
    heads, rows, lanes = mine.shape
    steps = 1
    while (1 << (steps - 1)) < count:
        steps += 1
    return pl.pallas_call(
        functools.partial(scan_kernel, count, width),
        out_shape=jax.ShapeDtypeStruct((heads, width, lanes), jnp.float32),
        in_specs=[pl.BlockSpec(memory_space=pltpu.VMEM)],
        out_specs=pl.BlockSpec(memory_space=pltpu.VMEM),
        scratch_shapes=[
            pltpu.VMEM(mine.shape, jnp.float32),
            pltpu.VMEM((steps,) + mine.shape, jnp.float32),
            pltpu.VMEM((steps,) + mine.shape, jnp.float32),
            pltpu.SemaphoreType.DMA((steps,)),
            pltpu.SemaphoreType.DMA((steps,)),
        ],
        compiler_params=pltpu.CompilerParams(collective_id=1, has_side_effects=True),
    )(mine)


def round_up(n, m):
    return (n + m - 1) // m * m


def on_device(
    tokens,
    w_zx,
    w_dt,
    w_bc,
    conv_x_weight,
    conv_x_bias,
    conv_bc_weight,
    conv_bc_bias,
    dt_bias,
    a_log,
    skip,
    norm_weight,
    w_out,
    lengths,
    request_group,
):
    tp_count = lax.axis_size("tp")
    seq_count = lax.axis_size(SEQ)
    seq_index = lax.axis_index(SEQ)
    tok_dev = tokens.shape[0]
    d_model = tokens.shape[1]
    local_rows = w_zx.shape[0]
    inner_local = conv_x_weight.shape[1]
    heads_local = dt_bias.shape[0]
    head_width = inner_local // heads_local
    bc_width = conv_bc_weight.shape[1]
    state_width = bc_width // 2
    taps = conv_x_weight.shape[0]
    groups_dev = tok_dev // GROUP

    zx_part = w_zx.astype(jnp.bfloat16).reshape(local_rows, 2, tp_count, inner_local)
    zx_part = zx_part.transpose(0, 2, 1, 3).reshape(local_rows, tp_count, 2 * inner_local)
    bc_part = jnp.broadcast_to(
        w_bc.astype(jnp.bfloat16)[:, None, :], (local_rows, tp_count, bc_width)
    )
    dt_part = w_dt.astype(jnp.bfloat16).reshape(local_rows, tp_count, heads_local)
    used = 2 * inner_local + bc_width + heads_local
    width = round_up(used, 128)
    pad_part = jnp.zeros((local_rows, tp_count, width - used), jnp.bfloat16)
    packed = jnp.concatenate([zx_part, bc_part, dt_part, pad_part], axis=2)
    packed = packed.reshape(local_rows, tp_count * width)
    block = lax.all_to_all(packed, "tp", split_axis=1, concat_axis=0, tiled=True)
    block_rows = block.shape[0]
    out_rows, out_cols = w_out.shape
    out_piece = w_out.astype(jnp.bfloat16).T
    gathered = gather_seq(jnp.concatenate([block, out_piece], axis=1))
    gathered = gathered.reshape(seq_count * block_rows, width + out_rows)
    proj = jnp.dot(tokens, gathered[:, :width], preferred_element_type=jnp.float32)
    zx_low = proj[:, : 2 * inner_local].astype(jnp.bfloat16)
    gate_z = zx_low[:, :inner_local]
    x_raw = zx_low[:, inner_local:]
    bc_raw = proj[:, 2 * inner_local : 2 * inner_local + bc_width].astype(jnp.bfloat16)
    dt_pre = proj[:, 2 * inner_local + bc_width : used]

    raw_mix = jnp.concatenate([x_raw, bc_raw], axis=1)
    conv_weight = jnp.concatenate([conv_x_weight, conv_bc_weight], axis=1)
    conv_bias = jnp.concatenate([conv_x_bias, conv_bc_bias], axis=0)
    rim_rows = from_behind(raw_mix[tok_dev - (taps - 1) :], 1)
    padded = jnp.concatenate([rim_rows, raw_mix], axis=0)
    offset = seq_index * tok_dev
    seg_pad = segment_of(
        offset - (taps - 1) + jnp.arange(tok_dev + taps - 1, dtype=jnp.int32), lengths
    )
    seg_tok = seg_pad[taps - 1 :]
    conv_sum = jnp.zeros((tok_dev, raw_mix.shape[1]), jnp.float32) + conv_bias[None, :]
    for offset_tap in range(taps):
        rows_wide = padded[offset_tap : offset_tap + tok_dev].astype(jnp.float32)
        keep_tap = seg_pad[offset_tap : offset_tap + tok_dev] == seg_tok
        conv_sum = conv_sum + jnp.where(
            keep_tap[:, None], rows_wide * conv_weight[offset_tap][None, :], 0.0
        )
    convolved = jax.nn.silu(conv_sum).astype(jnp.bfloat16)
    inputs = convolved[:, :inner_local].reshape(groups_dev, GROUP, heads_local, head_width)
    b_matrix = convolved[:, inner_local : inner_local + state_width].reshape(
        groups_dev, GROUP, state_width
    )
    c_matrix = convolved[:, inner_local + state_width :].reshape(groups_dev, GROUP, state_width)
    step_size = jax.nn.softplus(dt_pre + dt_bias[None, :]).reshape(groups_dev, GROUP, heads_local)
    step_heads = step_size.transpose(0, 2, 1)
    decay_rate = -jnp.exp(a_log)
    within_group = jnp.arange(GROUP, dtype=jnp.int32)
    lower = (within_group[:, None] >= within_group[None, :]).astype(jnp.float32)
    cumul_heads = jnp.einsum(
        "ij,cjh->chi",
        lower,
        step_size * decay_rate[None, None, :],
        precision=lax.Precision.HIGHEST,
        preferred_element_type=jnp.float32,
    )
    segments = seg_tok.reshape(groups_dev, GROUP)
    seg_before = segment_of(offset + jnp.arange(groups_dev, dtype=jnp.int32) * GROUP - 1, lengths)
    within = jnp.arange(GROUP, dtype=jnp.int32)
    same_prompt = (segments[:, :, None] == segments[:, None, :]) & (
        within[:, None] >= within[None, :]
    )[None]
    log_decay = cumul_heads[:, :, :, None] - cumul_heads[:, :, None, :]
    decay_matrix = jnp.where(
        same_prompt[:, None], jnp.exp(jnp.where(same_prompt[:, None], log_decay, 0.0)), 0.0
    )
    scores = jnp.einsum("cin,cjn->cij", c_matrix, b_matrix, preferred_element_type=jnp.float32)
    mix_weights = (decay_matrix * scores[:, None] * step_heads[:, :, None, :]).astype(jnp.bfloat16)
    diag_out = jnp.einsum(
        "chij,cjhp->cihp", mix_weights, inputs, preferred_element_type=jnp.float32
    )
    last_segment = segments[:, -1]
    tail_weight = (
        jnp.where(
            (segments == last_segment[:, None])[:, None, :],
            jnp.exp(cumul_heads[:, :, -1:] - cumul_heads),
            0.0,
        )
        * step_heads
    )
    b_weighted = (b_matrix.astype(jnp.float32)[:, None] * tail_weight[:, :, :, None]).astype(
        jnp.bfloat16
    )
    contrib = jnp.einsum("cjhp,chjn->chpn", inputs, b_weighted, preferred_element_type=jnp.float32)
    pass_gate = jnp.where(
        (last_segment == seg_before)[:, None], jnp.exp(cumul_heads[:, :, -1]), 0.0
    )

    ends = [contrib[0]]
    for c in range(1, groups_dev):
        ends.append(pass_gate[c][:, None, None] * ends[-1] + contrib[c])
    local_end = jnp.stack(ends)
    local_in = jnp.concatenate([jnp.zeros_like(local_end[:1]), local_end[:-1]], axis=0)
    through_group = jnp.cumprod(pass_gate, axis=0)
    before_group = jnp.concatenate(
        [jnp.ones((1, heads_local), jnp.float32), through_group[:-1]], axis=0
    )

    dev_row = jnp.zeros((heads_local, 8, state_width), jnp.float32)
    dev_row = dev_row.at[:, 0, :].set(
        jnp.broadcast_to(through_group[-1][:, None], (heads_local, state_width))
    )
    carried = carry_in(jnp.concatenate([local_end[-1], dev_row], axis=1), head_width)
    group_end = through_group[:, :, None, None] * carried[None] + local_end
    every = gather_seq(group_end.astype(jnp.bfloat16)).reshape(
        (seq_count * groups_dev,) + group_end.shape[1:]
    )
    req_dev = request_group.shape[0] // seq_count
    mine = lax.dynamic_slice_in_dim(request_group, seq_index * req_dev, req_dev)
    request_states = jnp.stack(
        [lax.dynamic_index_in_dim(every, mine[i], 0, keepdims=False) for i in range(req_dev)]
    ).astype(jnp.float32)

    group_in = before_group[:, :, None, None] * carried[None] + local_in
    state_low = group_in.astype(jnp.bfloat16)
    carry_keep = jnp.where((segments == seg_before[:, None])[:, None, :], jnp.exp(cumul_heads), 0.0)
    carry_out = jnp.einsum(
        "cin,chpn->cihp", c_matrix, state_low, preferred_element_type=jnp.float32
    )
    carry_out = carry_out * carry_keep.transpose(0, 2, 1)[:, :, :, None]
    y_local = diag_out + carry_out + skip[None, None, :, None] * inputs.astype(jnp.float32)
    y_local = y_local.reshape(tok_dev, inner_local)
    gated = y_local * jax.nn.silu(gate_z.astype(jnp.float32))
    square_sum = jnp.sum(gated * gated, axis=1)
    scaled = (gated * norm_weight[None, :]).astype(jnp.bfloat16)
    partial = lax.dot_general(
        scaled, gathered[:, width:], (((1,), (1,)), ((), ())), preferred_element_type=jnp.float32
    )
    rows_out = tok_dev // tp_count
    side = square_sum.reshape(tp_count, 1, rows_out)
    side = jnp.concatenate(
        [side, jnp.zeros((tp_count, 1, 128 - rows_out), jnp.float32)], axis=2
    )
    side = jnp.concatenate([side, jnp.zeros((tp_count, 7, 128), jnp.float32)], axis=1)
    summed, side_sum = scatter_sum(
        partial.astype(jnp.bfloat16), side.reshape(tp_count * 8, 128), tp_count
    )
    mean_square = side_sum[0, :rows_out] / INNER
    mixed = (summed * lax.rsqrt(mean_square + epsilon)[:, None]).astype(jnp.bfloat16)
    return (mixed, request_states)


def solution(mesh):
    return jax.shard_map(
        on_device,
        mesh=mesh,
        in_specs=(
            P(SEQ, None),
            P((SEQ, "tp"), None),
            P((SEQ, "tp"), None),
            P((SEQ, "tp"), None),
            P(None, "tp"),
            P("tp"),
            P(),
            P(),
            P("tp"),
            P("tp"),
            P("tp"),
            P("tp"),
            P("tp", SEQ),
            P(),
            P(),
        ),
        out_specs=(P((SEQ, "tp"), None), P(SEQ, "tp", None, None)),
        check_vma=False,
    )
```

```python
import functools

import jax
import jax.numpy as jnp
from jax import lax
from jax.experimental import pallas as pl
from jax.experimental.pallas import tpu as pltpu
from jax.sharding import PartitionSpec as P

INNER = 4096
GROUP = 256
SEQ = "seq"


epsilon = 1e-05


def from_behind(x, by):
    count = lax.axis_size(SEQ)
    pairs = [(i, i + by) for i in range(count) if 0 <= i + by < count]
    return lax.ppermute(x, SEQ, pairs)


def gather_seq(x):
    return lax.all_gather(x, SEQ, axis=0, tiled=False)


def segment_of(position, lengths):
    count = lengths.shape[0]
    upto = jnp.arange(count)[:, None] >= jnp.arange(count)[None, :]
    prompt_ends = jnp.sum(jnp.where(upto, lengths[None, :], 0), axis=1)
    return jnp.sum((position[:, None] >= prompt_ends[None, :]).astype(jnp.int32), axis=1)


def scatter_sum_kernel(count, rows, x_ref, q_ref, o_ref, qo_ref, recv, recv_q, send_sem, recv_sem):
    me = lax.axis_index("tp")
    barrier = pltpu.get_barrier_semaphore()
    for d in range(1, count):
        peer = lax.rem(me + d, count)
        pl.semaphore_signal(barrier, inc=1, device_id={"tp": peer}, device_id_type=pl.DeviceIdType.MESH)
    pl.semaphore_wait(barrier, count - 1)

    def pair(d, peer, slot):
        big = pltpu.make_async_remote_copy(
            src_ref=x_ref.at[pl.ds(pl.multiple_of(peer * rows, rows), rows)],
            dst_ref=recv.at[slot],
            send_sem=send_sem.at[0, d],
            recv_sem=recv_sem.at[0, slot],
            device_id={"tp": peer},
            device_id_type=pl.DeviceIdType.MESH,
        )
        small = pltpu.make_async_remote_copy(
            src_ref=q_ref.at[pl.ds(pl.multiple_of(peer * 8, 8), 8)],
            dst_ref=recv_q.at[slot],
            send_sem=send_sem.at[1, d],
            recv_sem=recv_sem.at[1, slot],
            device_id={"tp": peer},
            device_id_type=pl.DeviceIdType.MESH,
        )
        return big, small

    copies = []
    for d in range(1, count):
        peer = lax.rem(me + d, count)
        big, small = pair(d, peer, me)
        big.start()
        small.start()
        copies.append((big, small))
    total = x_ref[pl.ds(pl.multiple_of(me * rows, rows), rows), :].astype(jnp.float32)
    side = q_ref[pl.ds(pl.multiple_of(me * 8, 8), 8), :]
    for d in range(1, count):
        sender = lax.rem(me + count - d, count)
        big, small = pair(0, sender, sender)
        big.wait_recv()
        small.wait_recv()
        total = total + recv[sender].astype(jnp.float32)
        side = side + recv_q[sender]
    for big, small in copies:
        big.wait_send()
        small.wait_send()
    o_ref[...] = total
    qo_ref[...] = side


def scatter_sum(x, q, count):
    rows = x.shape[0] // count
    cols = x.shape[1]
    return pl.pallas_call(
        functools.partial(scatter_sum_kernel, count, rows),
        out_shape=(
            jax.ShapeDtypeStruct((rows, cols), jnp.float32),
            jax.ShapeDtypeStruct((8, q.shape[1]), jnp.float32),
        ),
        in_specs=[pl.BlockSpec(memory_space=pltpu.VMEM)] * 2,
        out_specs=(pl.BlockSpec(memory_space=pltpu.VMEM), pl.BlockSpec(memory_space=pltpu.VMEM)),
        scratch_shapes=[
            pltpu.VMEM((count, rows, cols), x.dtype),
            pltpu.VMEM((count, 8, q.shape[1]), jnp.float32),
            pltpu.SemaphoreType.DMA((2, count)),
            pltpu.SemaphoreType.DMA((2, count)),
        ],
        compiler_params=pltpu.CompilerParams(collective_id=0, has_side_effects=True),
    )(x, q)


def scan_kernel(count, width, mine_ref, out_ref, acc, send_buf, recv, send_sem, recv_sem):
    me = lax.axis_index(SEQ)
    barrier = pltpu.get_barrier_semaphore()
    for d in range(1, count):
        peer = lax.rem(me + d, count)
        pl.semaphore_signal(barrier, inc=1, device_id={SEQ: peer}, device_id_type=pl.DeviceIdType.MESH)
    pl.semaphore_wait(barrier, count - 1)
    distances = [1]
    while distances[-1] * 2 < count:
        distances.append(distances[-1] * 2)
    rounds = [1] + distances

    def link(r, dist, target):
        return pltpu.make_async_remote_copy(
            src_ref=mine_ref if r == 0 else send_buf.at[r],
            dst_ref=recv.at[r],
            send_sem=send_sem.at[r],
            recv_sem=recv_sem.at[r],
            device_id={SEQ: target},
            device_id_type=pl.DeviceIdType.MESH,
        )

    rows = acc.shape[1]
    is_gate_row = lax.broadcasted_iota(jnp.int32, acc.shape, 1) == width
    acc[...] = jnp.where(is_gate_row, 1.0, 0.0).astype(acc.dtype)
    for r, dist in enumerate(rounds):
        if r > 0:
            send_buf[r] = acc[...]

        @pl.when(me + dist < count)
        def _():
            link(r, dist, me + dist).start()

        @pl.when(me >= dist)
        def _():
            link(r, dist, me - dist).wait_recv()
            if r == 0:
                acc[...] = recv[0]
            else:
                came = recv[r]
                mine_gate = acc[:, width : width + 8, :][:, 0:1, :]
                came_gate = came[:, width : width + 8, :][:, 0:1, :]
                state = mine_gate * came + acc[...]
                acc[...] = jnp.where(is_gate_row, mine_gate * came_gate, state)

    for r, dist in enumerate(rounds):
        @pl.when(me + dist < count)
        def _():
            link(r, dist, me + dist).wait_send()
    out_ref[...] = acc[:, :width, :]


def carry_in(mine, width):
    count = lax.axis_size(SEQ)
    heads, rows, lanes = mine.shape
    steps = 1
    while (1 << (steps - 1)) < count:
        steps += 1
    return pl.pallas_call(
        functools.partial(scan_kernel, count, width),
        out_shape=jax.ShapeDtypeStruct((heads, width, lanes), jnp.float32),
        in_specs=[pl.BlockSpec(memory_space=pltpu.VMEM)],
        out_specs=pl.BlockSpec(memory_space=pltpu.VMEM),
        scratch_shapes=[
            pltpu.VMEM(mine.shape, jnp.float32),
            pltpu.VMEM((steps,) + mine.shape, jnp.float32),
            pltpu.VMEM((steps,) + mine.shape, jnp.float32),
            pltpu.SemaphoreType.DMA((steps,)),
            pltpu.SemaphoreType.DMA((steps,)),
        ],
        compiler_params=pltpu.CompilerParams(collective_id=1, has_side_effects=True),
    )(mine)


def round_up(n, m):
    return (n + m - 1) // m * m


def on_device(
    tokens,
    w_zx,
    w_dt,
    w_bc,
    conv_x_weight,
    conv_x_bias,
    conv_bc_weight,
    conv_bc_bias,
    dt_bias,
    a_log,
    skip,
    norm_weight,
    w_out,
    lengths,
    request_group,
):
    tp_count = lax.axis_size("tp")
    seq_count = lax.axis_size(SEQ)
    seq_index = lax.axis_index(SEQ)
    tok_dev = tokens.shape[0]
    d_model = tokens.shape[1]
    local_rows = w_zx.shape[0]
    inner_local = conv_x_weight.shape[1]
    heads_local = dt_bias.shape[0]
    head_width = inner_local // heads_local
    bc_width = conv_bc_weight.shape[1]
    state_width = bc_width // 2
    taps = conv_x_weight.shape[0]
    groups_dev = tok_dev // GROUP

    zx_part = w_zx.astype(jnp.bfloat16).reshape(local_rows, 2, tp_count, inner_local)
    zx_part = zx_part.transpose(0, 2, 1, 3).reshape(local_rows, tp_count, 2 * inner_local)
    bc_part = jnp.broadcast_to(
        w_bc.astype(jnp.bfloat16)[:, None, :], (local_rows, tp_count, bc_width)
    )
    dt_part = w_dt.astype(jnp.bfloat16).reshape(local_rows, tp_count, heads_local)
    used = 2 * inner_local + bc_width + heads_local
    width = round_up(used, 128)
    pad_part = jnp.zeros((local_rows, tp_count, width - used), jnp.bfloat16)
    packed = jnp.concatenate([zx_part, bc_part, dt_part, pad_part], axis=2)
    packed = packed.reshape(local_rows, tp_count * width)
    block = lax.all_to_all(packed, "tp", split_axis=1, concat_axis=0, tiled=True)
    block_rows = block.shape[0]
    out_rows, out_cols = w_out.shape
    out_piece = w_out.astype(jnp.bfloat16).T
    gathered = gather_seq(jnp.concatenate([block, out_piece], axis=1))
    gathered = gathered.reshape(seq_count * block_rows, width + out_rows)
    proj = jnp.dot(tokens, gathered[:, :width], preferred_element_type=jnp.float32)
    zx_low = proj[:, : 2 * inner_local].astype(jnp.bfloat16)
    gate_z = zx_low[:, :inner_local]
    x_raw = zx_low[:, inner_local:]
    bc_raw = proj[:, 2 * inner_local : 2 * inner_local + bc_width].astype(jnp.bfloat16)
    dt_pre = proj[:, 2 * inner_local + bc_width : used]

    raw_mix = jnp.concatenate([x_raw, bc_raw], axis=1)
    conv_weight = jnp.concatenate([conv_x_weight, conv_bc_weight], axis=1)
    conv_bias = jnp.concatenate([conv_x_bias, conv_bc_bias], axis=0)
    rim_rows = from_behind(raw_mix[tok_dev - (taps - 1) :], 1)
    padded = jnp.concatenate([rim_rows, raw_mix], axis=0)
    offset = seq_index * tok_dev
    seg_pad = segment_of(
        offset - (taps - 1) + jnp.arange(tok_dev + taps - 1, dtype=jnp.int32), lengths
    )
    seg_tok = seg_pad[taps - 1 :]
    conv_sum = jnp.zeros((tok_dev, raw_mix.shape[1]), jnp.float32) + conv_bias[None, :]
    for offset_tap in range(taps):
        rows_wide = padded[offset_tap : offset_tap + tok_dev].astype(jnp.float32)
        keep_tap = seg_pad[offset_tap : offset_tap + tok_dev] == seg_tok
        conv_sum = conv_sum + jnp.where(
            keep_tap[:, None], rows_wide * conv_weight[offset_tap][None, :], 0.0
        )
    convolved = jax.nn.silu(conv_sum).astype(jnp.bfloat16)
    inputs = convolved[:, :inner_local].reshape(groups_dev, GROUP, heads_local, head_width)
    b_matrix = convolved[:, inner_local : inner_local + state_width].reshape(
        groups_dev, GROUP, state_width
    )
    c_matrix = convolved[:, inner_local + state_width :].reshape(groups_dev, GROUP, state_width)
    step_size = jax.nn.softplus(dt_pre + dt_bias[None, :]).reshape(groups_dev, GROUP, heads_local)
    step_heads = step_size.transpose(0, 2, 1)
    decay_rate = -jnp.exp(a_log)
    within_group = jnp.arange(GROUP, dtype=jnp.int32)
    lower = (within_group[:, None] >= within_group[None, :]).astype(jnp.float32)
    cumul_heads = jnp.einsum(
        "ij,cjh->chi",
        lower,
        step_size * decay_rate[None, None, :],
        precision=lax.Precision.HIGHEST,
        preferred_element_type=jnp.float32,
    )
    segments = seg_tok.reshape(groups_dev, GROUP)
    seg_before = segment_of(offset + jnp.arange(groups_dev, dtype=jnp.int32) * GROUP - 1, lengths)
    within = jnp.arange(GROUP, dtype=jnp.int32)
    same_prompt = (segments[:, :, None] == segments[:, None, :]) & (
        within[:, None] >= within[None, :]
    )[None]
    log_decay = cumul_heads[:, :, :, None] - cumul_heads[:, :, None, :]
    decay_matrix = jnp.where(
        same_prompt[:, None], jnp.exp(jnp.where(same_prompt[:, None], log_decay, 0.0)), 0.0
    )
    scores = jnp.einsum("cin,cjn->cij", c_matrix, b_matrix, preferred_element_type=jnp.float32)
    mix_weights = (decay_matrix * scores[:, None] * step_heads[:, :, None, :]).astype(jnp.bfloat16)
    diag_out = jnp.einsum(
        "chij,cjhp->cihp", mix_weights, inputs, preferred_element_type=jnp.float32
    )
    last_segment = segments[:, -1]
    tail_weight = (
        jnp.where(
            (segments == last_segment[:, None])[:, None, :],
            jnp.exp(cumul_heads[:, :, -1:] - cumul_heads),
            0.0,
        )
        * step_heads
    )
    b_weighted = (b_matrix.astype(jnp.float32)[:, None] * tail_weight[:, :, :, None]).astype(
        jnp.bfloat16
    )
    contrib = jnp.einsum("cjhp,chjn->chpn", inputs, b_weighted, preferred_element_type=jnp.float32)
    pass_gate = jnp.where(
        (last_segment == seg_before)[:, None], jnp.exp(cumul_heads[:, :, -1]), 0.0
    )

    ends = [contrib[0]]
    for c in range(1, groups_dev):
        ends.append(pass_gate[c][:, None, None] * ends[-1] + contrib[c])
    local_end = jnp.stack(ends)
    local_in = jnp.concatenate([jnp.zeros_like(local_end[:1]), local_end[:-1]], axis=0)
    products = [pass_gate[0]]
    for c in range(1, groups_dev):
        products.append(products[-1] * pass_gate[c])
    through_group = jnp.stack(products)
    before_group = jnp.concatenate(
        [jnp.ones((1, heads_local), jnp.float32), through_group[:-1]], axis=0
    )

    dev_row = jnp.zeros((heads_local, 8, state_width), jnp.float32)
    dev_row = dev_row.at[:, 0, :].set(
        jnp.broadcast_to(through_group[-1][:, None], (heads_local, state_width))
    )
    carried = carry_in(jnp.concatenate([local_end[-1], dev_row], axis=1), head_width)
    group_end = through_group[:, :, None, None] * carried[None] + local_end
    every = gather_seq(group_end.astype(jnp.bfloat16)).reshape(
        (seq_count * groups_dev,) + group_end.shape[1:]
    )
    req_dev = request_group.shape[0] // seq_count
    mine = lax.dynamic_slice_in_dim(request_group, seq_index * req_dev, req_dev)
    request_states = jnp.stack(
        [lax.dynamic_index_in_dim(every, mine[i], 0, keepdims=False) for i in range(req_dev)]
    ).astype(jnp.float32)

    group_in = before_group[:, :, None, None] * carried[None] + local_in
    state_low = group_in.astype(jnp.bfloat16)
    carry_keep = jnp.where((segments == seg_before[:, None])[:, None, :], jnp.exp(cumul_heads), 0.0)
    carry_out = jnp.einsum(
        "cin,chpn->cihp", c_matrix, state_low, preferred_element_type=jnp.float32
    )
    carry_out = carry_out * carry_keep.transpose(0, 2, 1)[:, :, :, None]
    y_local = diag_out + carry_out + skip[None, None, :, None] * inputs.astype(jnp.float32)
    y_local = y_local.reshape(tok_dev, inner_local)
    gated = y_local * jax.nn.silu(gate_z.astype(jnp.float32))
    square_sum = jnp.sum(gated * gated, axis=1)
    scaled = (gated * norm_weight[None, :]).astype(jnp.bfloat16)
    partial = lax.dot_general(
        scaled, gathered[:, width:], (((1,), (1,)), ((), ())), preferred_element_type=jnp.float32
    )
    rows_out = tok_dev // tp_count
    side = square_sum.reshape(tp_count, 1, rows_out)
    side = jnp.concatenate(
        [side, jnp.zeros((tp_count, 1, 128 - rows_out), jnp.float32)], axis=2
    )
    side = jnp.concatenate([side, jnp.zeros((tp_count, 7, 128), jnp.float32)], axis=1)
    summed, side_sum = scatter_sum(
        partial.astype(jnp.bfloat16), side.reshape(tp_count * 8, 128), tp_count
    )
    mean_square = side_sum[0, :rows_out] / INNER
    mixed = (summed * lax.rsqrt(mean_square + epsilon)[:, None]).astype(jnp.bfloat16)
    return (mixed, request_states)


def solution(mesh):
    return jax.shard_map(
        on_device,
        mesh=mesh,
        in_specs=(
            P(SEQ, None),
            P((SEQ, "tp"), None),
            P((SEQ, "tp"), None),
            P((SEQ, "tp"), None),
            P(None, "tp"),
            P("tp"),
            P(),
            P(),
            P("tp"),
            P("tp"),
            P("tp"),
            P("tp"),
            P("tp", SEQ),
            P(),
            P(),
        ),
        out_specs=(P((SEQ, "tp"), None), P(SEQ, "tp", None, None)),
        check_vma=False,
    )
```

```python
import functools

import jax
import jax.numpy as jnp
from jax import lax
from jax.experimental import pallas as pl
from jax.experimental.pallas import tpu as pltpu
from jax.sharding import PartitionSpec as P

INNER = 4096
GROUP = 256
SEQ = "seq"


epsilon = 1e-05


def from_behind(x, by):
    count = lax.axis_size(SEQ)
    pairs = [(i, i + by) for i in range(count) if 0 <= i + by < count]
    return lax.ppermute(x, SEQ, pairs)


def gather_seq(x):
    return lax.all_gather(x, SEQ, axis=0, tiled=False)


def segment_of(position, lengths):
    count = lengths.shape[0]
    upto = jnp.arange(count)[:, None] >= jnp.arange(count)[None, :]
    prompt_ends = jnp.sum(jnp.where(upto, lengths[None, :], 0), axis=1)
    return jnp.sum((position[:, None] >= prompt_ends[None, :]).astype(jnp.int32), axis=1)


def scatter_sum_kernel(count, rows, x_ref, q_ref, o_ref, qo_ref, recv, recv_q, send_sem, recv_sem):
    me = lax.axis_index("tp")
    barrier = pltpu.get_barrier_semaphore()
    for d in range(1, count):
        peer = lax.rem(me + d, count)
        pl.semaphore_signal(barrier, inc=1, device_id={"tp": peer}, device_id_type=pl.DeviceIdType.MESH)
    pl.semaphore_wait(barrier, count - 1)

    def pair(d, peer, slot):
        big = pltpu.make_async_remote_copy(
            src_ref=x_ref.at[pl.ds(pl.multiple_of(peer * rows, rows), rows)],
            dst_ref=recv.at[slot],
            send_sem=send_sem.at[0, d],
            recv_sem=recv_sem.at[0, slot],
            device_id={"tp": peer},
            device_id_type=pl.DeviceIdType.MESH,
        )
        small = pltpu.make_async_remote_copy(
            src_ref=q_ref.at[pl.ds(pl.multiple_of(peer * 8, 8), 8)],
            dst_ref=recv_q.at[slot],
            send_sem=send_sem.at[1, d],
            recv_sem=recv_sem.at[1, slot],
            device_id={"tp": peer},
            device_id_type=pl.DeviceIdType.MESH,
        )
        return big, small

    copies = []
    for d in range(1, count):
        peer = lax.rem(me + d, count)
        big, small = pair(d, peer, me)
        big.start()
        small.start()
        copies.append((big, small))
    total = x_ref[pl.ds(pl.multiple_of(me * rows, rows), rows), :].astype(jnp.float32)
    side = q_ref[pl.ds(pl.multiple_of(me * 8, 8), 8), :]
    for d in range(1, count):
        sender = lax.rem(me + count - d, count)
        big, small = pair(0, sender, sender)
        big.wait_recv()
        small.wait_recv()
        total = total + recv[sender].astype(jnp.float32)
        side = side + recv_q[sender]
    for big, small in copies:
        big.wait_send()
        small.wait_send()
    o_ref[...] = total
    qo_ref[...] = side


def scatter_sum(x, q, count):
    rows = x.shape[0] // count
    cols = x.shape[1]
    return pl.pallas_call(
        functools.partial(scatter_sum_kernel, count, rows),
        out_shape=(
            jax.ShapeDtypeStruct((rows, cols), jnp.float32),
            jax.ShapeDtypeStruct((8, q.shape[1]), jnp.float32),
        ),
        in_specs=[pl.BlockSpec(memory_space=pltpu.VMEM)] * 2,
        out_specs=(pl.BlockSpec(memory_space=pltpu.VMEM), pl.BlockSpec(memory_space=pltpu.VMEM)),
        scratch_shapes=[
            pltpu.VMEM((count, rows, cols), x.dtype),
            pltpu.VMEM((count, 8, q.shape[1]), jnp.float32),
            pltpu.SemaphoreType.DMA((2, count)),
            pltpu.SemaphoreType.DMA((2, count)),
        ],
        compiler_params=pltpu.CompilerParams(collective_id=0, has_side_effects=True),
    )(x, q)


def scan_kernel(count, width, mine_ref, out_ref, acc_s, acc_g, send_s, send_g, recv_s, recv_g, send_sem, recv_sem):
    me = lax.axis_index(SEQ)
    barrier = pltpu.get_barrier_semaphore()
    for d in range(1, count):
        peer = lax.rem(me + d, count)
        pl.semaphore_signal(barrier, inc=1, device_id={SEQ: peer}, device_id_type=pl.DeviceIdType.MESH)
    pl.semaphore_wait(barrier, count - 1)
    distances = [1]
    while distances[-1] * 2 < count:
        distances.append(distances[-1] * 2)
    rounds = [1] + distances

    def links(r, target):
        state = pltpu.make_async_remote_copy(
            src_ref=send_s.at[r],
            dst_ref=recv_s.at[r],
            send_sem=send_sem.at[0, r],
            recv_sem=recv_sem.at[0, r],
            device_id={SEQ: target},
            device_id_type=pl.DeviceIdType.MESH,
        )
        gate = pltpu.make_async_remote_copy(
            src_ref=send_g.at[r],
            dst_ref=recv_g.at[r],
            send_sem=send_sem.at[1, r],
            recv_sem=recv_sem.at[1, r],
            device_id={SEQ: target},
            device_id_type=pl.DeviceIdType.MESH,
        )
        return state, gate

    acc_s[...] = jnp.zeros_like(acc_s)
    acc_g[...] = jnp.ones_like(acc_g)
    for r, dist in enumerate(rounds):
        if r == 0:
            send_s[0] = mine_ref[:, :width, :].astype(send_s.dtype)
            send_g[0] = mine_ref[:, width : width + 8, :]
        else:
            send_s[r] = acc_s[...].astype(send_s.dtype)
            send_g[r] = acc_g[...]

        @pl.when(me + dist < count)
        def _():
            state, gate = links(r, me + dist)
            state.start()
            gate.start()

        @pl.when(me >= dist)
        def _():
            state, gate = links(r, me - dist)
            state.wait_recv()
            gate.wait_recv()
            if r == 0:
                acc_s[...] = recv_s[0].astype(jnp.float32)
                acc_g[...] = recv_g[0]
            else:
                mine_gate = acc_g[...][:, 0:1, :]
                acc_s[...] = mine_gate * recv_s[r].astype(jnp.float32) + acc_s[...]
                acc_g[...] = mine_gate * recv_g[r]

    for r, dist in enumerate(rounds):
        @pl.when(me + dist < count)
        def _():
            state, gate = links(r, me + dist)
            state.wait_send()
            gate.wait_send()
    out_ref[...] = acc_s[...]


def carry_in(mine, width):
    count = lax.axis_size(SEQ)
    heads, rows, lanes = mine.shape
    steps = 1
    while (1 << (steps - 1)) < count:
        steps += 1
    return pl.pallas_call(
        functools.partial(scan_kernel, count, width),
        out_shape=jax.ShapeDtypeStruct((heads, width, lanes), jnp.float32),
        in_specs=[pl.BlockSpec(memory_space=pltpu.VMEM)],
        out_specs=pl.BlockSpec(memory_space=pltpu.VMEM),
        scratch_shapes=[
            pltpu.VMEM((heads, width, lanes), jnp.float32),
            pltpu.VMEM((heads, 8, lanes), jnp.float32),
            pltpu.VMEM((steps, heads, width, lanes), jnp.bfloat16),
            pltpu.VMEM((steps, heads, 8, lanes), jnp.float32),
            pltpu.VMEM((steps, heads, width, lanes), jnp.bfloat16),
            pltpu.VMEM((steps, heads, 8, lanes), jnp.float32),
            pltpu.SemaphoreType.DMA((2, steps)),
            pltpu.SemaphoreType.DMA((2, steps)),
        ],
        compiler_params=pltpu.CompilerParams(collective_id=1, has_side_effects=True),
    )(mine)


def round_up(n, m):
    return (n + m - 1) // m * m


def on_device(
    tokens,
    w_zx,
    w_dt,
    w_bc,
    conv_x_weight,
    conv_x_bias,
    conv_bc_weight,
    conv_bc_bias,
    dt_bias,
    a_log,
    skip,
    norm_weight,
    w_out,
    lengths,
    request_group,
):
    tp_count = lax.axis_size("tp")
    seq_count = lax.axis_size(SEQ)
    seq_index = lax.axis_index(SEQ)
    tok_dev = tokens.shape[0]
    d_model = tokens.shape[1]
    local_rows = w_zx.shape[0]
    inner_local = conv_x_weight.shape[1]
    heads_local = dt_bias.shape[0]
    head_width = inner_local // heads_local
    bc_width = conv_bc_weight.shape[1]
    state_width = bc_width // 2
    taps = conv_x_weight.shape[0]
    groups_dev = tok_dev // GROUP

    zx_part = w_zx.astype(jnp.bfloat16).reshape(local_rows, 2, tp_count, inner_local)
    zx_part = zx_part.transpose(0, 2, 1, 3).reshape(local_rows, tp_count, 2 * inner_local)
    bc_part = jnp.broadcast_to(
        w_bc.astype(jnp.bfloat16)[:, None, :], (local_rows, tp_count, bc_width)
    )
    dt_part = w_dt.astype(jnp.bfloat16).reshape(local_rows, tp_count, heads_local)
    used = 2 * inner_local + bc_width + heads_local
    width = round_up(used, 128)
    pad_part = jnp.zeros((local_rows, tp_count, width - used), jnp.bfloat16)
    packed = jnp.concatenate([zx_part, bc_part, dt_part, pad_part], axis=2)
    packed = packed.reshape(local_rows, tp_count * width)
    block = lax.all_to_all(packed, "tp", split_axis=1, concat_axis=0, tiled=True)
    block_rows = block.shape[0]
    out_rows, out_cols = w_out.shape
    out_piece = w_out.astype(jnp.bfloat16).T
    gathered = gather_seq(jnp.concatenate([block, out_piece], axis=1))
    gathered = gathered.reshape(seq_count * block_rows, width + out_rows)
    proj = jnp.dot(tokens, gathered[:, :width], preferred_element_type=jnp.float32)
    zx_low = proj[:, : 2 * inner_local].astype(jnp.bfloat16)
    gate_z = zx_low[:, :inner_local]
    x_raw = zx_low[:, inner_local:]
    bc_raw = proj[:, 2 * inner_local : 2 * inner_local + bc_width].astype(jnp.bfloat16)
    dt_pre = proj[:, 2 * inner_local + bc_width : used]

    raw_mix = jnp.concatenate([x_raw, bc_raw], axis=1)
    conv_weight = jnp.concatenate([conv_x_weight, conv_bc_weight], axis=1)
    conv_bias = jnp.concatenate([conv_x_bias, conv_bc_bias], axis=0)
    rim_rows = from_behind(raw_mix[tok_dev - (taps - 1) :], 1)
    padded = jnp.concatenate([rim_rows, raw_mix], axis=0)
    offset = seq_index * tok_dev
    seg_pad = segment_of(
        offset - (taps - 1) + jnp.arange(tok_dev + taps - 1, dtype=jnp.int32), lengths
    )
    seg_tok = seg_pad[taps - 1 :]
    conv_sum = jnp.zeros((tok_dev, raw_mix.shape[1]), jnp.float32) + conv_bias[None, :]
    for offset_tap in range(taps):
        rows_wide = padded[offset_tap : offset_tap + tok_dev].astype(jnp.float32)
        keep_tap = seg_pad[offset_tap : offset_tap + tok_dev] == seg_tok
        conv_sum = conv_sum + jnp.where(
            keep_tap[:, None], rows_wide * conv_weight[offset_tap][None, :], 0.0
        )
    convolved = jax.nn.silu(conv_sum).astype(jnp.bfloat16)
    inputs = convolved[:, :inner_local].reshape(groups_dev, GROUP, heads_local, head_width)
    b_matrix = convolved[:, inner_local : inner_local + state_width].reshape(
        groups_dev, GROUP, state_width
    )
    c_matrix = convolved[:, inner_local + state_width :].reshape(groups_dev, GROUP, state_width)
    step_size = jax.nn.softplus(dt_pre + dt_bias[None, :]).reshape(groups_dev, GROUP, heads_local)
    step_heads = step_size.transpose(0, 2, 1)
    decay_rate = -jnp.exp(a_log)
    within_group = jnp.arange(GROUP, dtype=jnp.int32)
    lower = (within_group[:, None] >= within_group[None, :]).astype(jnp.float32)
    cumul_heads = jnp.einsum(
        "ij,cjh->chi",
        lower,
        step_size * decay_rate[None, None, :],
        precision=lax.Precision.HIGHEST,
        preferred_element_type=jnp.float32,
    )
    segments = seg_tok.reshape(groups_dev, GROUP)
    seg_before = segment_of(offset + jnp.arange(groups_dev, dtype=jnp.int32) * GROUP - 1, lengths)
    within = jnp.arange(GROUP, dtype=jnp.int32)
    same_prompt = (segments[:, :, None] == segments[:, None, :]) & (
        within[:, None] >= within[None, :]
    )[None]
    log_decay = cumul_heads[:, :, :, None] - cumul_heads[:, :, None, :]
    decay_matrix = jnp.where(
        same_prompt[:, None], jnp.exp(jnp.where(same_prompt[:, None], log_decay, 0.0)), 0.0
    )
    scores = jnp.einsum("cin,cjn->cij", c_matrix, b_matrix, preferred_element_type=jnp.float32)
    mix_weights = (decay_matrix * scores[:, None] * step_heads[:, :, None, :]).astype(jnp.bfloat16)
    diag_out = jnp.einsum(
        "chij,cjhp->cihp", mix_weights, inputs, preferred_element_type=jnp.float32
    )
    last_segment = segments[:, -1]
    tail_weight = (
        jnp.where(
            (segments == last_segment[:, None])[:, None, :],
            jnp.exp(cumul_heads[:, :, -1:] - cumul_heads),
            0.0,
        )
        * step_heads
    )
    b_weighted = (b_matrix.astype(jnp.float32)[:, None] * tail_weight[:, :, :, None]).astype(
        jnp.bfloat16
    )
    contrib = jnp.einsum("cjhp,chjn->chpn", inputs, b_weighted, preferred_element_type=jnp.float32)
    pass_gate = jnp.where(
        (last_segment == seg_before)[:, None], jnp.exp(cumul_heads[:, :, -1]), 0.0
    )

    ends = [contrib[0]]
    for c in range(1, groups_dev):
        ends.append(pass_gate[c][:, None, None] * ends[-1] + contrib[c])
    local_end = jnp.stack(ends)
    local_in = jnp.concatenate([jnp.zeros_like(local_end[:1]), local_end[:-1]], axis=0)
    products = [pass_gate[0]]
    for c in range(1, groups_dev):
        products.append(products[-1] * pass_gate[c])
    through_group = jnp.stack(products)
    before_group = jnp.concatenate(
        [jnp.ones((1, heads_local), jnp.float32), through_group[:-1]], axis=0
    )

    dev_row = jnp.zeros((heads_local, 8, state_width), jnp.float32)
    dev_row = dev_row.at[:, 0, :].set(
        jnp.broadcast_to(through_group[-1][:, None], (heads_local, state_width))
    )
    carried = carry_in(jnp.concatenate([local_end[-1], dev_row], axis=1), head_width)
    group_end = through_group[:, :, None, None] * carried[None] + local_end
    every = gather_seq(group_end.astype(jnp.bfloat16)).reshape(
        (seq_count * groups_dev,) + group_end.shape[1:]
    )
    req_dev = request_group.shape[0] // seq_count
    mine = lax.dynamic_slice_in_dim(request_group, seq_index * req_dev, req_dev)
    request_states = jnp.stack(
        [lax.dynamic_index_in_dim(every, mine[i], 0, keepdims=False) for i in range(req_dev)]
    ).astype(jnp.float32)

    group_in = before_group[:, :, None, None] * carried[None] + local_in
    state_low = group_in.astype(jnp.bfloat16)
    carry_keep = jnp.where((segments == seg_before[:, None])[:, None, :], jnp.exp(cumul_heads), 0.0)
    carry_out = jnp.einsum(
        "cin,chpn->cihp", c_matrix, state_low, preferred_element_type=jnp.float32
    )
    carry_out = carry_out * carry_keep.transpose(0, 2, 1)[:, :, :, None]
    y_local = diag_out + carry_out + skip[None, None, :, None] * inputs.astype(jnp.float32)
    y_local = y_local.reshape(tok_dev, inner_local)
    gated = y_local * jax.nn.silu(gate_z.astype(jnp.float32))
    square_sum = jnp.sum(gated * gated, axis=1)
    scaled = (gated * norm_weight[None, :]).astype(jnp.bfloat16)
    partial = lax.dot_general(
        scaled, gathered[:, width:], (((1,), (1,)), ((), ())), preferred_element_type=jnp.float32
    )
    rows_out = tok_dev // tp_count
    side = square_sum.reshape(tp_count, 1, rows_out)
    side = jnp.concatenate(
        [side, jnp.zeros((tp_count, 1, 128 - rows_out), jnp.float32)], axis=2
    )
    side = jnp.concatenate([side, jnp.zeros((tp_count, 7, 128), jnp.float32)], axis=1)
    summed, side_sum = scatter_sum(
        partial.astype(jnp.bfloat16), side.reshape(tp_count * 8, 128), tp_count
    )
    mean_square = side_sum[0, :rows_out] / INNER
    mixed = (summed * lax.rsqrt(mean_square + epsilon)[:, None]).astype(jnp.bfloat16)
    return (mixed, request_states)


def solution(mesh):
    return jax.shard_map(
        on_device,
        mesh=mesh,
        in_specs=(
            P(SEQ, None),
            P((SEQ, "tp"), None),
            P((SEQ, "tp"), None),
            P((SEQ, "tp"), None),
            P(None, "tp"),
            P("tp"),
            P(),
            P(),
            P("tp"),
            P("tp"),
            P("tp"),
            P("tp"),
            P("tp", SEQ),
            P(),
            P(),
        ),
        out_specs=(P((SEQ, "tp"), None), P(SEQ, "tp", None, None)),
        check_vma=False,
    )
```

```python
import functools

import jax
import jax.numpy as jnp
from jax import lax
from jax.experimental import pallas as pl
from jax.experimental.pallas import tpu as pltpu
from jax.sharding import PartitionSpec as P

INNER = 4096
GROUP = 256
SEQ = "seq"


epsilon = 1e-05


def from_behind(x, by):
    count = lax.axis_size(SEQ)
    pairs = [(i, i + by) for i in range(count) if 0 <= i + by < count]
    return lax.ppermute(x, SEQ, pairs)


def gather_seq(x):
    return lax.all_gather(x, SEQ, axis=0, tiled=False)


def segment_of(position, lengths):
    count = lengths.shape[0]
    upto = jnp.arange(count)[:, None] >= jnp.arange(count)[None, :]
    prompt_ends = jnp.sum(jnp.where(upto, lengths[None, :], 0), axis=1)
    return jnp.sum((position[:, None] >= prompt_ends[None, :]).astype(jnp.int32), axis=1)


def scatter_sum_kernel(count, rows, x_ref, q_ref, o_ref, qo_ref, recv, recv_q, send_sem, recv_sem):
    me = lax.axis_index("tp")
    barrier = pltpu.get_barrier_semaphore()
    for d in range(1, count):
        peer = lax.rem(me + d, count)
        pl.semaphore_signal(barrier, inc=1, device_id={"tp": peer}, device_id_type=pl.DeviceIdType.MESH)
    pl.semaphore_wait(barrier, count - 1)

    def pair(d, peer, slot):
        big = pltpu.make_async_remote_copy(
            src_ref=x_ref.at[pl.ds(pl.multiple_of(peer * rows, rows), rows)],
            dst_ref=recv.at[slot],
            send_sem=send_sem.at[0, d],
            recv_sem=recv_sem.at[0, slot],
            device_id={"tp": peer},
            device_id_type=pl.DeviceIdType.MESH,
        )
        small = pltpu.make_async_remote_copy(
            src_ref=q_ref.at[pl.ds(pl.multiple_of(peer * 8, 8), 8)],
            dst_ref=recv_q.at[slot],
            send_sem=send_sem.at[1, d],
            recv_sem=recv_sem.at[1, slot],
            device_id={"tp": peer},
            device_id_type=pl.DeviceIdType.MESH,
        )
        return big, small

    copies = []
    for d in range(1, count):
        peer = lax.rem(me + d, count)
        big, small = pair(d, peer, me)
        big.start()
        small.start()
        copies.append((big, small))
    total = x_ref[pl.ds(pl.multiple_of(me * rows, rows), rows), :].astype(jnp.float32)
    side = q_ref[pl.ds(pl.multiple_of(me * 8, 8), 8), :]
    for d in range(1, count):
        sender = lax.rem(me + count - d, count)
        big, small = pair(0, sender, sender)
        big.wait_recv()
        small.wait_recv()
        total = total + recv[sender].astype(jnp.float32)
        side = side + recv_q[sender]
    for big, small in copies:
        big.wait_send()
        small.wait_send()
    o_ref[...] = total
    qo_ref[...] = side


def scatter_sum(x, q, count):
    rows = x.shape[0] // count
    cols = x.shape[1]
    return pl.pallas_call(
        functools.partial(scatter_sum_kernel, count, rows),
        out_shape=(
            jax.ShapeDtypeStruct((rows, cols), jnp.float32),
            jax.ShapeDtypeStruct((8, q.shape[1]), jnp.float32),
        ),
        in_specs=[pl.BlockSpec(memory_space=pltpu.VMEM)] * 2,
        out_specs=(pl.BlockSpec(memory_space=pltpu.VMEM), pl.BlockSpec(memory_space=pltpu.VMEM)),
        scratch_shapes=[
            pltpu.VMEM((count, rows, cols), x.dtype),
            pltpu.VMEM((count, 8, q.shape[1]), jnp.float32),
            pltpu.SemaphoreType.DMA((2, count)),
            pltpu.SemaphoreType.DMA((2, count)),
        ],
        compiler_params=pltpu.CompilerParams(collective_id=0, has_side_effects=True),
    )(x, q)


def scan_kernel(count, width, mine_ref, out_ref, acc_s, acc_g, send_s, send_g, recv_s, recv_g, send_sem, recv_sem):
    me = lax.axis_index(SEQ)
    barrier = pltpu.get_barrier_semaphore()
    for d in range(1, count):
        peer = lax.rem(me + d, count)
        pl.semaphore_signal(barrier, inc=1, device_id={SEQ: peer}, device_id_type=pl.DeviceIdType.MESH)
    pl.semaphore_wait(barrier, count - 1)
    distances = [1]
    while distances[-1] * 4 < count:
        distances.append(distances[-1] * 4)
    rounds = [(1, [1])] + [(d, [1, 2, 3]) for d in distances]

    def links(r, k, target):
        state = pltpu.make_async_remote_copy(
            src_ref=send_s.at[r],
            dst_ref=recv_s.at[r, k],
            send_sem=send_sem.at[0, r, k],
            recv_sem=recv_sem.at[0, r, k],
            device_id={SEQ: target},
            device_id_type=pl.DeviceIdType.MESH,
        )
        gate = pltpu.make_async_remote_copy(
            src_ref=send_g.at[r],
            dst_ref=recv_g.at[r, k],
            send_sem=send_sem.at[1, r, k],
            recv_sem=recv_sem.at[1, r, k],
            device_id={SEQ: target},
            device_id_type=pl.DeviceIdType.MESH,
        )
        return state, gate

    acc_s[...] = jnp.zeros_like(acc_s)
    acc_g[...] = jnp.ones_like(acc_g)
    for r, (dist, steps) in enumerate(rounds):
        if r == 0:
            send_s[0] = mine_ref[:, :width, :].astype(send_s.dtype)
            send_g[0] = mine_ref[:, width : width + 8, :]
        else:
            send_s[r] = acc_s[...].astype(send_s.dtype)
            send_g[r] = acc_g[...]
        for k in steps:
            @pl.when(me + k * dist < count)
            def _():
                state, gate = links(r, k - 1, me + k * dist)
                state.start()
                gate.start()
        for k in steps:
            @pl.when(me >= k * dist)
            def _():
                state, gate = links(r, k - 1, me - k * dist)
                state.wait_recv()
                gate.wait_recv()
                if r == 0:
                    acc_s[...] = recv_s[0, 0].astype(jnp.float32)
                    acc_g[...] = recv_g[0, 0]
                else:
                    mine_gate = acc_g[...][:, 0:1, :]
                    acc_s[...] = mine_gate * recv_s[r, k - 1].astype(jnp.float32) + acc_s[...]
                    acc_g[...] = mine_gate * recv_g[r, k - 1]

    for r, (dist, steps) in enumerate(rounds):
        for k in steps:
            @pl.when(me + k * dist < count)
            def _():
                state, gate = links(r, k - 1, me + k * dist)
                state.wait_send()
                gate.wait_send()
    out_ref[...] = acc_s[...]


def carry_in(mine, width):
    count = lax.axis_size(SEQ)
    heads, rows, lanes = mine.shape
    steps = 1
    span = 1
    while span < count:
        steps += 1
        span *= 4
    return pl.pallas_call(
        functools.partial(scan_kernel, count, width),
        out_shape=jax.ShapeDtypeStruct((heads, width, lanes), jnp.float32),
        in_specs=[pl.BlockSpec(memory_space=pltpu.VMEM)],
        out_specs=pl.BlockSpec(memory_space=pltpu.VMEM),
        scratch_shapes=[
            pltpu.VMEM((heads, width, lanes), jnp.float32),
            pltpu.VMEM((heads, 8, lanes), jnp.float32),
            pltpu.VMEM((steps, heads, width, lanes), jnp.bfloat16),
            pltpu.VMEM((steps, heads, 8, lanes), jnp.float32),
            pltpu.VMEM((steps, 3, heads, width, lanes), jnp.bfloat16),
            pltpu.VMEM((steps, 3, heads, 8, lanes), jnp.float32),
            pltpu.SemaphoreType.DMA((2, steps, 3)),
            pltpu.SemaphoreType.DMA((2, steps, 3)),
        ],
        compiler_params=pltpu.CompilerParams(collective_id=1, has_side_effects=True),
    )(mine)


def round_up(n, m):
    return (n + m - 1) // m * m


def on_device(
    tokens,
    w_zx,
    w_dt,
    w_bc,
    conv_x_weight,
    conv_x_bias,
    conv_bc_weight,
    conv_bc_bias,
    dt_bias,
    a_log,
    skip,
    norm_weight,
    w_out,
    lengths,
    request_group,
):
    tp_count = lax.axis_size("tp")
    seq_count = lax.axis_size(SEQ)
    seq_index = lax.axis_index(SEQ)
    tok_dev = tokens.shape[0]
    d_model = tokens.shape[1]
    local_rows = w_zx.shape[0]
    inner_local = conv_x_weight.shape[1]
    heads_local = dt_bias.shape[0]
    head_width = inner_local // heads_local
    bc_width = conv_bc_weight.shape[1]
    state_width = bc_width // 2
    taps = conv_x_weight.shape[0]
    groups_dev = tok_dev // GROUP

    zx_part = w_zx.astype(jnp.bfloat16).reshape(local_rows, 2, tp_count, inner_local)
    zx_part = zx_part.transpose(0, 2, 1, 3).reshape(local_rows, tp_count, 2 * inner_local)
    bc_part = jnp.broadcast_to(
        w_bc.astype(jnp.bfloat16)[:, None, :], (local_rows, tp_count, bc_width)
    )
    dt_part = w_dt.astype(jnp.bfloat16).reshape(local_rows, tp_count, heads_local)
    used = 2 * inner_local + bc_width + heads_local
    width = round_up(used, 128)
    pad_part = jnp.zeros((local_rows, tp_count, width - used), jnp.bfloat16)
    packed = jnp.concatenate([zx_part, bc_part, dt_part, pad_part], axis=2)
    packed = packed.reshape(local_rows, tp_count * width)
    block = lax.all_to_all(packed, "tp", split_axis=1, concat_axis=0, tiled=True)
    block_rows = block.shape[0]
    out_rows, out_cols = w_out.shape
    out_piece = w_out.astype(jnp.bfloat16).T
    gathered = gather_seq(jnp.concatenate([block, out_piece], axis=1))
    gathered = gathered.reshape(seq_count * block_rows, width + out_rows)
    proj = jnp.dot(tokens, gathered[:, :width], preferred_element_type=jnp.float32)
    zx_low = proj[:, : 2 * inner_local].astype(jnp.bfloat16)
    gate_z = zx_low[:, :inner_local]
    x_raw = zx_low[:, inner_local:]
    bc_raw = proj[:, 2 * inner_local : 2 * inner_local + bc_width].astype(jnp.bfloat16)
    dt_pre = proj[:, 2 * inner_local + bc_width : used]

    raw_mix = jnp.concatenate([x_raw, bc_raw], axis=1)
    conv_weight = jnp.concatenate([conv_x_weight, conv_bc_weight], axis=1)
    conv_bias = jnp.concatenate([conv_x_bias, conv_bc_bias], axis=0)
    rim_rows = from_behind(raw_mix[tok_dev - (taps - 1) :], 1)
    padded = jnp.concatenate([rim_rows, raw_mix], axis=0)
    offset = seq_index * tok_dev
    seg_pad = segment_of(
        offset - (taps - 1) + jnp.arange(tok_dev + taps - 1, dtype=jnp.int32), lengths
    )
    seg_tok = seg_pad[taps - 1 :]
    conv_sum = jnp.zeros((tok_dev, raw_mix.shape[1]), jnp.float32) + conv_bias[None, :]
    for offset_tap in range(taps):
        rows_wide = padded[offset_tap : offset_tap + tok_dev].astype(jnp.float32)
        keep_tap = seg_pad[offset_tap : offset_tap + tok_dev] == seg_tok
        conv_sum = conv_sum + jnp.where(
            keep_tap[:, None], rows_wide * conv_weight[offset_tap][None, :], 0.0
        )
    convolved = jax.nn.silu(conv_sum).astype(jnp.bfloat16)
    inputs = convolved[:, :inner_local].reshape(groups_dev, GROUP, heads_local, head_width)
    b_matrix = convolved[:, inner_local : inner_local + state_width].reshape(
        groups_dev, GROUP, state_width
    )
    c_matrix = convolved[:, inner_local + state_width :].reshape(groups_dev, GROUP, state_width)
    step_size = jax.nn.softplus(dt_pre + dt_bias[None, :]).reshape(groups_dev, GROUP, heads_local)
    step_heads = step_size.transpose(0, 2, 1)
    decay_rate = -jnp.exp(a_log)
    within_group = jnp.arange(GROUP, dtype=jnp.int32)
    lower = (within_group[:, None] >= within_group[None, :]).astype(jnp.float32)
    cumul_heads = jnp.einsum(
        "ij,cjh->chi",
        lower,
        step_size * decay_rate[None, None, :],
        precision=lax.Precision.HIGHEST,
        preferred_element_type=jnp.float32,
    )
    segments = seg_tok.reshape(groups_dev, GROUP)
    seg_before = segment_of(offset + jnp.arange(groups_dev, dtype=jnp.int32) * GROUP - 1, lengths)
    within = jnp.arange(GROUP, dtype=jnp.int32)
    same_prompt = (segments[:, :, None] == segments[:, None, :]) & (
        within[:, None] >= within[None, :]
    )[None]
    log_decay = cumul_heads[:, :, :, None] - cumul_heads[:, :, None, :]
    decay_matrix = jnp.where(
        same_prompt[:, None], jnp.exp(jnp.where(same_prompt[:, None], log_decay, 0.0)), 0.0
    )
    scores = jnp.einsum("cin,cjn->cij", c_matrix, b_matrix, preferred_element_type=jnp.float32)
    mix_weights = (decay_matrix * scores[:, None] * step_heads[:, :, None, :]).astype(jnp.bfloat16)
    diag_out = jnp.einsum(
        "chij,cjhp->cihp", mix_weights, inputs, preferred_element_type=jnp.float32
    )
    last_segment = segments[:, -1]
    tail_weight = (
        jnp.where(
            (segments == last_segment[:, None])[:, None, :],
            jnp.exp(cumul_heads[:, :, -1:] - cumul_heads),
            0.0,
        )
        * step_heads
    )
    b_weighted = (b_matrix.astype(jnp.float32)[:, None] * tail_weight[:, :, :, None]).astype(
        jnp.bfloat16
    )
    contrib = jnp.einsum("cjhp,chjn->chpn", inputs, b_weighted, preferred_element_type=jnp.float32)
    pass_gate = jnp.where(
        (last_segment == seg_before)[:, None], jnp.exp(cumul_heads[:, :, -1]), 0.0
    )

    ends = [contrib[0]]
    for c in range(1, groups_dev):
        ends.append(pass_gate[c][:, None, None] * ends[-1] + contrib[c])
    local_end = jnp.stack(ends)
    local_in = jnp.concatenate([jnp.zeros_like(local_end[:1]), local_end[:-1]], axis=0)
    products = [pass_gate[0]]
    for c in range(1, groups_dev):
        products.append(products[-1] * pass_gate[c])
    through_group = jnp.stack(products)
    before_group = jnp.concatenate(
        [jnp.ones((1, heads_local), jnp.float32), through_group[:-1]], axis=0
    )

    dev_row = jnp.zeros((heads_local, 8, state_width), jnp.float32)
    dev_row = dev_row.at[:, 0, :].set(
        jnp.broadcast_to(through_group[-1][:, None], (heads_local, state_width))
    )
    carried = carry_in(jnp.concatenate([local_end[-1], dev_row], axis=1), head_width)
    group_end = through_group[:, :, None, None] * carried[None] + local_end
    every = gather_seq(group_end.astype(jnp.bfloat16)).reshape(
        (seq_count * groups_dev,) + group_end.shape[1:]
    )
    req_dev = request_group.shape[0] // seq_count
    mine = lax.dynamic_slice_in_dim(request_group, seq_index * req_dev, req_dev)
    request_states = jnp.stack(
        [lax.dynamic_index_in_dim(every, mine[i], 0, keepdims=False) for i in range(req_dev)]
    ).astype(jnp.float32)

    group_in = before_group[:, :, None, None] * carried[None] + local_in
    state_low = group_in.astype(jnp.bfloat16)
    carry_keep = jnp.where((segments == seg_before[:, None])[:, None, :], jnp.exp(cumul_heads), 0.0)
    carry_out = jnp.einsum(
        "cin,chpn->cihp", c_matrix, state_low, preferred_element_type=jnp.float32
    )
    carry_out = carry_out * carry_keep.transpose(0, 2, 1)[:, :, :, None]
    y_local = diag_out + carry_out + skip[None, None, :, None] * inputs.astype(jnp.float32)
    y_local = y_local.reshape(tok_dev, inner_local)
    gated = y_local * jax.nn.silu(gate_z.astype(jnp.float32))
    square_sum = jnp.sum(gated * gated, axis=1)
    scaled = (gated * norm_weight[None, :]).astype(jnp.bfloat16)
    partial = lax.dot_general(
        scaled, gathered[:, width:], (((1,), (1,)), ((), ())), preferred_element_type=jnp.float32
    )
    rows_out = tok_dev // tp_count
    side = square_sum.reshape(tp_count, 1, rows_out)
    side = jnp.concatenate(
        [side, jnp.zeros((tp_count, 1, 128 - rows_out), jnp.float32)], axis=2
    )
    side = jnp.concatenate([side, jnp.zeros((tp_count, 7, 128), jnp.float32)], axis=1)
    summed, side_sum = scatter_sum(
        partial.astype(jnp.bfloat16), side.reshape(tp_count * 8, 128), tp_count
    )
    mean_square = side_sum[0, :rows_out] / INNER
    mixed = (summed * lax.rsqrt(mean_square + epsilon)[:, None]).astype(jnp.bfloat16)
    return (mixed, request_states)


def solution(mesh):
    return jax.shard_map(
        on_device,
        mesh=mesh,
        in_specs=(
            P(SEQ, None),
            P((SEQ, "tp"), None),
            P((SEQ, "tp"), None),
            P((SEQ, "tp"), None),
            P(None, "tp"),
            P("tp"),
            P(),
            P(),
            P("tp"),
            P("tp"),
            P("tp"),
            P("tp"),
            P("tp", SEQ),
            P(),
            P(),
        ),
        out_specs=(P((SEQ, "tp"), None), P(SEQ, "tp", None, None)),
        check_vma=False,
    )
```

```python
import functools

import jax
import jax.numpy as jnp
from jax import lax
from jax.experimental import pallas as pl
from jax.experimental.pallas import tpu as pltpu
from jax.sharding import PartitionSpec as P

INNER = 4096
GROUP = 256
SEQ = "seq"


epsilon = 1e-05


def from_behind(x, by):
    count = lax.axis_size(SEQ)
    pairs = [(i, i + by) for i in range(count) if 0 <= i + by < count]
    return lax.ppermute(x, SEQ, pairs)


def gather_seq(x):
    return lax.all_gather(x, SEQ, axis=0, tiled=False)


def segment_of(position, lengths):
    count = lengths.shape[0]
    upto = jnp.arange(count)[:, None] >= jnp.arange(count)[None, :]
    prompt_ends = jnp.sum(jnp.where(upto, lengths[None, :], 0), axis=1)
    return jnp.sum((position[:, None] >= prompt_ends[None, :]).astype(jnp.int32), axis=1)


def scatter_sum_kernel(count, rows, x_ref, q_ref, o_ref, qo_ref, recv, recv_q, send_sem, recv_sem):
    me = lax.axis_index("tp")
    barrier = pltpu.get_barrier_semaphore()
    for d in range(1, count):
        peer = lax.rem(me + d, count)
        pl.semaphore_signal(barrier, inc=1, device_id={"tp": peer}, device_id_type=pl.DeviceIdType.MESH)
    pl.semaphore_wait(barrier, count - 1)

    def pair(d, peer, slot):
        big = pltpu.make_async_remote_copy(
            src_ref=x_ref.at[pl.ds(pl.multiple_of(peer * rows, rows), rows)],
            dst_ref=recv.at[slot],
            send_sem=send_sem.at[0, d],
            recv_sem=recv_sem.at[0, slot],
            device_id={"tp": peer},
            device_id_type=pl.DeviceIdType.MESH,
        )
        small = pltpu.make_async_remote_copy(
            src_ref=q_ref.at[pl.ds(pl.multiple_of(peer * 8, 8), 8)],
            dst_ref=recv_q.at[slot],
            send_sem=send_sem.at[1, d],
            recv_sem=recv_sem.at[1, slot],
            device_id={"tp": peer},
            device_id_type=pl.DeviceIdType.MESH,
        )
        return big, small

    copies = []
    for d in range(1, count):
        peer = lax.rem(me + d, count)
        big, small = pair(d, peer, me)
        big.start()
        small.start()
        copies.append((big, small))
    total = x_ref[pl.ds(pl.multiple_of(me * rows, rows), rows), :].astype(jnp.float32)
    side = q_ref[pl.ds(pl.multiple_of(me * 8, 8), 8), :]
    for d in range(1, count):
        sender = lax.rem(me + count - d, count)
        big, small = pair(0, sender, sender)
        big.wait_recv()
        small.wait_recv()
        total = total + recv[sender].astype(jnp.float32)
        side = side + recv_q[sender]
    for big, small in copies:
        big.wait_send()
        small.wait_send()
    o_ref[...] = total
    qo_ref[...] = side


def scatter_sum(x, q, count):
    rows = x.shape[0] // count
    cols = x.shape[1]
    return pl.pallas_call(
        functools.partial(scatter_sum_kernel, count, rows),
        out_shape=(
            jax.ShapeDtypeStruct((rows, cols), jnp.float32),
            jax.ShapeDtypeStruct((8, q.shape[1]), jnp.float32),
        ),
        in_specs=[pl.BlockSpec(memory_space=pltpu.VMEM)] * 2,
        out_specs=(pl.BlockSpec(memory_space=pltpu.VMEM), pl.BlockSpec(memory_space=pltpu.VMEM)),
        scratch_shapes=[
            pltpu.VMEM((count, rows, cols), x.dtype),
            pltpu.VMEM((count, 8, q.shape[1]), jnp.float32),
            pltpu.SemaphoreType.DMA((2, count)),
            pltpu.SemaphoreType.DMA((2, count)),
        ],
        compiler_params=pltpu.CompilerParams(collective_id=0, has_side_effects=True),
    )(x, q)


def scan_kernel(count, width, mine_ref, out_ref, acc_s, acc_g, send_s, recv_s, send_sem, recv_sem):
    me = lax.axis_index(SEQ)
    barrier = pltpu.get_barrier_semaphore()
    for d in range(1, count):
        peer = lax.rem(me + d, count)
        pl.semaphore_signal(barrier, inc=1, device_id={SEQ: peer}, device_id_type=pl.DeviceIdType.MESH)
    pl.semaphore_wait(barrier, count - 1)
    distances = [1]
    while distances[-1] * 2 < count:
        distances.append(distances[-1] * 2)
    rounds = [1] + distances

    def links(r, target):
        return pltpu.make_async_remote_copy(
            src_ref=send_s.at[r],
            dst_ref=recv_s.at[r],
            send_sem=send_sem.at[0, r],
            recv_sem=recv_sem.at[0, r],
            device_id={SEQ: target},
            device_id_type=pl.DeviceIdType.MESH,
        )

    tail_row = lax.broadcasted_iota(jnp.int32, (acc_s.shape[0], 16, acc_s.shape[2]), 1)

    def pack(state, gate):
        hi = gate.astype(jnp.bfloat16).astype(jnp.float32)
        lo = (gate - hi).astype(jnp.bfloat16).astype(jnp.float32)
        tail = jnp.where(tail_row == 0, hi, jnp.where(tail_row == 1, lo, 0.0))
        send_s[r_now[0], :, :width, :] = state.astype(send_s.dtype)
        send_s[r_now[0], :, width : width + 16, :] = tail.astype(send_s.dtype)

    r_now = [0]
    acc_s[...] = jnp.zeros_like(acc_s)
    acc_g[...] = jnp.ones_like(acc_g)
    for r, dist in enumerate(rounds):
        r_now[0] = r
        if r == 0:
            pack(mine_ref[:, :width, :], mine_ref[:, width : width + 8, :][:, 0:1, :])
        else:
            pack(acc_s[...], acc_g[...][:, 0:1, :])

        @pl.when(me + dist < count)
        def _():
            links(r, me + dist).start()

        @pl.when(me >= dist)
        def _():
            links(r, me - dist).wait_recv()
            tail = recv_s[r, :, width : width + 16, :].astype(jnp.float32)
            came_gate = tail[:, 0:1, :] + tail[:, 1:2, :]
            came_state = recv_s[r, :, :width, :].astype(jnp.float32)
            if r == 0:
                acc_s[...] = came_state
                acc_g[...] = jnp.broadcast_to(came_gate, acc_g.shape)
            else:
                mine_gate = acc_g[...][:, 0:1, :]
                acc_s[...] = mine_gate * came_state + acc_s[...]
                acc_g[...] = jnp.broadcast_to(mine_gate * came_gate, acc_g.shape)

    for r, dist in enumerate(rounds):
        @pl.when(me + dist < count)
        def _():
            links(r, me + dist).wait_send()
    out_ref[...] = acc_s[...]


def carry_in(mine, width):
    count = lax.axis_size(SEQ)
    heads, rows, lanes = mine.shape
    steps = 1
    while (1 << (steps - 1)) < count:
        steps += 1
    return pl.pallas_call(
        functools.partial(scan_kernel, count, width),
        out_shape=jax.ShapeDtypeStruct((heads, width, lanes), jnp.float32),
        in_specs=[pl.BlockSpec(memory_space=pltpu.VMEM)],
        out_specs=pl.BlockSpec(memory_space=pltpu.VMEM),
        scratch_shapes=[
            pltpu.VMEM((heads, width, lanes), jnp.float32),
            pltpu.VMEM((heads, 8, lanes), jnp.float32),
            pltpu.VMEM((steps, heads, width + 16, lanes), jnp.bfloat16),
            pltpu.VMEM((steps, heads, width + 16, lanes), jnp.bfloat16),
            pltpu.SemaphoreType.DMA((1, steps)),
            pltpu.SemaphoreType.DMA((1, steps)),
        ],
        compiler_params=pltpu.CompilerParams(collective_id=1, has_side_effects=True),
    )(mine)


def round_up(n, m):
    return (n + m - 1) // m * m


def on_device(
    tokens,
    w_zx,
    w_dt,
    w_bc,
    conv_x_weight,
    conv_x_bias,
    conv_bc_weight,
    conv_bc_bias,
    dt_bias,
    a_log,
    skip,
    norm_weight,
    w_out,
    lengths,
    request_group,
):
    tp_count = lax.axis_size("tp")
    seq_count = lax.axis_size(SEQ)
    seq_index = lax.axis_index(SEQ)
    tok_dev = tokens.shape[0]
    d_model = tokens.shape[1]
    local_rows = w_zx.shape[0]
    inner_local = conv_x_weight.shape[1]
    heads_local = dt_bias.shape[0]
    head_width = inner_local // heads_local
    bc_width = conv_bc_weight.shape[1]
    state_width = bc_width // 2
    taps = conv_x_weight.shape[0]
    groups_dev = tok_dev // GROUP

    zx_part = w_zx.astype(jnp.bfloat16).reshape(local_rows, 2, tp_count, inner_local)
    zx_part = zx_part.transpose(0, 2, 1, 3).reshape(local_rows, tp_count, 2 * inner_local)
    bc_part = jnp.broadcast_to(
        w_bc.astype(jnp.bfloat16)[:, None, :], (local_rows, tp_count, bc_width)
    )
    dt_part = w_dt.astype(jnp.bfloat16).reshape(local_rows, tp_count, heads_local)
    used = 2 * inner_local + bc_width + heads_local
    width = round_up(used, 128)
    pad_part = jnp.zeros((local_rows, tp_count, width - used), jnp.bfloat16)
    packed = jnp.concatenate([zx_part, bc_part, dt_part, pad_part], axis=2)
    packed = packed.reshape(local_rows, tp_count * width)
    block = lax.all_to_all(packed, "tp", split_axis=1, concat_axis=0, tiled=True)
    block_rows = block.shape[0]
    out_rows, out_cols = w_out.shape
    out_piece = w_out.astype(jnp.bfloat16).T
    gathered = gather_seq(jnp.concatenate([block, out_piece], axis=1))
    gathered = gathered.reshape(seq_count * block_rows, width + out_rows)
    proj = jnp.dot(tokens, gathered[:, :width], preferred_element_type=jnp.float32)
    zx_low = proj[:, : 2 * inner_local].astype(jnp.bfloat16)
    gate_z = zx_low[:, :inner_local]
    x_raw = zx_low[:, inner_local:]
    bc_raw = proj[:, 2 * inner_local : 2 * inner_local + bc_width].astype(jnp.bfloat16)
    dt_pre = proj[:, 2 * inner_local + bc_width : used]

    raw_mix = jnp.concatenate([x_raw, bc_raw], axis=1)
    conv_weight = jnp.concatenate([conv_x_weight, conv_bc_weight], axis=1)
    conv_bias = jnp.concatenate([conv_x_bias, conv_bc_bias], axis=0)
    rim_rows = from_behind(raw_mix[tok_dev - (taps - 1) :], 1)
    padded = jnp.concatenate([rim_rows, raw_mix], axis=0)
    offset = seq_index * tok_dev
    seg_pad = segment_of(
        offset - (taps - 1) + jnp.arange(tok_dev + taps - 1, dtype=jnp.int32), lengths
    )
    seg_tok = seg_pad[taps - 1 :]
    conv_sum = jnp.zeros((tok_dev, raw_mix.shape[1]), jnp.float32) + conv_bias[None, :]
    for offset_tap in range(taps):
        rows_wide = padded[offset_tap : offset_tap + tok_dev].astype(jnp.float32)
        keep_tap = seg_pad[offset_tap : offset_tap + tok_dev] == seg_tok
        conv_sum = conv_sum + jnp.where(
            keep_tap[:, None], rows_wide * conv_weight[offset_tap][None, :], 0.0
        )
    convolved = jax.nn.silu(conv_sum).astype(jnp.bfloat16)
    inputs = convolved[:, :inner_local].reshape(groups_dev, GROUP, heads_local, head_width)
    b_matrix = convolved[:, inner_local : inner_local + state_width].reshape(
        groups_dev, GROUP, state_width
    )
    c_matrix = convolved[:, inner_local + state_width :].reshape(groups_dev, GROUP, state_width)
    step_size = jax.nn.softplus(dt_pre + dt_bias[None, :]).reshape(groups_dev, GROUP, heads_local)
    step_heads = step_size.transpose(0, 2, 1)
    decay_rate = -jnp.exp(a_log)
    within_group = jnp.arange(GROUP, dtype=jnp.int32)
    lower = (within_group[:, None] >= within_group[None, :]).astype(jnp.float32)
    cumul_heads = jnp.einsum(
        "ij,cjh->chi",
        lower,
        step_size * decay_rate[None, None, :],
        precision=lax.Precision.HIGHEST,
        preferred_element_type=jnp.float32,
    )
    segments = seg_tok.reshape(groups_dev, GROUP)
    seg_before = segment_of(offset + jnp.arange(groups_dev, dtype=jnp.int32) * GROUP - 1, lengths)
    within = jnp.arange(GROUP, dtype=jnp.int32)
    same_prompt = (segments[:, :, None] == segments[:, None, :]) & (
        within[:, None] >= within[None, :]
    )[None]
    log_decay = cumul_heads[:, :, :, None] - cumul_heads[:, :, None, :]
    decay_matrix = jnp.where(
        same_prompt[:, None], jnp.exp(jnp.where(same_prompt[:, None], log_decay, 0.0)), 0.0
    )
    scores = jnp.einsum("cin,cjn->cij", c_matrix, b_matrix, preferred_element_type=jnp.float32)
    mix_weights = (decay_matrix * scores[:, None] * step_heads[:, :, None, :]).astype(jnp.bfloat16)
    diag_out = jnp.einsum(
        "chij,cjhp->cihp", mix_weights, inputs, preferred_element_type=jnp.float32
    )
    last_segment = segments[:, -1]
    tail_weight = (
        jnp.where(
            (segments == last_segment[:, None])[:, None, :],
            jnp.exp(cumul_heads[:, :, -1:] - cumul_heads),
            0.0,
        )
        * step_heads
    )
    b_weighted = (b_matrix.astype(jnp.float32)[:, None] * tail_weight[:, :, :, None]).astype(
        jnp.bfloat16
    )
    contrib = jnp.einsum("cjhp,chjn->chpn", inputs, b_weighted, preferred_element_type=jnp.float32)
    pass_gate = jnp.where(
        (last_segment == seg_before)[:, None], jnp.exp(cumul_heads[:, :, -1]), 0.0
    )

    ends = [contrib[0]]
    for c in range(1, groups_dev):
        ends.append(pass_gate[c][:, None, None] * ends[-1] + contrib[c])
    local_end = jnp.stack(ends)
    local_in = jnp.concatenate([jnp.zeros_like(local_end[:1]), local_end[:-1]], axis=0)
    products = [pass_gate[0]]
    for c in range(1, groups_dev):
        products.append(products[-1] * pass_gate[c])
    through_group = jnp.stack(products)
    before_group = jnp.concatenate(
        [jnp.ones((1, heads_local), jnp.float32), through_group[:-1]], axis=0
    )

    dev_row = jnp.zeros((heads_local, 8, state_width), jnp.float32)
    dev_row = dev_row.at[:, 0, :].set(
        jnp.broadcast_to(through_group[-1][:, None], (heads_local, state_width))
    )
    carried = carry_in(jnp.concatenate([local_end[-1], dev_row], axis=1), head_width)
    group_end = through_group[:, :, None, None] * carried[None] + local_end
    every = gather_seq(group_end.astype(jnp.bfloat16)).reshape(
        (seq_count * groups_dev,) + group_end.shape[1:]
    )
    req_dev = request_group.shape[0] // seq_count
    mine = lax.dynamic_slice_in_dim(request_group, seq_index * req_dev, req_dev)
    request_states = jnp.stack(
        [lax.dynamic_index_in_dim(every, mine[i], 0, keepdims=False) for i in range(req_dev)]
    ).astype(jnp.float32)

    group_in = before_group[:, :, None, None] * carried[None] + local_in
    state_low = group_in.astype(jnp.bfloat16)
    carry_keep = jnp.where((segments == seg_before[:, None])[:, None, :], jnp.exp(cumul_heads), 0.0)
    carry_out = jnp.einsum(
        "cin,chpn->cihp", c_matrix, state_low, preferred_element_type=jnp.float32
    )
    carry_out = carry_out * carry_keep.transpose(0, 2, 1)[:, :, :, None]
    y_local = diag_out + carry_out + skip[None, None, :, None] * inputs.astype(jnp.float32)
    y_local = y_local.reshape(tok_dev, inner_local)
    gated = y_local * jax.nn.silu(gate_z.astype(jnp.float32))
    square_sum = jnp.sum(gated * gated, axis=1)
    scaled = (gated * norm_weight[None, :]).astype(jnp.bfloat16)
    partial = lax.dot_general(
        scaled, gathered[:, width:], (((1,), (1,)), ((), ())), preferred_element_type=jnp.float32
    )
    rows_out = tok_dev // tp_count
    side = square_sum.reshape(tp_count, 1, rows_out)
    side = jnp.concatenate(
        [side, jnp.zeros((tp_count, 1, 128 - rows_out), jnp.float32)], axis=2
    )
    side = jnp.concatenate([side, jnp.zeros((tp_count, 7, 128), jnp.float32)], axis=1)
    summed, side_sum = scatter_sum(
        partial.astype(jnp.bfloat16), side.reshape(tp_count * 8, 128), tp_count
    )
    mean_square = side_sum[0, :rows_out] / INNER
    mixed = (summed * lax.rsqrt(mean_square + epsilon)[:, None]).astype(jnp.bfloat16)
    return (mixed, request_states)


def solution(mesh):
    return jax.shard_map(
        on_device,
        mesh=mesh,
        in_specs=(
            P(SEQ, None),
            P((SEQ, "tp"), None),
            P((SEQ, "tp"), None),
            P((SEQ, "tp"), None),
            P(None, "tp"),
            P("tp"),
            P(),
            P(),
            P("tp"),
            P("tp"),
            P("tp"),
            P("tp"),
            P("tp", SEQ),
            P(),
            P(),
        ),
        out_specs=(P((SEQ, "tp"), None), P(SEQ, "tp", None, None)),
        check_vma=False,
    )
```
